128 devices in a mesh: cuts: 16 (over x_lo, z, core), slab: 8 (over y, x_hi).
Axes of the slice: x: 4 (x_hi: 2, x_lo: 2; x = x_hi * 2 + x_lo), y: 4, z: 4, core: 2. Of those that a mesh axis runs over, the one named last changes fastest.
Arguments:
- current_block: float32 [16, 64, 16, 512], P('cuts', 'slab'), may hold values from -6 to 6
- previous_block: float32 [16, 64, 16, 512], P('cuts', 'slab'), may hold values from -6 to 6
- previous_coupling: float32 [16, 16, 16], P('cuts'), may hold values from -3 to 3
- locked_vectors: bfloat16 [16, 64, 64, 512], P('cuts', None, 'slab'), may hold values from -6 to 6
- pivot_inverse: bfloat16 [2, 64, 512, 512], P(None, 'slab'), as said below
- hopping: float32 [64, 512], P('slab'), may hold values from 0.7 to 1.3
- partner: int32 [64, 512], P('slab'), may hold values from 0 to 511, each once within a row
- shift_index: int32 [16], P('cuts'), may hold values from 0 to 1
Outputs:
- next_block: float32 [16, 64, 16, 512], P('cuts', 'slab')
- coupling: float32 [16, 16, 16], P('cuts')
- ritz_values: float32 [16, 16], P('cuts')
The draws below stay inside these ranges and needn't reach their ends.
Inputs may be any that keep to these rules, and one draw needn't show every extreme that they name: `pivot_inverse`: every pivot block is symmetric. `partner`: each row is a permutation of 0 to 511.
All inputs are finite; a program needn't handle non-finite values.
Results may differ from the reference program's by a relative error of at most 0.03.
Values may be sent and summed in bfloat16 or wider, within the bound.
No kernel may reach another device: no remote copies, remote signals or barrier semaphores. Data moves between devices by JAX's collectives and lax.ppermute only.
A program may use at most 64 MiB of HBM per device.

```python
import jax
import jax.numpy as jnp
import numpy as np
from jax import lax

W = 512
NB = 16
LOCK = 64
NSHIFT = 2
JSWEEPS = 8
NSLICE = 16
NSLAB = 64
NORB = 32768


def draw_pivot_inverse(key, part):
    noise_key, diagonal_key = jax.random.split(jax.random.fold_in(key, 17))
    full_shape = (NSHIFT, NSLAB, W, W)
    noise_part = jax.random.normal(noise_key, full_shape, jnp.float32)
    symmetric = (noise_part + jnp.swapaxes(noise_part, -1, -2)) * (0.7071067811865476 * 0.45 * W ** (-0.5))
    diagonal = jax.random.uniform(diagonal_key, (NSHIFT, NSLAB, W), jnp.float32, 0.5, 1.1)
    return (symmetric + diagonal[..., None] * jnp.eye(W, dtype=jnp.float32)).astype(jnp.bfloat16)


def touch_ends(values, rng, smallest, top_value):
    dims = values.shape
    place = [jax.random.randint(jax.random.fold_in(rng, axis), (), 0, dims[axis]) for axis in range(len(dims))]
    values = values.at[tuple(place)].set(smallest)
    longest = dims.index(max(dims))
    place[longest] = (place[longest] + 1) % dims[longest]
    return values.at[tuple(place)].set(top_value)


def steps_of(rng, dims, cuts, smallest, largest):
    gain, own = 1.0, jax.random.fold_in(rng, 6)
    for position, parts in cuts:
        heights = jnp.exp(jax.random.uniform(jax.random.fold_in(own, position), (parts,), jnp.float32, smallest / len(cuts), largest / len(cuts)))
        gain = gain * jnp.repeat(heights, dims[position] // parts).reshape([-1 if axis == position else 1 for axis in range(len(dims))])
    return gain


def scatter_about(key, extent, width, most, cuts=(), held_as=jnp.bfloat16):
    values = jax.random.normal(key, extent, jnp.float32) * width
    if len(cuts) > 0:
        values = steps_of(key, extent, cuts, -0.22, 0.18) * values
    return jnp.clip(values, min=-most, max=most).astype(held_as)


def setup_inputs(seed: int = 0) -> dict:
    splits = jax.random.split(jax.random.key(seed), 9)
    return {
        "current_block": scatter_about(splits[0], (NSLICE, NSLAB, NB, W), 1.0, 6.0, ((0, 16), (1, 8)), jnp.float32),
        "previous_block": scatter_about(splits[1], (NSLICE, NSLAB, NB, W), 1.0, 6.0, ((0, 16), (1, 8)), jnp.float32),
        "previous_coupling": scatter_about(splits[2], (NSLICE, NB, NB), 0.5, 3.0, ((0, 16),), jnp.float32),
        "locked_vectors": scatter_about(splits[3], (NSLICE, LOCK, NSLAB, W), 1.0, 6.0, ((0, 16), (2, 8))),
        "pivot_inverse": draw_pivot_inverse(jax.random.fold_in(splits[8], 71), 0),
        "hopping": jnp.clip(0.7 + 0.59999996 * jax.random.uniform(splits[5], (NSLAB, W), jnp.float32) ** steps_of(splits[5], (NSLAB, W), ((0, 8),), -0.2, 0.2), 0.7, 1.3),
        "partner": jax.vmap(lambda own: jax.random.permutation(own, W))(jax.random.split(splits[6], NSLAB)).reshape((NSLAB, W)).astype(jnp.int32),
        "shift_index": touch_ends(jax.random.randint(splits[7], (NSLICE,), 0, NSHIFT), jax.random.fold_in(splits[7], 1), 0, NSHIFT - 1).astype(jnp.int32),
    }


def round_robin(order_size):
    players = list(range(order_size))
    plan = []
    for round_index in range(order_size - 1):
        plan.append([(min(players[place_index], players[order_size - 1 - place_index]), max(players[place_index], players[order_size - 1 - place_index])) for place_index in range(order_size // 2)])
        players = [players[0], players[-1]] + players[1:-1]
    return np.array(plan, dtype=np.int32)

def jacobi_values(matrix):
    order_size = matrix.shape[-1]
    plan = round_robin(order_size)
    identity = jnp.eye(order_size, dtype=matrix.dtype)
    highest = lax.Precision.HIGHEST

    def one_sweep(sweep_index, current):
        for round_index in range(order_size - 1):
            first_rows = plan[round_index, :, 0]
            second_rows = plan[round_index, :, 1]
            onehot_first = identity[first_rows]
            onehot_second = identity[second_rows]
            first_first = current[:, first_rows, first_rows]
            second_second = current[:, second_rows, second_rows]
            first_second = current[:, first_rows, second_rows]
            rotation_angle = 0.5 * jnp.arctan2(2.0 * first_second, second_second - first_first)
            cosine_less = jnp.cos(rotation_angle) - 1.0
            sine_value = jnp.sin(rotation_angle)
            rotation = identity[None] + jnp.einsum('hi,sh,hj->sij', onehot_first, cosine_less, onehot_first, precision=highest)
            rotation = rotation + jnp.einsum('hi,sh,hj->sij', onehot_second, cosine_less, onehot_second, precision=highest)
            rotation = rotation + jnp.einsum('hi,sh,hj->sij', onehot_first, sine_value, onehot_second, precision=highest)
            rotation = rotation - jnp.einsum('hi,sh,hj->sij', onehot_second, sine_value, onehot_first, precision=highest)
            current = jnp.einsum('sji,sjk,skl->sil', rotation, current, rotation, precision=highest)
        return current
    settled = lax.fori_loop(0, JSWEEPS, one_sweep, matrix)
    return jnp.sort(jnp.diagonal(settled, axis1=-2, axis2=-1), axis=-1)

def cholesky_upper(gram_matrix):
    order_size = gram_matrix.shape[-1]
    positions = jnp.arange(order_size, dtype=jnp.int32)
    columns = []
    for column_index in range(order_size):
        column = gram_matrix[:, :, column_index]
        for done_index in range(column_index):
            column = column - columns[done_index] * columns[done_index][:, column_index:column_index + 1]
        pivot_root = jnp.sqrt(column[:, column_index:column_index + 1])
        columns.append(jnp.where((positions >= column_index)[None, :], column / pivot_root, jnp.zeros_like(column)))
    lower_factor = jnp.stack(columns, axis=2)
    return jnp.swapaxes(lower_factor, 1, 2)

def upper_inverse(upper_factor):
    order_size = upper_factor.shape[-1]
    identity = jnp.eye(order_size, dtype=upper_factor.dtype)
    rows = [None] * order_size
    for row_index in range(order_size - 1, -1, -1):
        row_value = jnp.broadcast_to(identity[row_index][None, :], (upper_factor.shape[0], order_size))
        for later_index in range(row_index + 1, order_size):
            row_value = row_value - upper_factor[:, row_index, later_index:later_index + 1] * rows[later_index]
        rows[row_index] = row_value / upper_factor[:, row_index, row_index:row_index + 1]
    return jnp.stack(rows, axis=1)

def reference(current_block, previous_block, previous_coupling, locked_vectors, pivot_inverse, hopping, partner, shift_index):
    highest = lax.Precision.HIGHEST
    inverse = jnp.zeros(partner.shape, jnp.int32).at[jnp.arange(partner.shape[0], dtype=jnp.int32)[:, None], partner].set(jnp.broadcast_to(jnp.arange(partner.shape[1], dtype=jnp.int32), partner.shape))

    def one_slice(slice_index):
        current = current_block[slice_index]
        before = previous_block[slice_index]
        back_coupling = previous_coupling[slice_index]
        pivots = pivot_inverse[shift_index[slice_index]]

        def advance(carry_value, inputs):
            source, pivot_block, hop_row, part_row = inputs
            reduced = source - hop_row * jnp.take(carry_value, part_row, axis=1)
            result = jnp.dot(reduced.astype(jnp.bfloat16), pivot_block, preferred_element_type=jnp.float32)
            return (result, result)
        start_value = jnp.zeros((NB, W), jnp.float32)
        unused, lower_values = lax.scan(advance, start_value, (current, pivots, hopping, partner))

        def retreat(carry_value, inputs):
            lower_slab, pivot_block, hop_row, inverse_row = inputs
            result = lower_slab - jnp.dot(carry_value.astype(jnp.bfloat16), pivot_block, preferred_element_type=jnp.float32)
            carried = jnp.take(hop_row * result, inverse_row, axis=1)
            return (carried, result)
        unused_two, solved = lax.scan(retreat, start_value, (lower_values, pivots, hopping, inverse), reverse=True)
        projection = jnp.einsum('kaw,kbw->ab', current, solved, precision=highest) / NORB
        first = solved - jnp.einsum('kaw,ba->kbw', before, back_coupling, precision=highest)
        first = first - jnp.einsum('kaw,ab->kbw', current, projection, precision=highest)
        below = locked_vectors[jnp.maximum(slice_index - 1, 0)]
        above = locked_vectors[jnp.minimum(slice_index + 1, NSLICE - 1)]
        below = jnp.where(slice_index > 0, below, jnp.zeros_like(below))
        above = jnp.where(slice_index < NSLICE - 1, above, jnp.zeros_like(above))
        neighbours = jnp.concatenate([below, above], axis=0).astype(jnp.float32)
        coefficients = jnp.einsum('lkw,kbw->lb', neighbours, first, precision=highest) / NORB
        second = first - jnp.einsum('lkw,lb->kbw', neighbours, coefficients, precision=highest)
        gram_matrix = jnp.einsum('kaw,kbw->ab', second, second, precision=highest) / NORB
        upper_factor = cholesky_upper(gram_matrix[None])
        inverse_factor = upper_inverse(upper_factor)[0]
        upper_factor = upper_factor[0]
        following = jnp.einsum('kbw,ba->kaw', second, inverse_factor, precision=highest)
        return (following, upper_factor, projection)
    next_block, coupling, projections = lax.map(one_slice, jnp.arange(NSLICE, dtype=jnp.int32))
    ritz_values = jacobi_values(0.5 * (projections + jnp.swapaxes(projections, 1, 2)))
    return (next_block, coupling, ritz_values)
```

```python
import functools

import jax
import jax.numpy as jnp
from jax import lax
from jax.experimental import pallas as pl
from jax.experimental.pallas import tpu as pltpu
from jax.sharding import PartitionSpec as P

F32 = jnp.float32
BF16 = jnp.bfloat16
VMEM_LIMIT = 32 * 1024 * 1024
SMALL_LIMIT = 16 * 1024 * 1024
SECTIONS = 5


def mm(left, right):
    return jnp.dot(left, right, preferred_element_type=F32)


def mm_t(left, right):
    return lax.dot_general(left, right, (((1,), (1,)), ((), ())), preferred_element_type=F32)


def exact(left, right):
    return jnp.dot(left, right, precision=lax.Precision.HIGHEST, preferred_element_type=F32)


def exact_t(left, right):
    return lax.dot_general(
        left, right, (((1,), (1,)), ((), ())),
        precision=lax.Precision.HIGHEST, preferred_element_type=F32,
    )


def halves(value):
    high = value.astype(BF16)
    return high, (value - high.astype(F32)).astype(BF16)


def forward_kernel(
    shift_ref, hop_ref, part_ref, cur_ref, piv_ref,
    fg_ref, source_ref, own_ref, w_ref, pp_ref, op_ref,
    pbuf, in_sem,
):
    slabs, width = hop_ref.shape
    shift = shift_ref[0]

    def fetch(k):
        return pltpu.make_async_copy(piv_ref.at[shift, k], pbuf.at[k], in_sem.at[k])

    for k in range(slabs):
        fetch(k).start()
    down = lax.broadcasted_iota(jnp.int32, (width, width), 0)
    across = lax.broadcasted_iota(jnp.int32, (width, width), 1)
    part_columns = jnp.transpose(part_ref[...].astype(F32)).astype(jnp.int32)
    hop_columns = jnp.transpose(hop_ref[...])
    response = None
    vectors = None
    for k in range(slabs):
        gather = jnp.where(down == part_ref[k : k + 1, :], 1.0, 0.0).astype(BF16)
        weight = jnp.sum(
            jnp.where(across == part_columns[:, k : k + 1], hop_columns[:, k : k + 1], 0.0),
            axis=0, keepdims=True,
        )
        w_ref[k : k + 1, :] = weight
        fetch(k).wait()
        pivot = pbuf[k]
        permuted = mm(gather, pivot).astype(BF16)
        pp_ref[k] = permuted
        source = mm(cur_ref[k].astype(BF16), pivot)
        source_ref[k] = source
        if k == 0:
            unit = jnp.where(down == across, weight, 0.0).astype(BF16)
            response = -mm(unit, permuted)
            vectors = source
        else:
            response = -mm((response * weight).astype(BF16), permuted)
            vectors = source - mm((vectors * weight).astype(BF16), permuted)
        own_ref[k] = vectors
        op_ref[k] = response.astype(BF16)
    fg_ref[:width, :] = response.astype(BF16)
    fg_ref[width:, :] = vectors.astype(BF16)


def forward_range(shift_index, hopping, partner, current, pivot_inverse):
    slabs, rows, width = current.shape
    vm = pl.BlockSpec(memory_space=pltpu.VMEM)
    hbm = pl.BlockSpec(memory_space=pltpu.HBM)
    stack = jax.ShapeDtypeStruct((slabs, width, width), BF16)
    vectors = jax.ShapeDtypeStruct((slabs, rows, width), F32)
    return pl.pallas_call(
        forward_kernel,
        out_shape=(
            jax.ShapeDtypeStruct((width + rows, width), BF16),
            vectors,
            vectors,
            jax.ShapeDtypeStruct((slabs, width), F32),
            stack,
            stack,
        ),
        in_specs=[pl.BlockSpec(memory_space=pltpu.SMEM), vm, vm, vm, hbm],
        out_specs=(vm,) * 6,
        scratch_shapes=[
            pltpu.VMEM((slabs, width, width), BF16),
            pltpu.SemaphoreType.DMA((slabs,)),
        ],
        compiler_params=pltpu.CompilerParams(vmem_limit_bytes=VMEM_LIMIT),
        cost_estimate=pl.CostEstimate(
            flops=4 * slabs * width**3, bytes_accessed=6 * slabs * width**2, transcendentals=0
        ),
        name="forward_range",
    )(shift_index, hopping, partner, current, pivot_inverse)


def backward_kernel(
    shift_ref, hop_ref, part_ref, own_ref, op_ref, piv_ref,
    sh_ref, q_ref,
    pbuf, in_sem,
):
    slabs, width = hop_ref.shape
    shift = shift_ref[0]

    def fetch(k):
        return pltpu.make_async_copy(piv_ref.at[shift, k], pbuf.at[k], in_sem.at[k])

    last = slabs - 1
    for k in range(last, -1, -1):
        fetch(k).start()
    across = lax.broadcasted_iota(jnp.int32, (width, width), 1)
    part_columns = jnp.transpose(part_ref[...].astype(F32)).astype(jnp.int32)

    def scatter(k):
        return jnp.where(across == part_columns[:, k : k + 1], 1.0, 0.0).astype(BF16)

    fetch(last).wait()
    q_ref[last] = pbuf[last]
    response = op_ref[last].astype(F32)
    vectors = own_ref[last]
    for k in range(slabs - 2, -1, -1):
        fetch(k).wait()
        permuted = mm(scatter(k + 1), pbuf[k]).astype(BF16)
        q_ref[k] = permuted
        hop = hop_ref[k + 1 : k + 2, :]
        response = op_ref[k].astype(F32) - mm((response * hop).astype(BF16), permuted)
        vectors = own_ref[k] - mm((vectors * hop).astype(BF16), permuted)
    hop = hop_ref[0:1, :]
    spread = scatter(0)
    sh_ref[:width, :] = mm((response * hop).astype(BF16), spread).astype(BF16)
    sh_ref[width:, :] = mm((vectors * hop).astype(BF16), spread).astype(BF16)


def backward_range(shift_index, hopping, partner, own, op, pivot_inverse):
    slabs, rows, width = own.shape
    vm = pl.BlockSpec(memory_space=pltpu.VMEM)
    hbm = pl.BlockSpec(memory_space=pltpu.HBM)
    stack = jax.ShapeDtypeStruct((slabs, width, width), BF16)
    return pl.pallas_call(
        backward_kernel,
        out_shape=(jax.ShapeDtypeStruct((width + rows, width), BF16), stack),
        in_specs=[pl.BlockSpec(memory_space=pltpu.SMEM), vm, vm, vm, vm, hbm],
        out_specs=(vm, vm),
        scratch_shapes=[
            pltpu.VMEM((slabs, width, width), BF16),
            pltpu.SemaphoreType.DMA((slabs,)),
        ],
        compiler_params=pltpu.CompilerParams(vmem_limit_bytes=VMEM_LIMIT),
        cost_estimate=pl.CostEstimate(
            flops=4 * slabs * width**3, bytes_accessed=6 * slabs * width**2, transcendentals=0
        ),
        name="backward_range",
    )(shift_index, hopping, partner, own, op, pivot_inverse)


def lower_kernel(inflow_ref, source_ref, w_ref, pp_ref, low_ref):
    slabs = source_ref.shape[0]
    value = inflow_ref[...].astype(F32)
    for k in range(slabs):
        value = source_ref[k] - mm((value * w_ref[k : k + 1, :]).astype(BF16), pp_ref[k])
        low_ref[k] = value


def lower_sweep(inflow, source, weights, pp):
    slabs, rows, width = source.shape
    vm = pl.BlockSpec(memory_space=pltpu.VMEM)
    return pl.pallas_call(
        lower_kernel,
        out_shape=jax.ShapeDtypeStruct((slabs, rows, width), F32),
        in_specs=[vm] * 4,
        out_specs=vm,
        compiler_params=pltpu.CompilerParams(vmem_limit_bytes=SMALL_LIMIT),
        cost_estimate=pl.CostEstimate(
            flops=2 * slabs * rows * width**2, bytes_accessed=2 * slabs * width**2, transcendentals=0
        ),
        name="lower_sweep",
    )(inflow, source, weights, pp)


def known_kernel(cur_ref, prev_ref, below_ref, above_ref, out_ref):
    slabs, rows, width = cur_ref.shape
    near = 2 * below_ref.shape[1]
    two = 2 * rows
    total = None
    for k in range(slabs):
        cur_high, cur_low = halves(cur_ref[k])
        prev_high, prev_low = halves(prev_ref[k])
        stack = jnp.concatenate(
            [below_ref[k], above_ref[k], cur_high, prev_high, cur_low, prev_low], axis=0
        )
        part = mm_t(stack, stack)
        total = part if total is None else total + part
    first = total[near : near + two]
    second = total[near + two :]
    among = first[:, near : near + two] + first[:, near + two :]
    among = among + second[:, near : near + two] + second[:, near + two :]
    out_ref[:near, :] = total[:near, :near]
    out_ref[near : near + two, :] = first[:, :near] + second[:, :near]
    out_ref[near + two : near + two + rows, :] = jnp.zeros((rows, near), F32)
    out_ref[near + two + rows :, :] = jnp.concatenate(
        [jnp.zeros((rows, near - 2 * two), F32), among[:rows], among[rows:]], axis=1
    )


def known_products(current, previous, below, above):
    slabs, rows, width = current.shape
    near = 2 * below.shape[1]
    return pl.pallas_call(
        known_kernel,
        out_shape=jax.ShapeDtypeStruct((near + 4 * rows, near), F32),
        compiler_params=pltpu.CompilerParams(vmem_limit_bytes=SMALL_LIMIT),
        cost_estimate=pl.CostEstimate(
            flops=2 * slabs * 192 * 192 * width, bytes_accessed=3 * 2**19, transcendentals=0
        ),
        name="known_products",
    )(current, previous, below, above)


def upper_kernel(
    carried_ref, low_ref, hop_ref, cur_ref, prev_ref, below_ref, above_ref, known_ref, q_ref,
    x_ref, out_ref,
):
    slabs, rows, width = low_ref.shape
    near = 2 * below_ref.shape[1]
    push = carried_ref[...]
    total = None
    for k in range(slabs - 1, -1, -1):
        value = low_ref[k] - mm(push, q_ref[k])
        x_ref[k] = value
        push = (value * hop_ref[k : k + 1, :]).astype(BF16)
        high, low = halves(value)
        pair = jnp.concatenate([high, low], axis=0)
        cur_high, cur_low = halves(cur_ref[k])
        prev_high, prev_low = halves(prev_ref[k])
        stack = jnp.concatenate(
            [below_ref[k], above_ref[k], high, cur_high, prev_high, low, cur_low, prev_low], axis=0
        )
        part = mm_t(pair, stack)
        total = part if total is None else total + part
    joined = total[:rows] + total[rows:]
    three = 3 * rows
    own = joined[:, near : near + three] + joined[:, near + three :]
    top = near + 2 * rows
    out_ref[:top, :] = known_ref[:top, :]
    out_ref[top : top + rows, :] = joined[:, :near]
    out_ref[top + rows :, :] = known_ref[top + rows :, :] + jnp.concatenate(
        [own, jnp.zeros((rows, near - three), F32)], axis=1
    )


def upper_sweep(carried, low, hopping, current, previous, below, above, known, q):
    slabs, rows, width = low.shape
    vm = pl.BlockSpec(memory_space=pltpu.VMEM)
    return pl.pallas_call(
        upper_kernel,
        out_shape=(
            jax.ShapeDtypeStruct((slabs, rows, width), F32),
            jax.ShapeDtypeStruct(known.shape, F32),
        ),
        in_specs=[vm] * 9,
        out_specs=(vm, vm),
        compiler_params=pltpu.CompilerParams(vmem_limit_bytes=SMALL_LIMIT),
        cost_estimate=pl.CostEstimate(
            flops=2 * slabs * rows * width**2, bytes_accessed=2 * slabs * width**2, transcendentals=0
        ),
        name="upper_sweep",
    )(carried, low, hopping, current, previous, below, above, known, q)


def factor(gram):
    size = gram.shape[0]
    down = lax.broadcasted_iota(jnp.int32, (size, size), 0)
    across = lax.broadcasted_iota(jnp.int32, (size, size), 1)
    left = gram
    right = jnp.where(down == across, 1.0, 0.0)
    column = lax.broadcasted_iota(jnp.int32, (size, 1), 0)
    pivots = jnp.zeros((size, 1), F32)
    for j in range(size):
        pivot = left[j : j + 1, j : j + 1]
        pivots = jnp.where(column == j, pivot, pivots)
        if j < size - 1:
            scale = jnp.where(column > j, left[:, j : j + 1] / pivot, 0.0)
            left_row = left[j : j + 1, :]
            right_row = right[j : j + 1, :]
            left = left - scale * left_row
            right = right - scale * right_row
    inverse_root = 1.0 / jnp.sqrt(pivots)
    upper = jnp.where(across >= down, left * inverse_root, 0.0)
    return upper, right * inverse_root


def tridiagonal(matrix):
    size = matrix.shape[0]
    row = lax.broadcasted_iota(jnp.int32, (1, size), 1)
    down = lax.broadcasted_iota(jnp.int32, (size, size), 0)
    across = lax.broadcasted_iota(jnp.int32, (size, size), 1)
    diagonal = []
    squares = []

    def upright(value):
        return jnp.sum(jnp.where(down == across, value, 0.0), axis=1, keepdims=True)

    for j in range(size - 2):
        diagonal.append(matrix[j : j + 1, j : j + 1])
        beside = jnp.where(row > j, matrix[j : j + 1, :], 0.0)
        square = jnp.sum(beside * beside, axis=1, keepdims=True)
        squares.append(square)
        length = jnp.sqrt(square)
        lead = matrix[j : j + 1, j + 1 : j + 2]
        signed = jnp.where(lead >= 0.0, length, -length)
        half = square + length * jnp.abs(lead)
        scale = jnp.where(half > 0.0, 1.0 / jnp.where(half > 0.0, half, 1.0), 0.0)
        v_row = beside + jnp.where(row == j + 1, signed, 0.0)
        v_col = upright(v_row)
        p_row = scale * jnp.sum(matrix * v_col, axis=0, keepdims=True)
        along = 0.5 * scale * jnp.sum(p_row * v_row, axis=1, keepdims=True)
        w_row = p_row - along * v_row
        w_col = upright(w_row)
        matrix = matrix - (v_col * w_row + w_col * v_row)
    a = size - 2
    diagonal.append(matrix[a : a + 1, a : a + 1])
    diagonal.append(matrix[a + 1 : a + 2, a + 1 : a + 2])
    squares.append(matrix[a : a + 1, a + 1 : a + 2] * matrix[a : a + 1, a + 1 : a + 2])
    return diagonal, squares


def eigenvalues(matrix):
    size = matrix.shape[0]
    diagonal, squares = tridiagonal(matrix)
    bound = jnp.max(jnp.sum(jnp.abs(matrix), axis=1, keepdims=True), axis=0, keepdims=True)
    bound = bound * (1.0 + 2.0**-18)
    shape = (8, 128)
    wide_diagonal = [jnp.broadcast_to(value, shape) for value in diagonal]
    wide_squares = [jnp.broadcast_to(value, shape) for value in squares]
    lane = lax.broadcasted_iota(jnp.int32, shape, 1)
    level = lax.broadcasted_iota(jnp.int32, shape, 0)
    second_half = lane >= 64
    rank = 2 * level + jnp.where(second_half, 1, 0)
    point = (lane - jnp.where(second_half, 64, 0) + 1).astype(F32)
    start = jnp.broadcast_to(-bound, shape)
    step = jnp.broadcast_to(bound * (2.0 / 65.0), shape)
    tiny = 1e-30
    for _ in range(SECTIONS):
        shifted = start + point * step
        pivot = wide_diagonal[0] - shifted
        pivot = jnp.where(jnp.abs(pivot) < tiny, -tiny, pivot)
        count = jnp.where(pivot < 0.0, 1, 0)
        for i in range(1, size):
            pivot = wide_diagonal[i] - shifted - wide_squares[i - 1] / pivot
            pivot = jnp.where(jnp.abs(pivot) < tiny, -tiny, pivot)
            count = count + jnp.where(pivot < 0.0, 1, 0)
        passed = jnp.where(count <= rank, 1.0, 0.0)
        all_passed = jnp.sum(passed, axis=1, keepdims=True)
        late_passed = jnp.sum(jnp.where(second_half, passed, 0.0), axis=1, keepdims=True)
        cut = jnp.where(second_half, late_passed, all_passed - late_passed)
        start = start + cut * step
        step = step * (1.0 / 65.0)
    middle = start + 32.5 * step
    even = jnp.broadcast_to(middle[:, 0:1], shape)
    odd = jnp.broadcast_to(middle[:, 127:128], shape)
    place = jnp.where(lane == 2 * level, even, jnp.where(lane == 2 * level + 1, odd, 0.0))
    return jnp.sum(place, axis=0, keepdims=True)[:, :size]


def finish_kernel(
    scale, products_ref, coupling_ref, x_ref, cur_ref, prev_ref, below_ref, above_ref,
    next_ref, upper_ref, ritz_ref,
):
    slabs, rows, width = x_ref.shape
    near = products_ref.shape[1]
    two = 2 * rows
    products = products_ref[...] * scale
    near_near = products[:near]
    known_near = products[near : near + two]
    x_near = products[near + two : near + two + rows]
    tail = products[near + two + rows :]
    x_x = tail[:, :rows]
    x_known = tail[:, rows : 3 * rows]
    among = jnp.concatenate([tail[:, near - 2 * two : near - two], tail[:, near - two :]], axis=0)
    projection_t = tail[:, rows:two]
    fixed = jnp.concatenate([-projection_t, -coupling_ref[...]], axis=1)
    coefficients_t = x_near + exact(fixed, known_near)
    with_known = x_known + exact(fixed, among) - exact_t(coefficients_t, known_near)
    with_near = coefficients_t - exact(coefficients_t, near_near)
    gram = x_x + exact_t(fixed, x_known) - exact_t(coefficients_t, x_near)
    gram = gram + exact_t(with_known, fixed) - exact_t(with_near, coefficients_t)
    upper, inverse_t = factor(gram)
    upper_ref[...] = upper
    ritz_ref[...] = eigenvalues(0.5 * (projection_t + jnp.transpose(projection_t)))
    down = lax.broadcasted_iota(jnp.int32, (rows, rows), 0)
    across = lax.broadcasted_iota(jnp.int32, (rows, rows), 1)
    unit = jnp.where(down == across, 1.0, 0.0)
    weights = exact(inverse_t, jnp.concatenate([unit, fixed, -coefficients_t], axis=1))
    weight_high, weight_low = halves(weights)
    both = jnp.concatenate([weight_high, weight_low], axis=0)
    for k in range(slabs):
        x_high, x_low = halves(x_ref[k])
        cur_high, cur_low = halves(cur_ref[k])
        prev_high, prev_low = halves(prev_ref[k])
        stack = jnp.concatenate(
            [x_high, cur_high, prev_high, below_ref[k], above_ref[k]], axis=0
        )
        rest = jnp.concatenate([x_low, cur_low, prev_low], axis=0)
        main = mm(both, stack)
        next_ref[k] = main[:rows] + main[rows:] + mm(weight_high[:, : 3 * rows], rest)


def finish(scale, products, coupling, x, current, previous, below, above):
    slabs, rows, width = x.shape
    return pl.pallas_call(
        functools.partial(finish_kernel, scale),
        out_shape=(
            jax.ShapeDtypeStruct((slabs, rows, width), F32),
            jax.ShapeDtypeStruct((rows, rows), F32),
            jax.ShapeDtypeStruct((1, rows), F32),
        ),
        compiler_params=pltpu.CompilerParams(vmem_limit_bytes=SMALL_LIMIT),
        name="finish",
    )(products, coupling, x, current, previous, below, above)


def per_device(
    current_block,
    previous_block,
    previous_coupling,
    locked_vectors,
    pivot_inverse,
    hopping,
    partner,
    shift_index,
):
    devices = lax.axis_size("slab")
    slices = lax.axis_size("cuts")
    odd = lax.axis_index("slab") % 2 == 1
    current = current_block[0]
    previous = previous_block[0]
    slabs, rows, width = current.shape
    scale = 1.0 / (slabs * devices * width)
    swap = [(i, i ^ 1) for i in range(devices)]

    def both(value):
        other = lax.ppermute(value, "slab", swap)
        return jnp.where(odd, other, value), jnp.where(odd, value, other)

    fg, source, own, weights, pp, op = forward_range(
        shift_index, hopping, partner, current, pivot_inverse
    )
    fg_first, fg_second = both(fg)
    sh, q = backward_range(shift_index, hopping, partner, own, op, pivot_inverse)
    sh_first, sh_second = both(sh)
    f_first, g_first = fg_first[:width], fg_first[width:].astype(F32)
    f_second, g_second = fg_second[:width], fg_second[width:].astype(F32)
    s_first, h_first = sh_first[:width], sh_first[width:].astype(F32)
    s_second, h_second = sh_second[:width], sh_second[width:].astype(F32)

    locked = jnp.swapaxes(locked_vectors[0], 0, 1)
    even_pairs = [(i, i ^ 1) for i in range(slices)]
    odd_pairs = [(i, i + 1) for i in range(1, slices - 1, 2)]
    odd_pairs = odd_pairs + [(j, i) for i, j in odd_pairs]
    below = lax.ppermute(locked, "cuts", even_pairs)
    above = lax.ppermute(locked, "cuts", odd_pairs)

    into_first = jnp.zeros((rows, width), BF16)
    for r in range(0, devices - 2, 2):
        into_second = (g_first + mm(into_first, f_first)).astype(BF16)
        sent = (g_second + mm(into_second, f_second)).astype(BF16)
        into_first = into_first + lax.ppermute(sent, "slab", [(r, r + 2), (r + 1, r + 3)])
    into_second = (g_first + mm(into_first, f_first)).astype(BF16)
    back_second = h_second + mm(into_second, s_second)
    back_first = h_first + mm(into_first, s_first)
    low = lower_sweep(jnp.where(odd, into_second, into_first), source, weights, pp)
    known = known_products(current, previous, below, above)
    to_second = jnp.zeros((rows, width), BF16)
    for r in range(devices - 2, 0, -2):
        to_first = (back_second + mm_t(to_second, f_second)).astype(BF16)
        sent = (back_first + mm_t(to_first, f_first)).astype(BF16)
        to_second = to_second + lax.ppermute(sent, "slab", [(r, r - 2), (r + 1, r - 1)])
    to_first = (back_second + mm_t(to_second, f_second)).astype(BF16)
    carried = jnp.where(odd, to_second, to_first)
    x, products = upper_sweep(
        carried, low, hopping, current, previous, below, above, known, q
    )
    step = 1
    while step < devices:
        products = products + lax.ppermute(products, "slab", [(i, i ^ step) for i in range(devices)])
        step *= 2
    next_block, upper, ritz = finish(
        scale, products, previous_coupling[0], x, current, previous, below, above
    )
    return next_block[None], upper[None], ritz


def solution(mesh):
    return jax.shard_map(
        per_device,
        mesh=mesh,
        in_specs=(
            P("cuts", "slab", None, None),
            P("cuts", "slab", None, None),
            P("cuts", None, None),
            P("cuts", None, "slab", None),
            P(None, "slab", None, None),
            P("slab", None),
            P("slab", None),
            P("cuts"),
        ),
        out_specs=(P("cuts", "slab", None, None), P("cuts", None, None), P("cuts", None)),
        check_vma=False,
    )
```

```python
import functools

import jax
import jax.numpy as jnp
from jax import lax
from jax.experimental import pallas as pl
from jax.experimental.pallas import tpu as pltpu
from jax.sharding import PartitionSpec as P

F32 = jnp.float32
BF16 = jnp.bfloat16
VMEM_LIMIT = 56 * 1024 * 1024
SMALL_LIMIT = 16 * 1024 * 1024
SECTIONS = 4


def mm(left, right):
    return jnp.dot(left, right, preferred_element_type=F32)


def mm_t(left, right):
    return lax.dot_general(left, right, (((1,), (1,)), ((), ())), preferred_element_type=F32)


def exact(left, right):
    return jnp.dot(left, right, precision=lax.Precision.HIGHEST, preferred_element_type=F32)


def exact_t(left, right):
    return lax.dot_general(
        left, right, (((1,), (1,)), ((), ())),
        precision=lax.Precision.HIGHEST, preferred_element_type=F32,
    )


def halves(value):
    high = value.astype(BF16)
    return high, (value - high.astype(F32)).astype(BF16)


def forward_kernel(
    shift_ref, hop_ref, part_ref, cur_ref, piv_ref,
    fg_ref, source_ref, own_ref, w_ref, pp_ref, op_ref,
    pbuf, ppbuf, opbuf, in_sem, pp_sem, op_sem,
):
    slabs, width = hop_ref.shape
    shift = shift_ref[0]

    def fetch(k):
        return pltpu.make_async_copy(piv_ref.at[shift, k], pbuf.at[k], in_sem.at[k])

    def give_pp(k):
        return pltpu.make_async_copy(ppbuf.at[k], pp_ref.at[k], pp_sem.at[k])

    def give_op(k):
        return pltpu.make_async_copy(opbuf.at[k], op_ref.at[k], op_sem.at[k])

    for k in range(slabs):
        fetch(k).start()
    down = lax.broadcasted_iota(jnp.int32, (width, width), 0)
    across = lax.broadcasted_iota(jnp.int32, (width, width), 1)
    hop_all = -hop_ref[...]
    hop_high = hop_all.astype(BF16)
    rest = hop_all - hop_high.astype(F32)
    hop_mid = rest.astype(BF16)
    hop_low = (rest - hop_mid.astype(F32)).astype(BF16)
    hops = jnp.concatenate(
        [hop_high.astype(F32), hop_mid.astype(F32), hop_low.astype(F32)], axis=0
    ).astype(BF16)
    response = None
    vectors = None
    for k in range(slabs):
        gather = jnp.where(down == part_ref[k : k + 1, :], 1.0, 0.0).astype(BF16)
        spread = mm_t(hops, gather)
        weight = (
            spread[k : k + 1]
            + spread[slabs + k : slabs + k + 1]
            + spread[2 * slabs + k : 2 * slabs + k + 1]
        )
        w_ref[k : k + 1, :] = weight
        fetch(k).wait()
        mixed = mm(jnp.concatenate([gather, cur_ref[k].astype(BF16)], axis=0), pbuf[k])
        permuted = mixed[:width].astype(BF16)
        source = mixed[width:]
        ppbuf[k] = permuted
        give_pp(k).start()
        source_ref[k] = source
        if k == 0:
            unit = jnp.where(down == across, weight, 0.0).astype(BF16)
            response = mm(unit, permuted)
            vectors = source
        else:
            scaled = jnp.concatenate(
                [(response * weight).astype(BF16), (vectors * weight).astype(BF16)], axis=0
            )
            moved = mm(scaled, permuted)
            response = moved[:width]
            vectors = source + moved[width:]
        own_ref[k] = vectors
        opbuf[k] = response.astype(BF16)
        give_op(k).start()
    fg_ref[:width, :] = response.astype(BF16)
    fg_ref[width:, :] = vectors.astype(BF16)
    for k in range(slabs):
        give_pp(k).wait()
        give_op(k).wait()


def forward_range(shift_index, hopping, partner, current, pivot_inverse):
    slabs, rows, width = current.shape
    vm = pl.BlockSpec(memory_space=pltpu.VMEM)
    hbm = pl.BlockSpec(memory_space=pl.ANY)
    stack = jax.ShapeDtypeStruct((slabs, width, width), BF16)
    vectors = jax.ShapeDtypeStruct((slabs, rows, width), F32)
    return pl.pallas_call(
        forward_kernel,
        out_shape=(
            jax.ShapeDtypeStruct((width + rows, width), BF16),
            vectors,
            vectors,
            jax.ShapeDtypeStruct((slabs, width), F32),
            stack,
            stack,
        ),
        in_specs=[pl.BlockSpec(memory_space=pltpu.SMEM), vm, vm, vm, hbm],
        out_specs=(vm, vm, vm, vm, hbm, hbm),
        scratch_shapes=[pltpu.VMEM((slabs, width, width), BF16)] * 3
        + [pltpu.SemaphoreType.DMA((slabs,))] * 3,
        compiler_params=pltpu.CompilerParams(vmem_limit_bytes=VMEM_LIMIT),
        cost_estimate=pl.CostEstimate(
            flops=4 * slabs * width**3, bytes_accessed=6 * slabs * width**2, transcendentals=0
        ),
        name="forward_range",
    )(shift_index, hopping, partner, current, pivot_inverse)


def backward_kernel(
    shift_ref, hop_ref, part_ref, own_ref, op_ref, piv_ref,
    sh_ref, q_ref,
    pbuf, opbuf, qbuf, in_sem, op_sem, q_sem,
):
    slabs, width = hop_ref.shape
    shift = shift_ref[0]

    def fetch(k):
        return pltpu.make_async_copy(piv_ref.at[shift, k], pbuf.at[k], in_sem.at[k])

    def fetch_op(k):
        return pltpu.make_async_copy(op_ref.at[k], opbuf.at[k], op_sem.at[k])

    def give_q(k, source):
        return pltpu.make_async_copy(source.at[k], q_ref.at[k], q_sem.at[k])

    last = slabs - 1
    for k in range(last, -1, -1):
        fetch(k).start()
        fetch_op(k).start()
    across = lax.broadcasted_iota(jnp.int32, (width, width), 1)
    part_columns = jnp.transpose(part_ref[...].astype(F32)).astype(jnp.int32)

    def scatter(k):
        return jnp.where(across == part_columns[:, k : k + 1], 1.0, 0.0).astype(BF16)

    def scaled(k):
        hop = hop_ref[k : k + 1, :]
        return jnp.concatenate(
            [(response * hop).astype(BF16), (vectors * hop).astype(BF16)], axis=0
        )

    fetch(last).wait()
    give_q(last, pbuf).start()
    fetch_op(last).wait()
    response = opbuf[last].astype(F32)
    vectors = own_ref[last]
    for k in range(slabs - 2, -1, -1):
        fetch(k).wait()
        permuted = mm(scatter(k + 1), pbuf[k]).astype(BF16)
        qbuf[k] = permuted
        give_q(k, qbuf).start()
        moved = mm(scaled(k + 1), permuted)
        fetch_op(k).wait()
        response = opbuf[k].astype(F32) - moved[:width]
        vectors = own_ref[k] - moved[width:]
    sh_ref[...] = mm(scaled(0), scatter(0)).astype(BF16)
    give_q(last, pbuf).wait()
    for k in range(last):
        give_q(k, qbuf).wait()


def backward_range(shift_index, hopping, partner, own, op, pivot_inverse):
    slabs, rows, width = own.shape
    vm = pl.BlockSpec(memory_space=pltpu.VMEM)
    hbm = pl.BlockSpec(memory_space=pl.ANY)
    stack = jax.ShapeDtypeStruct((slabs, width, width), BF16)
    return pl.pallas_call(
        backward_kernel,
        out_shape=(jax.ShapeDtypeStruct((width + rows, width), BF16), stack),
        in_specs=[pl.BlockSpec(memory_space=pltpu.SMEM), vm, vm, vm, hbm, hbm],
        out_specs=(vm, hbm),
        scratch_shapes=[pltpu.VMEM((slabs, width, width), BF16)] * 3
        + [pltpu.SemaphoreType.DMA((slabs,))] * 3,
        compiler_params=pltpu.CompilerParams(vmem_limit_bytes=VMEM_LIMIT),
        cost_estimate=pl.CostEstimate(
            flops=4 * slabs * width**3, bytes_accessed=6 * slabs * width**2, transcendentals=0
        ),
        name="backward_range",
    )(shift_index, hopping, partner, own, op, pivot_inverse)


def by_order(own_ref, other_ref, run):
    odd = lax.axis_index("slab") % 2

    @pl.when(odd == 0)
    def _():
        run(own_ref, other_ref, 0)

    @pl.when(odd == 1)
    def _():
        run(other_ref, own_ref, 1)


def through(op_ref, value):
    width = op_ref.shape[1]
    return op_ref[width:, :].astype(F32) + mm(value, op_ref[:width, :])


def returned(op_ref, value):
    width = op_ref.shape[1]
    return mm_t(value, op_ref[:width, :])


def start_kernel(own_ref, other_ref, sent_ref):
    def run(first_ref, second_ref, odd):
        width = first_ref.shape[1]
        sent_ref[...] = through(second_ref, first_ref[width:, :]).astype(BF16)

    by_order(own_ref, other_ref, run)


def pass_kernel(own_ref, other_ref, into_ref, new_ref, into_out_ref, sent_ref):
    into = into_ref[...] + new_ref[...]
    into_out_ref[...] = into

    def run(first_ref, second_ref, odd):
        middle = through(first_ref, into).astype(BF16)
        sent_ref[...] = through(second_ref, middle).astype(BF16)

    by_order(own_ref, other_ref, run)


def turn_kernel(
    own_ref, other_ref, own_back_ref, other_back_ref, into_ref, new_ref,
    inflow_ref, first_back_ref, second_back_ref, sent_ref,
):
    into = into_ref[...] + new_ref[...]

    def run(first_ref, second_ref, odd):
        first_sh, second_sh = (
            (other_back_ref, own_back_ref) if odd else (own_back_ref, other_back_ref)
        )
        middle = through(first_ref, into).astype(BF16)
        second_back = through(second_sh, middle)
        first_back = through(first_sh, into)
        sent = first_back + returned(first_ref, second_back.astype(BF16))
        sent_ref[...] = sent.astype(BF16)
        first_back_ref[...] = first_back
        second_back_ref[...] = second_back
        inflow_ref[...] = middle if odd else into

    by_order(own_ref, other_ref, run)


def back_kernel(
    own_ref, other_ref, first_back_ref, second_back_ref, to_ref, new_ref, to_out_ref, sent_ref
):
    to = to_ref[...] + new_ref[...]
    to_out_ref[...] = to

    def run(first_ref, second_ref, odd):
        middle = (second_back_ref[...] + returned(second_ref, to)).astype(BF16)
        sent_ref[...] = (first_back_ref[...] + returned(first_ref, middle)).astype(BF16)

    by_order(own_ref, other_ref, run)


def small_call(kernel, outs, name, *args):
    width = args[0].shape[1]
    rows = args[0].shape[0] - width
    vm = pl.BlockSpec(memory_space=pltpu.VMEM)
    return pl.pallas_call(
        kernel,
        out_shape=tuple(jax.ShapeDtypeStruct((rows, width), t) for t in outs),
        in_specs=[vm] * len(args),
        out_specs=(vm,) * len(outs),
        compiler_params=pltpu.CompilerParams(vmem_limit_bytes=SMALL_LIMIT),
        cost_estimate=pl.CostEstimate(
            flops=4 * rows * width**2, bytes_accessed=4 * width**2, transcendentals=0
        ),
        name=name,
    )(*args)


def lower_kernel(inflow_ref, source_ref, w_ref, pp_ref, low_ref):
    slabs = source_ref.shape[0]
    value = inflow_ref[...].astype(F32)
    for k in range(slabs):
        value = source_ref[k] + mm((value * w_ref[k : k + 1, :]).astype(BF16), pp_ref[k])
        low_ref[k] = value


def lower_sweep(inflow, source, weights, pp):
    slabs, rows, width = source.shape
    vm = pl.BlockSpec(memory_space=pltpu.VMEM)
    return pl.pallas_call(
        lower_kernel,
        out_shape=jax.ShapeDtypeStruct((slabs, rows, width), F32),
        in_specs=[vm] * 4,
        out_specs=vm,
        compiler_params=pltpu.CompilerParams(vmem_limit_bytes=SMALL_LIMIT),
        cost_estimate=pl.CostEstimate(
            flops=2 * slabs * rows * width**2, bytes_accessed=2 * slabs * width**2, transcendentals=0
        ),
        name="lower_sweep",
    )(inflow, source, weights, pp)


def known_kernel(cur_ref, prev_ref, below_ref, above_ref, out_ref):
    slabs, rows, width = cur_ref.shape
    near = 2 * below_ref.shape[1]
    two = 2 * rows
    total = None
    for k in range(slabs):
        cur_high, cur_low = halves(cur_ref[k])
        prev_high, prev_low = halves(prev_ref[k])
        stack = jnp.concatenate(
            [below_ref[k], above_ref[k], cur_high, prev_high, cur_low, prev_low], axis=0
        )
        part = mm_t(stack, stack)
        total = part if total is None else total + part
    first = total[near : near + two]
    second = total[near + two :]
    among = first[:, near : near + two] + first[:, near + two :]
    among = among + second[:, near : near + two] + second[:, near + two :]
    out_ref[:near, :] = total[:near, :near]
    out_ref[near : near + two, :] = first[:, :near] + second[:, :near]
    out_ref[near + two : near + two + rows, :] = jnp.zeros((rows, near), F32)
    out_ref[near + two + rows :, :] = jnp.concatenate(
        [jnp.zeros((rows, near - 2 * two), F32), among[:rows], among[rows:]], axis=1
    )


def known_products(current, previous, below, above):
    slabs, rows, width = current.shape
    near = 2 * below.shape[1]
    return pl.pallas_call(
        known_kernel,
        out_shape=jax.ShapeDtypeStruct((near + 4 * rows, near), F32),
        compiler_params=pltpu.CompilerParams(vmem_limit_bytes=SMALL_LIMIT),
        cost_estimate=pl.CostEstimate(
            flops=2 * slabs * 192 * 192 * width, bytes_accessed=3 * 2**19, transcendentals=0
        ),
        name="known_products",
    )(current, previous, below, above)


def upper_kernel(
    own_ref, other_ref, second_back_ref, to_ref, new_ref, low_ref, hop_ref, cur_ref, prev_ref, below_ref, above_ref, known_ref, q_ref,
    x_ref, out_ref, carried,
):
    slabs, rows, width = low_ref.shape
    near = 2 * below_ref.shape[1]
    to = to_ref[...] + new_ref[...]

    def run(first_ref, second_ref, odd):
        if odd:
            carried[...] = to
        else:
            carried[...] = (second_back_ref[...] + returned(second_ref, to)).astype(BF16)

    by_order(own_ref, other_ref, run)
    push = carried[...]
    total = None
    for k in range(slabs - 1, -1, -1):
        value = low_ref[k] - mm(push, q_ref[k])
        x_ref[k] = value
        push = (value * hop_ref[k : k + 1, :]).astype(BF16)
        high, low = halves(value)
        pair = jnp.concatenate([high, low], axis=0)
        cur_high, cur_low = halves(cur_ref[k])
        prev_high, prev_low = halves(prev_ref[k])
        stack = jnp.concatenate(
            [below_ref[k], above_ref[k], high, cur_high, prev_high, low, cur_low, prev_low], axis=0
        )
        part = mm_t(pair, stack)
        total = part if total is None else total + part
    joined = total[:rows] + total[rows:]
    three = 3 * rows
    own = joined[:, near : near + three] + joined[:, near + three :]
    top = near + 2 * rows
    out_ref[:top, :] = known_ref[:top, :]
    out_ref[top : top + rows, :] = joined[:, :near]
    out_ref[top + rows :, :] = known_ref[top + rows :, :] + jnp.concatenate(
        [own, jnp.zeros((rows, near - three), F32)], axis=1
    )


def upper_sweep(
    own, other, second_back, to, new, low, hopping, current, previous, below, above, known, q
):
    slabs, rows, width = low.shape
    vm = pl.BlockSpec(memory_space=pltpu.VMEM)
    return pl.pallas_call(
        upper_kernel,
        out_shape=(
            jax.ShapeDtypeStruct((slabs, rows, width), F32),
            jax.ShapeDtypeStruct(known.shape, F32),
        ),
        in_specs=[vm] * 13,
        out_specs=(vm, vm),
        scratch_shapes=[pltpu.VMEM((rows, width), BF16)],
        compiler_params=pltpu.CompilerParams(vmem_limit_bytes=SMALL_LIMIT),
        cost_estimate=pl.CostEstimate(
            flops=2 * slabs * rows * width**2, bytes_accessed=2 * slabs * width**2, transcendentals=0
        ),
        name="upper_sweep",
    )(own, other, second_back, to, new, low, hopping, current, previous, below, above, known, q)


def factor_steps(gram, done):
    size = gram.shape[0]
    down = lax.broadcasted_iota(jnp.int32, (size, size), 0)
    across = lax.broadcasted_iota(jnp.int32, (size, size), 1)
    left = gram
    right = jnp.where(down == across, 1.0, 0.0)
    column = lax.broadcasted_iota(jnp.int32, (size, 1), 0)
    pivots = jnp.zeros((size, 1), F32)
    for j in range(size):
        pivot = left[j : j + 1, j : j + 1]
        pivots = jnp.where(column == j, pivot, pivots)
        if j < size - 1:
            scale = jnp.where(column > j, left[:, j : j + 1] / pivot, 0.0)
            left_row = left[j : j + 1, :]
            right_row = right[j : j + 1, :]
            left = left - scale * left_row
            right = right - scale * right_row
            yield
    inverse_root = 1.0 / jnp.sqrt(pivots)
    done.append(jnp.where(across >= down, left * inverse_root, 0.0))
    done.append(right * inverse_root)


def eigenvalue_steps(matrix, done):
    size = matrix.shape[0]
    row = lax.broadcasted_iota(jnp.int32, (1, size), 1)
    down = lax.broadcasted_iota(jnp.int32, (size, size), 0)
    across = lax.broadcasted_iota(jnp.int32, (size, size), 1)
    diagonal = []
    squares = []
    bound = jnp.max(jnp.sum(jnp.abs(matrix), axis=1, keepdims=True), axis=0, keepdims=True)
    bound = bound * (1.0 + 2.0**-18)

    def upright(value):
        return jnp.sum(jnp.where(down == across, value, 0.0), axis=1, keepdims=True)

    for j in range(size - 2):
        diagonal.append(matrix[j : j + 1, j : j + 1])
        beside = jnp.where(row > j, matrix[j : j + 1, :], 0.0)
        square = jnp.sum(beside * beside, axis=1, keepdims=True)
        squares.append(square)
        length = jnp.sqrt(square)
        lead = matrix[j : j + 1, j + 1 : j + 2]
        signed = jnp.where(lead >= 0.0, length, -length)
        half = square + length * jnp.abs(lead)
        scale = jnp.where(half > 0.0, 1.0 / jnp.where(half > 0.0, half, 1.0), 0.0)
        v_row = beside + jnp.where(row == j + 1, signed, 0.0)
        v_col = upright(v_row)
        p_row = scale * jnp.sum(matrix * v_col, axis=0, keepdims=True)
        along = 0.5 * scale * jnp.sum(p_row * v_row, axis=1, keepdims=True)
        w_row = p_row - along * v_row
        w_col = upright(w_row)
        matrix = matrix - (v_col * w_row + w_col * v_row)
        yield
    a = size - 2
    diagonal.append(matrix[a : a + 1, a : a + 1])
    diagonal.append(matrix[a + 1 : a + 2, a + 1 : a + 2])
    squares.append(matrix[a : a + 1, a + 1 : a + 2] * matrix[a : a + 1, a + 1 : a + 2])
    shape = (8, 128)
    wide_diagonal = [jnp.broadcast_to(value, shape) for value in diagonal]
    wide_squares = [jnp.broadcast_to(value, shape) for value in squares]
    lane = lax.broadcasted_iota(jnp.int32, shape, 1)
    level = lax.broadcasted_iota(jnp.int32, shape, 0)
    second_half = lane >= 64
    rank = 2 * level + jnp.where(second_half, 1, 0)
    point = (lane - jnp.where(second_half, 64, 0) + 1).astype(F32)
    start = jnp.broadcast_to(-bound, shape)
    step = jnp.broadcast_to(bound * (2.0 / 65.0), shape)
    tiny = 1e-30
    for _ in range(SECTIONS):
        shifted = start + point * step
        pivot = wide_diagonal[0] - shifted
        pivot = jnp.where(jnp.abs(pivot) < tiny, -tiny, pivot)
        count = jnp.where(pivot < 0.0, 1, 0)
        for i in range(1, size):
            pivot = wide_diagonal[i] - shifted - wide_squares[i - 1] / pivot
            pivot = jnp.where(jnp.abs(pivot) < tiny, -tiny, pivot)
            count = count + jnp.where(pivot < 0.0, 1, 0)
            if i % 4 == 0:
                yield
        passed = jnp.where(count <= rank, 1.0, 0.0)
        all_passed = jnp.sum(passed, axis=1, keepdims=True)
        late_passed = jnp.sum(jnp.where(second_half, passed, 0.0), axis=1, keepdims=True)
        cut = jnp.where(second_half, late_passed, all_passed - late_passed)
        start = start + cut * step
        step = step * (1.0 / 65.0)
    middle = start + 32.5 * step
    even = jnp.broadcast_to(middle[:, 0:1], shape)
    odd = jnp.broadcast_to(middle[:, 127:128], shape)
    place = jnp.where(lane == 2 * level, even, jnp.where(lane == 2 * level + 1, odd, 0.0))
    done.append(jnp.sum(place, axis=0, keepdims=True)[:, :size])


def finish_kernel(
    scale, products_ref, coupling_ref, x_ref, cur_ref, prev_ref, below_ref, above_ref,
    next_ref, upper_ref, ritz_ref,
):
    slabs, rows, width = x_ref.shape
    near = products_ref.shape[1]
    two = 2 * rows
    products = products_ref[...] * scale
    near_near = products[:near]
    known_near = products[near : near + two]
    x_near = products[near + two : near + two + rows]
    tail = products[near + two + rows :]
    x_x = tail[:, :rows]
    x_known = tail[:, rows : 3 * rows]
    among = jnp.concatenate([tail[:, near - 2 * two : near - two], tail[:, near - two :]], axis=0)
    projection_t = tail[:, rows:two]
    ritz = []
    eigen = eigenvalue_steps(0.5 * (projection_t + jnp.transpose(projection_t)), ritz)
    next(eigen)
    fixed = jnp.concatenate([-projection_t, -coupling_ref[...]], axis=1)
    coefficients_t = x_near + exact(fixed, known_near)
    next(eigen)
    with_known = x_known + exact(fixed, among) - exact_t(coefficients_t, known_near)
    with_near = coefficients_t - exact(coefficients_t, near_near)
    next(eigen)
    gram = x_x + exact_t(fixed, x_known) - exact_t(coefficients_t, x_near)
    gram = gram + exact_t(with_known, fixed) - exact_t(with_near, coefficients_t)
    next(eigen)
    factors = []
    for _ in factor_steps(gram, factors):
        next(eigen)
    upper, inverse_t = factors
    upper_ref[...] = upper
    next(eigen)
    down = lax.broadcasted_iota(jnp.int32, (rows, rows), 0)
    across = lax.broadcasted_iota(jnp.int32, (rows, rows), 1)
    unit = jnp.where(down == across, 1.0, 0.0)
    weights = exact(inverse_t, jnp.concatenate([unit, fixed, -coefficients_t], axis=1))
    weight_high, weight_low = halves(weights)
    both = jnp.concatenate([weight_high, weight_low], axis=0)
    for k in range(slabs):
        x_high, x_low = halves(x_ref[k])
        cur_high, cur_low = halves(cur_ref[k])
        prev_high, prev_low = halves(prev_ref[k])
        stack = jnp.concatenate(
            [x_high, cur_high, prev_high, below_ref[k], above_ref[k]], axis=0
        )
        rest = jnp.concatenate([x_low, cur_low, prev_low], axis=0)
        main = mm(both, stack)
        next_ref[k] = main[:rows] + main[rows:] + mm(weight_high[:, : 3 * rows], rest)
        next(eigen, None)
    for _ in eigen:
        pass
    ritz_ref[...] = ritz[0]


def finish(scale, products, coupling, x, current, previous, below, above):
    slabs, rows, width = x.shape
    return pl.pallas_call(
        functools.partial(finish_kernel, scale),
        out_shape=(
            jax.ShapeDtypeStruct((slabs, rows, width), F32),
            jax.ShapeDtypeStruct((rows, rows), F32),
            jax.ShapeDtypeStruct((1, rows), F32),
        ),
        compiler_params=pltpu.CompilerParams(vmem_limit_bytes=SMALL_LIMIT),
        name="finish",
    )(products, coupling, x, current, previous, below, above)


def per_device(
    current_block,
    previous_block,
    previous_coupling,
    locked_vectors,
    pivot_inverse,
    hopping,
    partner,
    shift_index,
):
    devices = lax.axis_size("slab")
    slices = lax.axis_size("cuts")
    current = current_block[0]
    previous = previous_block[0]
    slabs, rows, width = current.shape
    scale = 1.0 / (slabs * devices * width)
    swap = [(i, i ^ 1) for i in range(devices)]

    fg, source, own, weights, pp, op = forward_range(
        shift_index, hopping, partner, current, pivot_inverse
    )
    fg_other = lax.ppermute(fg, "slab", swap)
    sh, q = backward_range(shift_index, hopping, partner, own, op, pivot_inverse)
    sh_other = lax.ppermute(sh, "slab", swap)

    locked = jnp.swapaxes(locked_vectors[0], 0, 1)
    even_pairs = [(i, i ^ 1) for i in range(slices)]
    odd_pairs = [(i, i + 1) for i in range(1, slices - 1, 2)]
    odd_pairs = odd_pairs + [(j, i) for i, j in odd_pairs]
    below = lax.ppermute(locked, "cuts", even_pairs)
    above = lax.ppermute(locked, "cuts", odd_pairs)

    def up(value, r):
        return lax.ppermute(value, "slab", [(r, r + 2), (r + 1, r + 3)])

    def back(value, r):
        return lax.ppermute(value, "slab", [(r, r - 2), (r + 1, r - 1)])

    (sent,) = small_call(start_kernel, (BF16,), "start", fg, fg_other)
    into = jnp.zeros((rows, width), BF16)
    new = up(sent, 0)
    for r in range(2, devices - 2, 2):
        into, sent = small_call(pass_kernel, (BF16, BF16), "pass_on", fg, fg_other, into, new)
        new = up(sent, r)
    inflow, first_back, second_back, sent = small_call(
        turn_kernel, (BF16, F32, F32, BF16), "turn", fg, fg_other, sh, sh_other, into, new
    )
    low = lower_sweep(inflow, source, weights, pp)
    known = known_products(current, previous, below, above)
    to = jnp.zeros((rows, width), BF16)
    new = back(sent, devices - 2)
    for r in range(devices - 4, 0, -2):
        to, sent = small_call(
            back_kernel, (BF16, BF16), "pass_back", fg, fg_other, first_back, second_back, to, new
        )
        new = back(sent, r)
    x, products = upper_sweep(
        fg, fg_other, second_back, to, new, low, hopping, current, previous, below, above, known, q
    )
    step = 1
    while step < devices:
        products = products + lax.ppermute(products, "slab", [(i, i ^ step) for i in range(devices)])
        step *= 2
    next_block, upper, ritz = finish(
        scale, products, previous_coupling[0], x, current, previous, below, above
    )
    return next_block[None], upper[None], ritz


def solution(mesh):
    return jax.shard_map(
        per_device,
        mesh=mesh,
        in_specs=(
            P("cuts", "slab", None, None),
            P("cuts", "slab", None, None),
            P("cuts", None, None),
            P("cuts", None, "slab", None),
            P(None, "slab", None, None),
            P("slab", None),
            P("slab", None),
            P("cuts"),
        ),
        out_specs=(P("cuts", "slab", None, None), P("cuts", None, None), P("cuts", None)),
        check_vma=False,
    )
```

```python
import functools

import jax
import jax.numpy as jnp
from jax import lax
from jax.experimental import pallas as pl
from jax.experimental.pallas import tpu as pltpu
from jax.sharding import PartitionSpec as P

F32 = jnp.float32
BF16 = jnp.bfloat16
VMEM_LIMIT = 56 * 1024 * 1024
SMALL_LIMIT = 16 * 1024 * 1024
SECTIONS = 4
AHEAD = 3


def mm(left, right):
    return jnp.dot(left, right, preferred_element_type=F32)


def mm_t(left, right):
    return lax.dot_general(left, right, (((1,), (1,)), ((), ())), preferred_element_type=F32)


def exact(left, right):
    return jnp.dot(left, right, precision=lax.Precision.HIGHEST, preferred_element_type=F32)


def exact_t(left, right):
    return lax.dot_general(
        left, right, (((1,), (1,)), ((), ())),
        precision=lax.Precision.HIGHEST, preferred_element_type=F32,
    )


def halves(value):
    high = value.astype(BF16)
    return high, (value - high.astype(F32)).astype(BF16)


def forward_kernel(
    shift_ref, hop_ref, part_ref, cur_ref, piv_ref,
    fg_ref, own_ref, op_ref,
    pbuf, opbuf, hops, parts, sources, in_sem, op_sem, small_sem,
):
    slabs, width = hop_ref.shape
    shift = shift_ref[0]

    def fetch(k):
        return pltpu.make_async_copy(piv_ref.at[shift, k], pbuf.at[k], in_sem.at[k])

    def give_op(k):
        return pltpu.make_async_copy(opbuf.at[k], op_ref.at[k], op_sem.at[k])

    small = [
        pltpu.make_async_copy(part_ref, parts, small_sem.at[0]),
        pltpu.make_async_copy(hop_ref, hops, small_sem.at[1]),
        pltpu.make_async_copy(cur_ref, sources, small_sem.at[2]),
    ]
    for copy in small:
        copy.start()
    for k in range(AHEAD):
        fetch(k).start()
    down = lax.broadcasted_iota(jnp.int32, (width, width), 0)
    for copy in small:
        copy.wait()
    vectors = None
    for k in range(slabs):
        gather = jnp.where(
            down == parts[k : k + 1, :], -hops[k : k + 1, :], 0.0
        ).astype(BF16)
        fetch(k).wait()
        if k + AHEAD < slabs:
            fetch(k + AHEAD).start()
        mixed = mm(jnp.concatenate([gather, sources[k].astype(BF16)], axis=0), pbuf[k])
        step = mixed[:width].astype(BF16)
        source = mixed[width:]
        if k == 0:
            opbuf[k] = step
            vectors = source
        else:
            moved = mm(jnp.concatenate([opbuf[k - 1], vectors.astype(BF16)], axis=0), step)
            opbuf[k] = moved[:width].astype(BF16)
            vectors = source + moved[width:]
        give_op(k).start()
        own_ref[k] = vectors
    fg_ref[:width, :] = opbuf[slabs - 1]
    fg_ref[width:, :] = vectors.astype(BF16)
    for k in range(slabs):
        give_op(k).wait()


def forward_range(shift_index, hopping, partner, current, pivot_inverse):
    slabs, rows, width = current.shape
    vm = pl.BlockSpec(memory_space=pltpu.VMEM)
    hbm = pl.BlockSpec(memory_space=pl.ANY)
    return pl.pallas_call(
        forward_kernel,
        out_shape=(
            jax.ShapeDtypeStruct((width + rows, width), BF16),
            jax.ShapeDtypeStruct((slabs, rows, width), F32),
            jax.ShapeDtypeStruct((slabs, width, width), BF16),
        ),
        in_specs=[pl.BlockSpec(memory_space=pltpu.SMEM), hbm, hbm, hbm, hbm],
        out_specs=(vm, vm, hbm),
        scratch_shapes=[
            pltpu.VMEM((slabs, width, width), BF16),
            pltpu.VMEM((slabs, width, width), BF16),
            pltpu.VMEM((slabs, width), F32),
            pltpu.VMEM((slabs, width), jnp.int32),
            pltpu.VMEM((slabs, rows, width), F32),
            pltpu.SemaphoreType.DMA((slabs,)),
            pltpu.SemaphoreType.DMA((slabs,)),
            pltpu.SemaphoreType.DMA((3,)),
        ],
        compiler_params=pltpu.CompilerParams(vmem_limit_bytes=VMEM_LIMIT),
        cost_estimate=pl.CostEstimate(
            flops=4 * slabs * width**3, bytes_accessed=6 * slabs * width**2, transcendentals=0
        ),
        name="forward_range",
    )(shift_index, hopping, partner, current, pivot_inverse)


def backward_kernel(
    shift_ref, hop_ref, part_ref, own_ref, op_ref, piv_ref,
    sh_ref, q_ref,
    pbuf, opbuf, qbuf, in_sem, op_sem, q_sem,
):
    slabs, width = hop_ref.shape
    shift = shift_ref[0]

    def fetch(k):
        return pltpu.make_async_copy(piv_ref.at[shift, k], pbuf.at[k], in_sem.at[k])

    def fetch_op(k):
        return pltpu.make_async_copy(op_ref.at[k], opbuf.at[k], op_sem.at[k])

    def give_q(k, source):
        return pltpu.make_async_copy(source.at[k], q_ref.at[k], q_sem.at[k])

    last = slabs - 1
    for k in range(last, -1, -1):
        fetch(k).start()
        fetch_op(k).start()
    across = lax.broadcasted_iota(jnp.int32, (width, width), 1)
    part_columns = jnp.transpose(part_ref[...].astype(F32)).astype(jnp.int32)

    def scatter(k):
        return jnp.where(across == part_columns[:, k : k + 1], 1.0, 0.0).astype(BF16)

    def scaled(k):
        hop = hop_ref[k : k + 1, :]
        return jnp.concatenate(
            [(response * hop).astype(BF16), (vectors * hop).astype(BF16)], axis=0
        )

    fetch(last).wait()
    give_q(last, pbuf).start()
    fetch_op(last).wait()
    response = opbuf[last].astype(F32)
    vectors = own_ref[last]
    for k in range(slabs - 2, -1, -1):
        fetch(k).wait()
        permuted = mm(scatter(k + 1), pbuf[k]).astype(BF16)
        qbuf[k] = permuted
        give_q(k, qbuf).start()
        moved = mm(scaled(k + 1), permuted)
        fetch_op(k).wait()
        response = opbuf[k].astype(F32) - moved[:width]
        vectors = own_ref[k] - moved[width:]
    sh_ref[...] = mm(scaled(0), scatter(0)).astype(BF16)
    give_q(last, pbuf).wait()
    for k in range(last):
        give_q(k, qbuf).wait()


def backward_range(shift_index, hopping, partner, own, op, pivot_inverse):
    slabs, rows, width = own.shape
    vm = pl.BlockSpec(memory_space=pltpu.VMEM)
    hbm = pl.BlockSpec(memory_space=pl.ANY)
    stack = jax.ShapeDtypeStruct((slabs, width, width), BF16)
    return pl.pallas_call(
        backward_kernel,
        out_shape=(jax.ShapeDtypeStruct((width + rows, width), BF16), stack),
        in_specs=[pl.BlockSpec(memory_space=pltpu.SMEM), vm, vm, vm, hbm, hbm],
        out_specs=(vm, hbm),
        scratch_shapes=[pltpu.VMEM((slabs, width, width), BF16)] * 3
        + [pltpu.SemaphoreType.DMA((slabs,))] * 3,
        compiler_params=pltpu.CompilerParams(vmem_limit_bytes=VMEM_LIMIT),
        cost_estimate=pl.CostEstimate(
            flops=4 * slabs * width**3, bytes_accessed=6 * slabs * width**2, transcendentals=0
        ),
        name="backward_range",
    )(shift_index, hopping, partner, own, op, pivot_inverse)


def by_order(own_ref, other_ref, run):
    odd = lax.axis_index("slab") % 2

    @pl.when(odd == 0)
    def _():
        run(own_ref, other_ref, 0)

    @pl.when(odd == 1)
    def _():
        run(other_ref, own_ref, 1)


def through(op_ref, value):
    width = op_ref.shape[1]
    return op_ref[width:, :].astype(F32) + mm(value, op_ref[:width, :])


def returned(op_ref, value):
    width = op_ref.shape[1]
    return mm_t(value, op_ref[:width, :])


def start_kernel(own_ref, other_ref, sent_ref):
    def run(first_ref, second_ref, odd):
        width = first_ref.shape[1]
        sent_ref[...] = through(second_ref, first_ref[width:, :]).astype(BF16)

    by_order(own_ref, other_ref, run)


def pass_kernel(own_ref, other_ref, into_ref, new_ref, into_out_ref, sent_ref):
    into = into_ref[...] + new_ref[...]
    into_out_ref[...] = into

    def run(first_ref, second_ref, odd):
        middle = through(first_ref, into).astype(BF16)
        sent_ref[...] = through(second_ref, middle).astype(BF16)

    by_order(own_ref, other_ref, run)


def turn_kernel(
    own_ref, other_ref, own_back_ref, other_back_ref, into_ref, new_ref,
    inflow_ref, first_back_ref, second_back_ref, sent_ref,
):
    into = into_ref[...] + new_ref[...]

    def run(first_ref, second_ref, odd):
        first_sh, second_sh = (
            (other_back_ref, own_back_ref) if odd else (own_back_ref, other_back_ref)
        )
        middle = through(first_ref, into).astype(BF16)
        second_back = through(second_sh, middle)
        first_back = through(first_sh, into)
        sent = first_back + returned(first_ref, second_back.astype(BF16))
        sent_ref[...] = sent.astype(BF16)
        first_back_ref[...] = first_back
        second_back_ref[...] = second_back
        inflow_ref[...] = middle if odd else into

    by_order(own_ref, other_ref, run)


def back_kernel(
    own_ref, other_ref, first_back_ref, second_back_ref, to_ref, new_ref, to_out_ref, sent_ref
):
    to = to_ref[...] + new_ref[...]
    to_out_ref[...] = to

    def run(first_ref, second_ref, odd):
        middle = (second_back_ref[...] + returned(second_ref, to)).astype(BF16)
        sent_ref[...] = (first_back_ref[...] + returned(first_ref, middle)).astype(BF16)

    by_order(own_ref, other_ref, run)


def small_call(kernel, outs, name, *args):
    width = args[0].shape[1]
    rows = args[0].shape[0] - width
    vm = pl.BlockSpec(memory_space=pltpu.VMEM)
    return pl.pallas_call(
        kernel,
        out_shape=tuple(jax.ShapeDtypeStruct((rows, width), t) for t in outs),
        in_specs=[vm] * len(args),
        out_specs=(vm,) * len(outs),
        compiler_params=pltpu.CompilerParams(vmem_limit_bytes=SMALL_LIMIT),
        cost_estimate=pl.CostEstimate(
            flops=4 * rows * width**2, bytes_accessed=4 * width**2, transcendentals=0
        ),
        name=name,
    )(*args)


def lower_kernel(shift_ref, inflow_ref, cur_ref, hop_ref, part_ref, piv_ref, low_ref, pbuf, sem):
    slabs, rows, width = cur_ref.shape
    shift = shift_ref[0]

    def fetch(k):
        return pltpu.make_async_copy(piv_ref.at[shift, k], pbuf.at[k], sem.at[k])

    for k in range(slabs):
        fetch(k).start()
    down = lax.broadcasted_iota(jnp.int32, (width, width), 0)
    value = inflow_ref[...].astype(F32)
    for k in range(slabs):
        bonds = jnp.where(down == part_ref[k : k + 1, :], 1.0, 0.0).astype(BF16)
        high, low = halves(value)
        pulled = mm(jnp.concatenate([high, low], axis=0), bonds)
        reduced = cur_ref[k] - hop_ref[k : k + 1, :] * (pulled[:rows] + pulled[rows:])
        fetch(k).wait()
        value = mm(reduced.astype(BF16), pbuf[k])
        low_ref[k] = value


def lower_sweep(shift_index, inflow, current, hopping, partner, pivot_inverse):
    slabs, rows, width = current.shape
    vm = pl.BlockSpec(memory_space=pltpu.VMEM)
    return pl.pallas_call(
        lower_kernel,
        out_shape=jax.ShapeDtypeStruct((slabs, rows, width), F32),
        in_specs=[pl.BlockSpec(memory_space=pltpu.SMEM), vm, vm, vm, vm]
        + [pl.BlockSpec(memory_space=pl.ANY)],
        out_specs=vm,
        scratch_shapes=[
            pltpu.VMEM((slabs, width, width), BF16),
            pltpu.SemaphoreType.DMA((slabs,)),
        ],
        compiler_params=pltpu.CompilerParams(vmem_limit_bytes=SMALL_LIMIT),
        cost_estimate=pl.CostEstimate(
            flops=2 * slabs * rows * width**2, bytes_accessed=2 * slabs * width**2, transcendentals=0
        ),
        name="lower_sweep",
    )(shift_index, inflow, current, hopping, partner, pivot_inverse)


def known_kernel(cur_ref, prev_ref, below_ref, above_ref, out_ref):
    slabs, rows, width = cur_ref.shape
    near = 2 * below_ref.shape[1]
    two = 2 * rows
    total = None
    for k in range(slabs):
        cur_high, cur_low = halves(cur_ref[k])
        prev_high, prev_low = halves(prev_ref[k])
        stack = jnp.concatenate(
            [below_ref[k], above_ref[k], cur_high, prev_high, cur_low, prev_low], axis=0
        )
        part = mm_t(stack, stack)
        total = part if total is None else total + part
    first = total[near : near + two]
    second = total[near + two :]
    among = first[:, near : near + two] + first[:, near + two :]
    among = among + second[:, near : near + two] + second[:, near + two :]
    out_ref[:near, :] = total[:near, :near]
    out_ref[near : near + two, :] = first[:, :near] + second[:, :near]
    out_ref[near + two : near + two + rows, :] = jnp.zeros((rows, near), F32)
    out_ref[near + two + rows :, :] = jnp.concatenate(
        [jnp.zeros((rows, near - 2 * two), F32), among[:rows], among[rows:]], axis=1
    )


def known_products(current, previous, below, above):
    slabs, rows, width = current.shape
    near = 2 * below.shape[1]
    return pl.pallas_call(
        known_kernel,
        out_shape=jax.ShapeDtypeStruct((near + 4 * rows, near), F32),
        compiler_params=pltpu.CompilerParams(vmem_limit_bytes=SMALL_LIMIT),
        cost_estimate=pl.CostEstimate(
            flops=2 * slabs * 192 * 192 * width, bytes_accessed=3 * 2**19, transcendentals=0
        ),
        name="known_products",
    )(current, previous, below, above)


def upper_kernel(
    own_ref, other_ref, second_back_ref, to_ref, new_ref, low_ref, hop_ref, cur_ref, prev_ref, below_ref, above_ref, known_ref, q_ref,
    x_ref, out_ref, carried,
):
    slabs, rows, width = low_ref.shape
    near = 2 * below_ref.shape[1]
    to = to_ref[...] + new_ref[...]

    def run(first_ref, second_ref, odd):
        if odd:
            carried[...] = to
        else:
            carried[...] = (second_back_ref[...] + returned(second_ref, to)).astype(BF16)

    by_order(own_ref, other_ref, run)
    push = carried[...]
    total = None
    for k in range(slabs - 1, -1, -1):
        value = low_ref[k] - mm(push, q_ref[k])
        x_ref[k] = value
        push = (value * hop_ref[k : k + 1, :]).astype(BF16)
        high, low = halves(value)
        pair = jnp.concatenate([high, low], axis=0)
        cur_high, cur_low = halves(cur_ref[k])
        prev_high, prev_low = halves(prev_ref[k])
        stack = jnp.concatenate(
            [below_ref[k], above_ref[k], high, cur_high, prev_high, low, cur_low, prev_low], axis=0
        )
        part = mm_t(pair, stack)
        total = part if total is None else total + part
    joined = total[:rows] + total[rows:]
    three = 3 * rows
    own = joined[:, near : near + three] + joined[:, near + three :]
    top = near + 2 * rows
    out_ref[:top, :] = known_ref[:top, :]
    out_ref[top : top + rows, :] = joined[:, :near]
    out_ref[top + rows :, :] = known_ref[top + rows :, :] + jnp.concatenate(
        [own, jnp.zeros((rows, near - three), F32)], axis=1
    )


def upper_sweep(
    own, other, second_back, to, new, low, hopping, current, previous, below, above, known, q
):
    slabs, rows, width = low.shape
    vm = pl.BlockSpec(memory_space=pltpu.VMEM)
    return pl.pallas_call(
        upper_kernel,
        out_shape=(
            jax.ShapeDtypeStruct((slabs, rows, width), F32),
            jax.ShapeDtypeStruct(known.shape, F32),
        ),
        in_specs=[vm] * 13,
        out_specs=(vm, vm),
        scratch_shapes=[pltpu.VMEM((rows, width), BF16)],
        compiler_params=pltpu.CompilerParams(vmem_limit_bytes=SMALL_LIMIT),
        cost_estimate=pl.CostEstimate(
            flops=2 * slabs * rows * width**2, bytes_accessed=2 * slabs * width**2, transcendentals=0
        ),
        name="upper_sweep",
    )(own, other, second_back, to, new, low, hopping, current, previous, below, above, known, q)


def factor_steps(gram, done):
    size = gram.shape[0]
    down = lax.broadcasted_iota(jnp.int32, (size, size), 0)
    across = lax.broadcasted_iota(jnp.int32, (size, size), 1)
    left = gram
    right = jnp.where(down == across, 1.0, 0.0)
    column = lax.broadcasted_iota(jnp.int32, (size, 1), 0)
    pivots = jnp.zeros((size, 1), F32)
    for j in range(size):
        pivot = left[j : j + 1, j : j + 1]
        pivots = jnp.where(column == j, pivot, pivots)
        if j < size - 1:
            scale = jnp.where(column > j, left[:, j : j + 1] / pivot, 0.0)
            left_row = left[j : j + 1, :]
            right_row = right[j : j + 1, :]
            left = left - scale * left_row
            right = right - scale * right_row
            yield
    inverse_root = 1.0 / jnp.sqrt(pivots)
    done.append(jnp.where(across >= down, left * inverse_root, 0.0))
    done.append(right * inverse_root)


def eigenvalue_steps(matrix, done):
    size = matrix.shape[0]
    full = (size, 128)
    down = lax.broadcasted_iota(jnp.int32, full, 0)
    across = lax.broadcasted_iota(jnp.int32, full, 1)
    bound = jnp.max(jnp.sum(jnp.abs(matrix), axis=1, keepdims=True), axis=0, keepdims=True)
    bound = bound * (1.0 + 2.0**-18)
    matrix = jnp.concatenate([matrix, jnp.zeros((size, 128 - size), F32)], axis=1)
    diagonal = []
    squares = []

    def upright(value):
        return jnp.broadcast_to(
            jnp.sum(jnp.where(down == across, value, 0.0), axis=1, keepdims=True), full
        )

    def line(value, i):
        return jnp.broadcast_to(value[i : i + 1, :], full)

    def total(value):
        return jnp.broadcast_to(jnp.sum(value, axis=0, keepdims=True), full)

    row = line(matrix, 0)
    col = upright(row)
    for j in range(size - 2):
        diagonal.append(col[j : j + 1, :])
        next_row = line(matrix, j + 1)
        next_col = upright(next_row)
        below = jnp.where(down > j, col, 0.0)
        beside = jnp.where(across > j, row, 0.0)
        image_row = total(matrix * below)
        image_col = upright(image_row)
        square = total(below * below)
        squares.append(square[0:1, :])
        length = jnp.sqrt(square)
        lead = line(col, j + 1)
        signed = jnp.where(lead >= 0.0, length, -length)
        half = square + length * jnp.abs(lead)
        scale = jnp.where(half > 0.0, 1.0 / jnp.where(half > 0.0, half, 1.0), 0.0)
        v_row = beside + jnp.where(across == j + 1, signed, 0.0)
        v_col = below + jnp.where(down == j + 1, signed, 0.0)
        q_row = image_row + signed * next_row
        q_col = image_col + signed * next_col
        along = 0.5 * scale * (scale * total(q_col * v_col))
        w_row = scale * q_row - along * v_row
        w_col = scale * q_col - along * v_col
        matrix = matrix - (v_col * w_row + w_col * v_row)
        lead_v = line(v_col, j + 1)
        lead_w = line(w_col, j + 1)
        row = next_row - (v_row * lead_w + w_row * lead_v)
        col = next_col - (v_col * lead_w + w_col * lead_v)
        yield
    a = size - 2
    diagonal.append(col[a : a + 1, :])
    squares.append(col[a + 1 : a + 2, :] * col[a + 1 : a + 2, :])
    diagonal.append(upright(line(matrix, a + 1))[a + 1 : a + 2, :])
    shape = (8, 128)
    wide_diagonal = [jnp.broadcast_to(value, shape) for value in diagonal]
    wide_squares = [jnp.broadcast_to(value, shape) for value in squares]
    lane = lax.broadcasted_iota(jnp.int32, shape, 1)
    level = lax.broadcasted_iota(jnp.int32, shape, 0)
    second_half = lane >= 64
    rank = 2 * level + jnp.where(second_half, 1, 0)
    point = (lane - jnp.where(second_half, 64, 0) + 1).astype(F32)
    start = jnp.broadcast_to(-bound, shape)
    step = jnp.broadcast_to(bound * (2.0 / 65.0), shape)
    tiny = 1e-30
    for _ in range(SECTIONS):
        shifted = start + point * step
        pivot = wide_diagonal[0] - shifted
        pivot = jnp.where(jnp.abs(pivot) < tiny, -tiny, pivot)
        count = jnp.where(pivot < 0.0, 1, 0)
        for i in range(1, size):
            pivot = wide_diagonal[i] - shifted - wide_squares[i - 1] / pivot
            pivot = jnp.where(jnp.abs(pivot) < tiny, -tiny, pivot)
            count = count + jnp.where(pivot < 0.0, 1, 0)
            if i % 4 == 0:
                yield
        passed = jnp.where(count <= rank, 1.0, 0.0)
        all_passed = jnp.sum(passed, axis=1, keepdims=True)
        late_passed = jnp.sum(jnp.where(second_half, passed, 0.0), axis=1, keepdims=True)
        cut = jnp.where(second_half, late_passed, all_passed - late_passed)
        start = start + cut * step
        step = step * (1.0 / 65.0)
    middle = start + 32.5 * step
    even = jnp.broadcast_to(middle[:, 0:1], shape)
    odd = jnp.broadcast_to(middle[:, 127:128], shape)
    place = jnp.where(lane == 2 * level, even, jnp.where(lane == 2 * level + 1, odd, 0.0))
    done.append(jnp.sum(place, axis=0, keepdims=True)[:, :size])


def finish_kernel(
    scale, products_ref, coupling_ref, x_ref, cur_ref, prev_ref, below_ref, above_ref,
    next_ref, upper_ref, ritz_ref,
):
    slabs, rows, width = x_ref.shape
    near = products_ref.shape[1]
    two = 2 * rows
    products = products_ref[...] * scale
    near_near = products[:near]
    known_near = products[near : near + two]
    x_near = products[near + two : near + two + rows]
    tail = products[near + two + rows :]
    x_x = tail[:, :rows]
    x_known = tail[:, rows : 3 * rows]
    among = jnp.concatenate([tail[:, near - 2 * two : near - two], tail[:, near - two :]], axis=0)
    projection_t = tail[:, rows:two]
    ritz = []
    eigen = eigenvalue_steps(0.5 * (projection_t + jnp.transpose(projection_t)), ritz)
    next(eigen)
    fixed = jnp.concatenate([-projection_t, -coupling_ref[...]], axis=1)
    coefficients_t = x_near + exact(fixed, known_near)
    next(eigen)
    with_known = x_known + exact(fixed, among) - exact_t(coefficients_t, known_near)
    with_near = coefficients_t - exact(coefficients_t, near_near)
    next(eigen)
    gram = x_x + exact_t(fixed, x_known) - exact_t(coefficients_t, x_near)
    gram = gram + exact_t(with_known, fixed) - exact_t(with_near, coefficients_t)
    next(eigen)
    factors = []
    for _ in factor_steps(gram, factors):
        next(eigen)
    upper, inverse_t = factors
    upper_ref[...] = upper
    next(eigen)
    down = lax.broadcasted_iota(jnp.int32, (rows, rows), 0)
    across = lax.broadcasted_iota(jnp.int32, (rows, rows), 1)
    unit = jnp.where(down == across, 1.0, 0.0)
    weights = exact(inverse_t, jnp.concatenate([unit, fixed, -coefficients_t], axis=1))
    weight_high, weight_low = halves(weights)
    both = jnp.concatenate([weight_high, weight_low], axis=0)
    for k in range(slabs):
        x_high, x_low = halves(x_ref[k])
        cur_high, cur_low = halves(cur_ref[k])
        prev_high, prev_low = halves(prev_ref[k])
        stack = jnp.concatenate(
            [x_high, cur_high, prev_high, below_ref[k], above_ref[k]], axis=0
        )
        rest = jnp.concatenate([x_low, cur_low, prev_low], axis=0)
        main = mm(both, stack)
        next_ref[k] = main[:rows] + main[rows:] + mm(weight_high[:, : 3 * rows], rest)
        next(eigen, None)
    for _ in eigen:
        pass
    ritz_ref[...] = ritz[0]


def finish(scale, products, coupling, x, current, previous, below, above):
    slabs, rows, width = x.shape
    return pl.pallas_call(
        functools.partial(finish_kernel, scale),
        out_shape=(
            jax.ShapeDtypeStruct((slabs, rows, width), F32),
            jax.ShapeDtypeStruct((rows, rows), F32),
            jax.ShapeDtypeStruct((1, rows), F32),
        ),
        compiler_params=pltpu.CompilerParams(vmem_limit_bytes=SMALL_LIMIT),
        name="finish",
    )(products, coupling, x, current, previous, below, above)


def per_device(
    current_block,
    previous_block,
    previous_coupling,
    locked_vectors,
    pivot_inverse,
    hopping,
    partner,
    shift_index,
):
    devices = lax.axis_size("slab")
    slices = lax.axis_size("cuts")
    current = current_block[0]
    previous = previous_block[0]
    slabs, rows, width = current.shape
    scale = 1.0 / (slabs * devices * width)
    swap = [(i, i ^ 1) for i in range(devices)]

    fg, own, op = forward_range(
        shift_index, hopping, partner, current, pivot_inverse
    )
    fg_other = lax.ppermute(fg, "slab", swap)
    sh, q = backward_range(shift_index, hopping, partner, own, op, pivot_inverse)
    sh_other = lax.ppermute(sh, "slab", swap)

    locked = jnp.swapaxes(locked_vectors[0], 0, 1)
    even_pairs = [(i, i ^ 1) for i in range(slices)]
    odd_pairs = [(i, i + 1) for i in range(1, slices - 1, 2)]
    odd_pairs = odd_pairs + [(j, i) for i, j in odd_pairs]
    below = lax.ppermute(locked, "cuts", even_pairs)
    above = lax.ppermute(locked, "cuts", odd_pairs)

    def up(value, r):
        return lax.ppermute(value, "slab", [(r, r + 2), (r + 1, r + 3)])

    def back(value, r):
        return lax.ppermute(value, "slab", [(r, r - 2), (r + 1, r - 1)])

    (sent,) = small_call(start_kernel, (BF16,), "start", fg, fg_other)
    into = jnp.zeros((rows, width), BF16)
    new = up(sent, 0)
    for r in range(2, devices - 2, 2):
        into, sent = small_call(pass_kernel, (BF16, BF16), "pass_on", fg, fg_other, into, new)
        new = up(sent, r)
    inflow, first_back, second_back, sent = small_call(
        turn_kernel, (BF16, F32, F32, BF16), "turn", fg, fg_other, sh, sh_other, into, new
    )
    low = lower_sweep(shift_index, inflow, current, hopping, partner, pivot_inverse)
    known = known_products(current, previous, below, above)
    to = jnp.zeros((rows, width), BF16)
    new = back(sent, devices - 2)
    for r in range(devices - 4, 0, -2):
        to, sent = small_call(
            back_kernel, (BF16, BF16), "pass_back", fg, fg_other, first_back, second_back, to, new
        )
        new = back(sent, r)
    x, products = upper_sweep(
        fg, fg_other, second_back, to, new, low, hopping, current, previous, below, above, known, q
    )
    step = 1
    while step < devices:
        products = products + lax.ppermute(products, "slab", [(i, i ^ step) for i in range(devices)])
        step *= 2
    next_block, upper, ritz = finish(
        scale, products, previous_coupling[0], x, current, previous, below, above
    )
    return next_block[None], upper[None], ritz


def solution(mesh):
    return jax.shard_map(
        per_device,
        mesh=mesh,
        in_specs=(
            P("cuts", "slab", None, None),
            P("cuts", "slab", None, None),
            P("cuts", None, None),
            P("cuts", None, "slab", None),
            P(None, "slab", None, None),
            P("slab", None),
            P("slab", None),
            P("cuts"),
        ),
        out_specs=(P("cuts", "slab", None, None), P("cuts", None, None), P("cuts", None)),
        check_vma=False,
    )
```

```python
import functools

import jax
import jax.numpy as jnp
from jax import lax
from jax.experimental import pallas as pl
from jax.experimental.pallas import tpu as pltpu
from jax.sharding import PartitionSpec as P

F32 = jnp.float32
BF16 = jnp.bfloat16
VMEM_LIMIT = 56 * 1024 * 1024
SMALL_LIMIT = 16 * 1024 * 1024
LOWER_LIMIT = 50 * 1024 * 1024
SECTIONS = 4
AHEAD = 3


def mm(left, right):
    return jnp.dot(left, right, preferred_element_type=F32)


def mm_t(left, right):
    return lax.dot_general(left, right, (((1,), (1,)), ((), ())), preferred_element_type=F32)


def exact(left, right):
    return jnp.dot(left, right, precision=lax.Precision.HIGHEST, preferred_element_type=F32)


def exact_t(left, right):
    return lax.dot_general(
        left, right, (((1,), (1,)), ((), ())),
        precision=lax.Precision.HIGHEST, preferred_element_type=F32,
    )


def halves(value):
    high = value.astype(BF16)
    return high, (value - high.astype(F32)).astype(BF16)


def forward_kernel(
    shift_ref, hop_ref, part_ref, cur_ref, piv_ref,
    fg_ref, own_ref, op_ref,
    pbuf, opbuf, hops, parts, sources, in_sem, op_sem, small_sem,
):
    slabs, width = hop_ref.shape
    shift = shift_ref[0]

    def fetch(k):
        return pltpu.make_async_copy(piv_ref.at[shift, k], pbuf.at[k], in_sem.at[k])

    def give_op(k):
        return pltpu.make_async_copy(opbuf.at[k], op_ref.at[k], op_sem.at[k])

    small = [
        pltpu.make_async_copy(part_ref, parts, small_sem.at[0]),
        pltpu.make_async_copy(hop_ref, hops, small_sem.at[1]),
        pltpu.make_async_copy(cur_ref, sources, small_sem.at[2]),
    ]
    for copy in small:
        copy.start()
    for k in range(AHEAD):
        fetch(k).start()
    down = lax.broadcasted_iota(jnp.int32, (width, width), 0).astype(jnp.int16)
    for copy in small:
        copy.wait()
    places = parts[...].astype(jnp.int16)
    weights = (-hops[...]).astype(BF16)
    vectors = None
    for k in range(slabs):
        gather = jnp.where(
            down == places[k : k + 1, :], weights[k : k + 1, :], jnp.zeros((), BF16)
        )
        fetch(k).wait()
        if k + AHEAD < slabs:
            fetch(k + AHEAD).start()
        mixed = mm(jnp.concatenate([gather, sources[k].astype(BF16)], axis=0), pbuf[k])
        step = mixed[:width].astype(BF16)
        source = mixed[width:]
        if k == 0:
            opbuf[k] = step
            vectors = source
        else:
            moved = mm(jnp.concatenate([opbuf[k - 1], vectors.astype(BF16)], axis=0), step)
            opbuf[k] = moved[:width].astype(BF16)
            vectors = source + moved[width:]
        give_op(k).start()
        own_ref[k] = vectors
    fg_ref[:width, :] = opbuf[slabs - 1]
    fg_ref[width:, :] = vectors.astype(BF16)
    for k in range(slabs):
        give_op(k).wait()


def forward_range(shift_index, hopping, partner, current, pivot_inverse):
    slabs, rows, width = current.shape
    vm = pl.BlockSpec(memory_space=pltpu.VMEM)
    hbm = pl.BlockSpec(memory_space=pl.ANY)
    return pl.pallas_call(
        forward_kernel,
        out_shape=(
            jax.ShapeDtypeStruct((width + rows, width), BF16),
            jax.ShapeDtypeStruct((slabs, rows, width), F32),
            jax.ShapeDtypeStruct((slabs, width, width), BF16),
        ),
        in_specs=[pl.BlockSpec(memory_space=pltpu.SMEM), hbm, hbm, hbm, hbm],
        out_specs=(vm, vm, hbm),
        scratch_shapes=[
            pltpu.VMEM((slabs, width, width), BF16),
            pltpu.VMEM((slabs, width, width), BF16),
            pltpu.VMEM((slabs, width), F32),
            pltpu.VMEM((slabs, width), jnp.int32),
            pltpu.VMEM((slabs, rows, width), F32),
            pltpu.SemaphoreType.DMA((slabs,)),
            pltpu.SemaphoreType.DMA((slabs,)),
            pltpu.SemaphoreType.DMA((3,)),
        ],
        compiler_params=pltpu.CompilerParams(vmem_limit_bytes=VMEM_LIMIT),
        cost_estimate=pl.CostEstimate(
            flops=4 * slabs * width**3, bytes_accessed=6 * slabs * width**2, transcendentals=0
        ),
        name="forward_range",
    )(shift_index, hopping, partner, current, pivot_inverse)


def backward_kernel(
    shift_ref, hop_ref, part_ref, own_ref, op_ref, piv_ref,
    sh_ref, q_ref,
    pbuf, opbuf, qbuf, in_sem, op_sem, q_sem,
):
    slabs, width = hop_ref.shape
    shift = shift_ref[0]

    def fetch(k):
        return pltpu.make_async_copy(piv_ref.at[shift, k], pbuf.at[k], in_sem.at[k])

    def fetch_op(k):
        return pltpu.make_async_copy(op_ref.at[k], opbuf.at[k], op_sem.at[k])

    def give_q(k, source):
        return pltpu.make_async_copy(source.at[k], q_ref.at[k], q_sem.at[k])

    last = slabs - 1
    for k in range(last, -1, -1):
        fetch(k).start()
        fetch_op(k).start()
    across = lax.broadcasted_iota(jnp.int32, (width, width), 1)
    part_columns = jnp.transpose(part_ref[...].astype(F32)).astype(jnp.int32)

    def scatter(k):
        return jnp.where(across == part_columns[:, k : k + 1], 1.0, 0.0).astype(BF16)

    def scaled(k):
        hop = hop_ref[k : k + 1, :]
        return jnp.concatenate(
            [(response * hop).astype(BF16), (vectors * hop).astype(BF16)], axis=0
        )

    fetch(last).wait()
    give_q(last, pbuf).start()
    fetch_op(last).wait()
    response = opbuf[last].astype(F32)
    vectors = own_ref[last]
    for k in range(slabs - 2, -1, -1):
        fetch(k).wait()
        permuted = mm(scatter(k + 1), pbuf[k]).astype(BF16)
        qbuf[k] = permuted
        give_q(k, qbuf).start()
        moved = mm(scaled(k + 1), permuted)
        fetch_op(k).wait()
        response = opbuf[k].astype(F32) - moved[:width]
        vectors = own_ref[k] - moved[width:]
    sh_ref[...] = mm(scaled(0), scatter(0)).astype(BF16)
    give_q(last, pbuf).wait()
    for k in range(last):
        give_q(k, qbuf).wait()


def backward_range(shift_index, hopping, partner, own, op, pivot_inverse):
    slabs, rows, width = own.shape
    vm = pl.BlockSpec(memory_space=pltpu.VMEM)
    hbm = pl.BlockSpec(memory_space=pl.ANY)
    stack = jax.ShapeDtypeStruct((slabs, width, width), BF16)
    return pl.pallas_call(
        backward_kernel,
        out_shape=(jax.ShapeDtypeStruct((width + rows, width), BF16), stack),
        in_specs=[pl.BlockSpec(memory_space=pltpu.SMEM), vm, vm, vm, hbm, hbm],
        out_specs=(vm, hbm),
        scratch_shapes=[pltpu.VMEM((slabs, width, width), BF16)] * 3
        + [pltpu.SemaphoreType.DMA((slabs,))] * 3,
        compiler_params=pltpu.CompilerParams(vmem_limit_bytes=VMEM_LIMIT),
        cost_estimate=pl.CostEstimate(
            flops=4 * slabs * width**3, bytes_accessed=6 * slabs * width**2, transcendentals=0
        ),
        name="backward_range",
    )(shift_index, hopping, partner, own, op, pivot_inverse)


def by_order(own_ref, other_ref, run):
    odd = lax.axis_index("slab") % 2

    @pl.when(odd == 0)
    def _():
        run(own_ref, other_ref, 0)

    @pl.when(odd == 1)
    def _():
        run(other_ref, own_ref, 1)


def through(op_ref, value):
    width = op_ref.shape[1]
    return op_ref[width:, :].astype(F32) + mm(value, op_ref[:width, :])


def returned(op_ref, value):
    width = op_ref.shape[1]
    return mm_t(value, op_ref[:width, :])


def start_kernel(own_ref, other_ref, sent_ref):
    def run(first_ref, second_ref, odd):
        width = first_ref.shape[1]
        sent_ref[...] = through(second_ref, first_ref[width:, :]).astype(BF16)

    by_order(own_ref, other_ref, run)


def pass_kernel(own_ref, other_ref, into_ref, new_ref, into_out_ref, sent_ref):
    into = into_ref[...] + new_ref[...]
    into_out_ref[...] = into

    def run(first_ref, second_ref, odd):
        middle = through(first_ref, into).astype(BF16)
        sent_ref[...] = through(second_ref, middle).astype(BF16)

    by_order(own_ref, other_ref, run)


def turn_kernel(
    own_ref, other_ref, own_back_ref, other_back_ref, into_ref, new_ref,
    inflow_ref, first_back_ref, second_back_ref, sent_ref,
):
    into = into_ref[...] + new_ref[...]

    def run(first_ref, second_ref, odd):
        first_sh, second_sh = (
            (other_back_ref, own_back_ref) if odd else (own_back_ref, other_back_ref)
        )
        middle = through(first_ref, into).astype(BF16)
        second_back = through(second_sh, middle)
        first_back = through(first_sh, into)
        sent = first_back + returned(first_ref, second_back.astype(BF16))
        sent_ref[...] = sent.astype(BF16)
        first_back_ref[...] = first_back
        second_back_ref[...] = second_back
        inflow_ref[...] = middle if odd else into

    by_order(own_ref, other_ref, run)


def back_kernel(
    own_ref, other_ref, first_back_ref, second_back_ref, to_ref, new_ref, to_out_ref, sent_ref
):
    to = to_ref[...] + new_ref[...]
    to_out_ref[...] = to

    def run(first_ref, second_ref, odd):
        middle = (second_back_ref[...] + returned(second_ref, to)).astype(BF16)
        sent_ref[...] = (first_back_ref[...] + returned(first_ref, middle)).astype(BF16)

    by_order(own_ref, other_ref, run)


def small_call(kernel, outs, name, *args):
    width = args[0].shape[1]
    rows = args[0].shape[0] - width
    vm = pl.BlockSpec(memory_space=pltpu.VMEM)
    return pl.pallas_call(
        kernel,
        out_shape=tuple(jax.ShapeDtypeStruct((rows, width), t) for t in outs),
        in_specs=[vm] * len(args),
        out_specs=(vm,) * len(outs),
        compiler_params=pltpu.CompilerParams(vmem_limit_bytes=SMALL_LIMIT),
        cost_estimate=pl.CostEstimate(
            flops=4 * rows * width**2, bytes_accessed=4 * width**2, transcendentals=0
        ),
        name=name,
    )(*args)


def lower_kernel(shift_ref, inflow_ref, cur_ref, hop_ref, part_ref, piv_ref, low_ref, pbuf, sem):
    slabs, rows, width = cur_ref.shape
    shift = shift_ref[0]

    def fetch(k):
        return pltpu.make_async_copy(piv_ref.at[shift, k], pbuf.at[k], sem.at[k])

    for k in range(slabs):
        fetch(k).start()
    down = lax.broadcasted_iota(jnp.int32, (width, width), 0).astype(jnp.int16)
    places = part_ref[...].astype(jnp.int16)
    value = inflow_ref[...].astype(F32)
    for k in range(slabs):
        bonds = jnp.where(down == places[k : k + 1, :], jnp.ones((), BF16), jnp.zeros((), BF16))
        high, low = halves(value)
        pulled = mm(jnp.concatenate([high, low], axis=0), bonds)
        reduced = cur_ref[k] - hop_ref[k : k + 1, :] * (pulled[:rows] + pulled[rows:])
        fetch(k).wait()
        value = mm(reduced.astype(BF16), pbuf[k])
        low_ref[k] = value


def lower_sweep(shift_index, inflow, current, hopping, partner, pivot_inverse):
    slabs, rows, width = current.shape
    vm = pl.BlockSpec(memory_space=pltpu.VMEM)
    return pl.pallas_call(
        lower_kernel,
        out_shape=jax.ShapeDtypeStruct((slabs, rows, width), F32),
        in_specs=[pl.BlockSpec(memory_space=pltpu.SMEM), vm, vm, vm, vm]
        + [pl.BlockSpec(memory_space=pl.ANY)],
        out_specs=vm,
        scratch_shapes=[
            pltpu.VMEM((slabs, width, width), BF16),
            pltpu.SemaphoreType.DMA((slabs,)),
        ],
        compiler_params=pltpu.CompilerParams(vmem_limit_bytes=LOWER_LIMIT),
        cost_estimate=pl.CostEstimate(
            flops=2 * slabs * rows * width**2, bytes_accessed=2 * slabs * width**2, transcendentals=0
        ),
        name="lower_sweep",
    )(shift_index, inflow, current, hopping, partner, pivot_inverse)


def known_kernel(cur_ref, prev_ref, below_ref, above_ref, out_ref):
    slabs, rows, width = cur_ref.shape
    near = 2 * below_ref.shape[1]
    two = 2 * rows
    total = None
    for k in range(slabs):
        cur_high, cur_low = halves(cur_ref[k])
        prev_high, prev_low = halves(prev_ref[k])
        stack = jnp.concatenate(
            [below_ref[k], above_ref[k], cur_high, prev_high, cur_low, prev_low], axis=0
        )
        part = mm_t(stack, stack)
        total = part if total is None else total + part
    first = total[near : near + two]
    second = total[near + two :]
    among = first[:, near : near + two] + first[:, near + two :]
    among = among + second[:, near : near + two] + second[:, near + two :]
    out_ref[:near, :] = total[:near, :near]
    out_ref[near : near + two, :] = first[:, :near] + second[:, :near]
    out_ref[near + two : near + two + rows, :] = jnp.zeros((rows, near), F32)
    out_ref[near + two + rows :, :] = jnp.concatenate(
        [jnp.zeros((rows, near - 2 * two), F32), among[:rows], among[rows:]], axis=1
    )


def known_products(current, previous, below, above):
    slabs, rows, width = current.shape
    near = 2 * below.shape[1]
    return pl.pallas_call(
        known_kernel,
        out_shape=jax.ShapeDtypeStruct((near + 4 * rows, near), F32),
        compiler_params=pltpu.CompilerParams(vmem_limit_bytes=SMALL_LIMIT),
        cost_estimate=pl.CostEstimate(
            flops=2 * slabs * 192 * 192 * width, bytes_accessed=3 * 2**19, transcendentals=0
        ),
        name="known_products",
    )(current, previous, below, above)


def upper_kernel(
    own_ref, other_ref, second_back_ref, to_ref, new_ref, low_ref, hop_ref, cur_ref, prev_ref, below_ref, above_ref, known_ref, q_ref,
    x_ref, out_ref, carried,
):
    slabs, rows, width = low_ref.shape
    near = 2 * below_ref.shape[1]
    to = to_ref[...] + new_ref[...]

    def run(first_ref, second_ref, odd):
        if odd:
            carried[...] = to
        else:
            carried[...] = (second_back_ref[...] + returned(second_ref, to)).astype(BF16)

    by_order(own_ref, other_ref, run)
    push = carried[...]
    total = None
    for k in range(slabs - 1, -1, -1):
        value = low_ref[k] - mm(push, q_ref[k])
        x_ref[k] = value
        push = (value * hop_ref[k : k + 1, :]).astype(BF16)
        high, low = halves(value)
        pair = jnp.concatenate([high, low], axis=0)
        cur_high, cur_low = halves(cur_ref[k])
        prev_high, prev_low = halves(prev_ref[k])
        stack = jnp.concatenate(
            [below_ref[k], above_ref[k], high, cur_high, prev_high, low, cur_low, prev_low], axis=0
        )
        part = mm_t(pair, stack)
        total = part if total is None else total + part
    joined = total[:rows] + total[rows:]
    three = 3 * rows
    own = joined[:, near : near + three] + joined[:, near + three :]
    top = near + 2 * rows
    out_ref[:top, :] = known_ref[:top, :]
    out_ref[top : top + rows, :] = joined[:, :near]
    out_ref[top + rows :, :] = known_ref[top + rows :, :] + jnp.concatenate(
        [own, jnp.zeros((rows, near - three), F32)], axis=1
    )


def upper_sweep(
    own, other, second_back, to, new, low, hopping, current, previous, below, above, known, q
):
    slabs, rows, width = low.shape
    vm = pl.BlockSpec(memory_space=pltpu.VMEM)
    return pl.pallas_call(
        upper_kernel,
        out_shape=(
            jax.ShapeDtypeStruct((slabs, rows, width), F32),
            jax.ShapeDtypeStruct(known.shape, F32),
        ),
        in_specs=[vm] * 13,
        out_specs=(vm, vm),
        scratch_shapes=[pltpu.VMEM((rows, width), BF16)],
        compiler_params=pltpu.CompilerParams(vmem_limit_bytes=SMALL_LIMIT),
        cost_estimate=pl.CostEstimate(
            flops=2 * slabs * rows * width**2, bytes_accessed=2 * slabs * width**2, transcendentals=0
        ),
        name="upper_sweep",
    )(own, other, second_back, to, new, low, hopping, current, previous, below, above, known, q)


def factor_steps(gram, done):
    size = gram.shape[0]
    down = lax.broadcasted_iota(jnp.int32, (size, size), 0)
    across = lax.broadcasted_iota(jnp.int32, (size, size), 1)
    left = gram
    right = jnp.where(down == across, 1.0, 0.0)
    column = lax.broadcasted_iota(jnp.int32, (size, 1), 0)
    pivots = jnp.zeros((size, 1), F32)
    for j in range(size):
        pivot = left[j : j + 1, j : j + 1]
        pivots = jnp.where(column == j, pivot, pivots)
        if j < size - 1:
            scale = jnp.where(column > j, left[:, j : j + 1] / pivot, 0.0)
            left_row = left[j : j + 1, :]
            right_row = right[j : j + 1, :]
            left = left - scale * left_row
            right = right - scale * right_row
            yield
    inverse_root = 1.0 / jnp.sqrt(pivots)
    done.append(jnp.where(across >= down, left * inverse_root, 0.0))
    done.append(right * inverse_root)


def eigenvalue_steps(matrix, done):
    size = matrix.shape[0]
    full = (size, 128)
    down = lax.broadcasted_iota(jnp.int32, full, 0)
    across = lax.broadcasted_iota(jnp.int32, full, 1)
    bound = jnp.max(jnp.sum(jnp.abs(matrix), axis=1, keepdims=True), axis=0, keepdims=True)
    bound = bound * (1.0 + 2.0**-18)
    matrix = jnp.concatenate([matrix, jnp.zeros((size, 128 - size), F32)], axis=1)
    diagonal = []
    squares = []

    def upright(value):
        return jnp.broadcast_to(
            jnp.sum(jnp.where(down == across, value, 0.0), axis=1, keepdims=True), full
        )

    def line(value, i):
        return jnp.broadcast_to(value[i : i + 1, :], full)

    def total(value):
        return jnp.broadcast_to(jnp.sum(value, axis=0, keepdims=True), full)

    row = line(matrix, 0)
    col = upright(row)
    for j in range(size - 2):
        diagonal.append(col[j : j + 1, :])
        next_row = line(matrix, j + 1)
        next_col = upright(next_row)
        below = jnp.where(down > j, col, 0.0)
        beside = jnp.where(across > j, row, 0.0)
        image_row = total(matrix * below)
        image_col = upright(image_row)
        square = total(below * below)
        squares.append(square[0:1, :])
        length = jnp.sqrt(square)
        lead = line(col, j + 1)
        signed = jnp.where(lead >= 0.0, length, -length)
        half = square + length * jnp.abs(lead)
        scale = jnp.where(half > 0.0, 1.0 / jnp.where(half > 0.0, half, 1.0), 0.0)
        v_row = beside + jnp.where(across == j + 1, signed, 0.0)
        v_col = below + jnp.where(down == j + 1, signed, 0.0)
        q_row = image_row + signed * next_row
        q_col = image_col + signed * next_col
        along = 0.5 * scale * (scale * total(q_col * v_col))
        w_row = scale * q_row - along * v_row
        w_col = scale * q_col - along * v_col
        matrix = matrix - (v_col * w_row + w_col * v_row)
        lead_v = line(v_col, j + 1)
        lead_w = line(w_col, j + 1)
        row = next_row - (v_row * lead_w + w_row * lead_v)
        col = next_col - (v_col * lead_w + w_col * lead_v)
        yield
    a = size - 2
    diagonal.append(col[a : a + 1, :])
    squares.append(col[a + 1 : a + 2, :] * col[a + 1 : a + 2, :])
    diagonal.append(upright(line(matrix, a + 1))[a + 1 : a + 2, :])
    shape = (8, 128)
    wide_diagonal = [jnp.broadcast_to(value, shape) for value in diagonal]
    wide_squares = [jnp.broadcast_to(value, shape) for value in squares]
    lane = lax.broadcasted_iota(jnp.int32, shape, 1)
    level = lax.broadcasted_iota(jnp.int32, shape, 0)
    second_half = lane >= 64
    rank = 2 * level + jnp.where(second_half, 1, 0)
    point = (lane - jnp.where(second_half, 64, 0) + 1).astype(F32)
    start = jnp.broadcast_to(-bound, shape)
    step = jnp.broadcast_to(bound * (2.0 / 65.0), shape)
    tiny = 1e-30
    for _ in range(SECTIONS):
        shifted = start + point * step
        pivot = wide_diagonal[0] - shifted
        pivot = jnp.where(jnp.abs(pivot) < tiny, -tiny, pivot)
        count = jnp.where(pivot < 0.0, 1, 0)
        for i in range(1, size):
            pivot = wide_diagonal[i] - shifted - wide_squares[i - 1] / pivot
            pivot = jnp.where(jnp.abs(pivot) < tiny, -tiny, pivot)
            count = count + jnp.where(pivot < 0.0, 1, 0)
            if i % 4 == 0:
                yield
        passed = jnp.where(count <= rank, 1.0, 0.0)
        all_passed = jnp.sum(passed, axis=1, keepdims=True)
        late_passed = jnp.sum(jnp.where(second_half, passed, 0.0), axis=1, keepdims=True)
        cut = jnp.where(second_half, late_passed, all_passed - late_passed)
        start = start + cut * step
        step = step * (1.0 / 65.0)
    middle = start + 32.5 * step
    even = jnp.broadcast_to(middle[:, 0:1], shape)
    odd = jnp.broadcast_to(middle[:, 127:128], shape)
    place = jnp.where(lane == 2 * level, even, jnp.where(lane == 2 * level + 1, odd, 0.0))
    done.append(jnp.sum(place, axis=0, keepdims=True)[:, :size])


def finish_kernel(
    scale, products_ref, coupling_ref, x_ref, cur_ref, prev_ref, below_ref, above_ref,
    next_ref, upper_ref, ritz_ref,
):
    slabs, rows, width = x_ref.shape
    near = products_ref.shape[1]
    two = 2 * rows
    products = products_ref[...] * scale
    near_near = products[:near]
    known_near = products[near : near + two]
    x_near = products[near + two : near + two + rows]
    tail = products[near + two + rows :]
    x_x = tail[:, :rows]
    x_known = tail[:, rows : 3 * rows]
    among = jnp.concatenate([tail[:, near - 2 * two : near - two], tail[:, near - two :]], axis=0)
    projection_t = tail[:, rows:two]
    ritz = []
    eigen = eigenvalue_steps(0.5 * (projection_t + jnp.transpose(projection_t)), ritz)
    next(eigen)
    fixed = jnp.concatenate([-projection_t, -coupling_ref[...]], axis=1)
    coefficients_t = x_near + exact(fixed, known_near)
    next(eigen)
    with_known = x_known + exact(fixed, among) - exact_t(coefficients_t, known_near)
    with_near = coefficients_t - exact(coefficients_t, near_near)
    next(eigen)
    gram = x_x + exact_t(fixed, x_known) - exact_t(coefficients_t, x_near)
    gram = gram + exact_t(with_known, fixed) - exact_t(with_near, coefficients_t)
    next(eigen)
    factors = []
    for _ in factor_steps(gram, factors):
        next(eigen)
    upper, inverse_t = factors
    upper_ref[...] = upper
    next(eigen)
    down = lax.broadcasted_iota(jnp.int32, (rows, rows), 0)
    across = lax.broadcasted_iota(jnp.int32, (rows, rows), 1)
    unit = jnp.where(down == across, 1.0, 0.0)
    weights = exact(inverse_t, jnp.concatenate([unit, fixed, -coefficients_t], axis=1))
    weight_high, weight_low = halves(weights)
    both = jnp.concatenate([weight_high, weight_low], axis=0)
    for k in range(slabs):
        x_high, x_low = halves(x_ref[k])
        cur_high, cur_low = halves(cur_ref[k])
        prev_high, prev_low = halves(prev_ref[k])
        stack = jnp.concatenate(
            [x_high, cur_high, prev_high, below_ref[k], above_ref[k]], axis=0
        )
        rest = jnp.concatenate([x_low, cur_low, prev_low], axis=0)
        main = mm(both, stack)
        next_ref[k] = main[:rows] + main[rows:] + mm(weight_high[:, : 3 * rows], rest)
        next(eigen, None)
    for _ in eigen:
        pass
    ritz_ref[...] = ritz[0]


def finish(scale, products, coupling, x, current, previous, below, above):
    slabs, rows, width = x.shape
    return pl.pallas_call(
        functools.partial(finish_kernel, scale),
        out_shape=(
            jax.ShapeDtypeStruct((slabs, rows, width), F32),
            jax.ShapeDtypeStruct((rows, rows), F32),
            jax.ShapeDtypeStruct((1, rows), F32),
        ),
        compiler_params=pltpu.CompilerParams(vmem_limit_bytes=SMALL_LIMIT),
        name="finish",
    )(products, coupling, x, current, previous, below, above)


def per_device(
    current_block,
    previous_block,
    previous_coupling,
    locked_vectors,
    pivot_inverse,
    hopping,
    partner,
    shift_index,
):
    devices = lax.axis_size("slab")
    slices = lax.axis_size("cuts")
    current = current_block[0]
    previous = previous_block[0]
    slabs, rows, width = current.shape
    scale = 1.0 / (slabs * devices * width)
    swap = [(i, i ^ 1) for i in range(devices)]

    fg, own, op = forward_range(
        shift_index, hopping, partner, current, pivot_inverse
    )
    fg_other = lax.ppermute(fg, "slab", swap)
    sh, q = backward_range(shift_index, hopping, partner, own, op, pivot_inverse)
    sh_other = lax.ppermute(sh, "slab", swap)

    locked = jnp.swapaxes(locked_vectors[0], 0, 1)
    even_pairs = [(i, i ^ 1) for i in range(slices)]
    odd_pairs = [(i, i + 1) for i in range(1, slices - 1, 2)]
    odd_pairs = odd_pairs + [(j, i) for i, j in odd_pairs]
    below = lax.ppermute(locked, "cuts", even_pairs)
    above = lax.ppermute(locked, "cuts", odd_pairs)

    def up(value, r):
        return lax.ppermute(value, "slab", [(r, r + 2), (r + 1, r + 3)])

    def back(value, r):
        return lax.ppermute(value, "slab", [(r, r - 2), (r + 1, r - 1)])

    (sent,) = small_call(start_kernel, (BF16,), "start", fg, fg_other)
    into = jnp.zeros((rows, width), BF16)
    new = up(sent, 0)
    for r in range(2, devices - 2, 2):
        into, sent = small_call(pass_kernel, (BF16, BF16), "pass_on", fg, fg_other, into, new)
        new = up(sent, r)
    inflow, first_back, second_back, sent = small_call(
        turn_kernel, (BF16, F32, F32, BF16), "turn", fg, fg_other, sh, sh_other, into, new
    )
    low = lower_sweep(shift_index, inflow, current, hopping, partner, pivot_inverse)
    known = known_products(current, previous, below, above)
    to = jnp.zeros((rows, width), BF16)
    new = back(sent, devices - 2)
    for r in range(devices - 4, 0, -2):
        to, sent = small_call(
            back_kernel, (BF16, BF16), "pass_back", fg, fg_other, first_back, second_back, to, new
        )
        new = back(sent, r)
    x, products = upper_sweep(
        fg, fg_other, second_back, to, new, low, hopping, current, previous, below, above, known, q
    )
    step = 1
    while step < devices:
        products = products + lax.ppermute(products, "slab", [(i, i ^ step) for i in range(devices)])
        step *= 2
    next_block, upper, ritz = finish(
        scale, products, previous_coupling[0], x, current, previous, below, above
    )
    return next_block[None], upper[None], ritz


def solution(mesh):
    return jax.shard_map(
        per_device,
        mesh=mesh,
        in_specs=(
            P("cuts", "slab", None, None),
            P("cuts", "slab", None, None),
            P("cuts", None, None),
            P("cuts", None, "slab", None),
            P(None, "slab", None, None),
            P("slab", None),
            P("slab", None),
            P("cuts"),
        ),
        out_specs=(P("cuts", "slab", None, None), P("cuts", None, None), P("cuts", None)),
        check_vma=False,
    )
```

```python
import functools

import jax
import jax.numpy as jnp
from jax import lax
from jax.experimental import pallas as pl
from jax.experimental.pallas import tpu as pltpu
from jax.sharding import PartitionSpec as P

F32 = jnp.float32
BF16 = jnp.bfloat16
VMEM_LIMIT = 56 * 1024 * 1024
SMALL_LIMIT = 16 * 1024 * 1024
LOWER_LIMIT = 50 * 1024 * 1024
SECTIONS = 4
AHEAD = 3


def mm(left, right):
    return jnp.dot(left, right, preferred_element_type=F32)


def mm_t(left, right):
    return lax.dot_general(left, right, (((1,), (1,)), ((), ())), preferred_element_type=F32)


def exact(left, right):
    return jnp.dot(left, right, precision=lax.Precision.HIGHEST, preferred_element_type=F32)


def exact_t(left, right):
    return lax.dot_general(
        left, right, (((1,), (1,)), ((), ())),
        precision=lax.Precision.HIGHEST, preferred_element_type=F32,
    )


def halves(value):
    high = value.astype(BF16)
    return high, (value - high.astype(F32)).astype(BF16)


def forward_kernel(
    shift_ref, hop_ref, part_ref, cur_ref, piv_ref,
    fg_ref, own_ref, op_ref,
    pbuf, opbuf, hops, parts, sources, in_sem, op_sem, small_sem,
):
    slabs, width = hop_ref.shape
    shift = shift_ref[0]

    def fetch(k):
        return pltpu.make_async_copy(piv_ref.at[shift, k], pbuf.at[k], in_sem.at[k])

    def give_op(k):
        return pltpu.make_async_copy(opbuf.at[k], op_ref.at[k], op_sem.at[k])

    small = [
        pltpu.make_async_copy(part_ref, parts, small_sem.at[0]),
        pltpu.make_async_copy(hop_ref, hops, small_sem.at[1]),
        pltpu.make_async_copy(cur_ref, sources, small_sem.at[2]),
    ]
    for copy in small:
        copy.start()
    for k in range(AHEAD):
        fetch(k).start()
    down = lax.broadcasted_iota(jnp.int32, (width, width), 0).astype(jnp.int16)
    for copy in small:
        copy.wait()
    places = parts[...].astype(jnp.int16)
    weights = (-hops[...]).astype(BF16)
    vectors = None
    for k in range(slabs):
        gather = jnp.where(
            down == places[k : k + 1, :], weights[k : k + 1, :], jnp.zeros((), BF16)
        )
        fetch(k).wait()
        if k + AHEAD < slabs:
            fetch(k + AHEAD).start()
        mixed = mm(jnp.concatenate([gather, sources[k].astype(BF16)], axis=0), pbuf[k])
        step = mixed[:width].astype(BF16)
        source = mixed[width:]
        if k == 0:
            opbuf[k] = step
            vectors = source
        else:
            moved = mm(jnp.concatenate([opbuf[k - 1], vectors.astype(BF16)], axis=0), step)
            opbuf[k] = moved[:width].astype(BF16)
            vectors = source + moved[width:]
        give_op(k).start()
        own_ref[k] = vectors
    fg_ref[:width, :] = opbuf[slabs - 1]
    fg_ref[width:, :] = vectors.astype(BF16)
    for k in range(slabs):
        give_op(k).wait()


def forward_range(shift_index, hopping, partner, current, pivot_inverse):
    slabs, rows, width = current.shape
    vm = pl.BlockSpec(memory_space=pltpu.VMEM)
    hbm = pl.BlockSpec(memory_space=pl.ANY)
    return pl.pallas_call(
        forward_kernel,
        out_shape=(
            jax.ShapeDtypeStruct((width + rows, width), BF16),
            jax.ShapeDtypeStruct((slabs, rows, width), F32),
            jax.ShapeDtypeStruct((slabs, width, width), BF16),
        ),
        in_specs=[pl.BlockSpec(memory_space=pltpu.SMEM), hbm, hbm, hbm, hbm],
        out_specs=(vm, vm, hbm),
        scratch_shapes=[
            pltpu.VMEM((slabs, width, width), BF16),
            pltpu.VMEM((slabs, width, width), BF16),
            pltpu.VMEM((slabs, width), F32),
            pltpu.VMEM((slabs, width), jnp.int32),
            pltpu.VMEM((slabs, rows, width), F32),
            pltpu.SemaphoreType.DMA((slabs,)),
            pltpu.SemaphoreType.DMA((slabs,)),
            pltpu.SemaphoreType.DMA((3,)),
        ],
        compiler_params=pltpu.CompilerParams(vmem_limit_bytes=VMEM_LIMIT),
        cost_estimate=pl.CostEstimate(
            flops=4 * slabs * width**3, bytes_accessed=6 * slabs * width**2, transcendentals=0
        ),
        name="forward_range",
    )(shift_index, hopping, partner, current, pivot_inverse)


def backward_kernel(
    shift_ref, hop_ref, part_ref, own_ref, op_ref, piv_ref,
    sh_ref, q_ref,
    pbuf, opbuf, qbuf, in_sem, op_sem, q_sem,
):
    slabs, width = hop_ref.shape
    shift = shift_ref[0]

    def fetch(k):
        return pltpu.make_async_copy(piv_ref.at[shift, k], pbuf.at[k], in_sem.at[k])

    def fetch_op(k):
        return pltpu.make_async_copy(op_ref.at[k], opbuf.at[k], op_sem.at[k])

    def give_q(k, source):
        return pltpu.make_async_copy(source.at[k], q_ref.at[k], q_sem.at[k])

    last = slabs - 1
    for k in range(last, -1, -1):
        fetch(k).start()
        fetch_op(k).start()
    across = lax.broadcasted_iota(jnp.int32, (width, width), 1)
    part_columns = jnp.transpose(part_ref[...].astype(F32)).astype(jnp.int32)

    def scatter(k):
        return jnp.where(across == part_columns[:, k : k + 1], 1.0, 0.0).astype(BF16)

    def scaled(k):
        hop = hop_ref[k : k + 1, :]
        return jnp.concatenate(
            [(response * hop).astype(BF16), (vectors * hop).astype(BF16)], axis=0
        )

    fetch(last).wait()
    give_q(last, pbuf).start()
    fetch_op(last).wait()
    response = opbuf[last].astype(F32)
    vectors = own_ref[last]
    for k in range(slabs - 2, -1, -1):
        fetch(k).wait()
        permuted = mm(scatter(k + 1), pbuf[k]).astype(BF16)
        qbuf[k] = permuted
        give_q(k, qbuf).start()
        moved = mm(scaled(k + 1), permuted)
        fetch_op(k).wait()
        response = opbuf[k].astype(F32) - moved[:width]
        vectors = own_ref[k] - moved[width:]
    sh_ref[...] = mm(scaled(0), scatter(0)).astype(BF16)
    give_q(last, pbuf).wait()
    for k in range(last):
        give_q(k, qbuf).wait()


def backward_range(shift_index, hopping, partner, own, op, pivot_inverse):
    slabs, rows, width = own.shape
    vm = pl.BlockSpec(memory_space=pltpu.VMEM)
    hbm = pl.BlockSpec(memory_space=pl.ANY)
    stack = jax.ShapeDtypeStruct((slabs, width, width), BF16)
    return pl.pallas_call(
        backward_kernel,
        out_shape=(jax.ShapeDtypeStruct((width + rows, width), BF16), stack),
        in_specs=[pl.BlockSpec(memory_space=pltpu.SMEM), vm, vm, vm, hbm, hbm],
        out_specs=(vm, hbm),
        scratch_shapes=[pltpu.VMEM((slabs, width, width), BF16)] * 3
        + [pltpu.SemaphoreType.DMA((slabs,))] * 3,
        compiler_params=pltpu.CompilerParams(vmem_limit_bytes=VMEM_LIMIT),
        cost_estimate=pl.CostEstimate(
            flops=4 * slabs * width**3, bytes_accessed=6 * slabs * width**2, transcendentals=0
        ),
        name="backward_range",
    )(shift_index, hopping, partner, own, op, pivot_inverse)


def by_order(own_ref, other_ref, run):
    odd = lax.axis_index("slab") % 2

    @pl.when(odd == 0)
    def _():
        run(own_ref, other_ref, 0)

    @pl.when(odd == 1)
    def _():
        run(other_ref, own_ref, 1)


def through(op_ref, value):
    width = op_ref.shape[1]
    return op_ref[width:, :].astype(F32) + mm(value, op_ref[:width, :])


def returned(op_ref, value):
    width = op_ref.shape[1]
    return mm_t(value, op_ref[:width, :])


def start_kernel(own_ref, other_ref, sent_ref):
    def run(first_ref, second_ref, odd):
        width = first_ref.shape[1]
        sent_ref[...] = through(second_ref, first_ref[width:, :]).astype(BF16)

    by_order(own_ref, other_ref, run)


def pass_kernel(own_ref, other_ref, into_ref, new_ref, into_out_ref, sent_ref):
    into = into_ref[...] + new_ref[...]
    into_out_ref[...] = into

    def run(first_ref, second_ref, odd):
        middle = through(first_ref, into).astype(BF16)
        sent_ref[...] = through(second_ref, middle).astype(BF16)

    by_order(own_ref, other_ref, run)


def turn_kernel(
    own_ref, other_ref, own_back_ref, other_back_ref, into_ref, new_ref,
    inflow_ref, first_back_ref, second_back_ref, sent_ref,
):
    into = into_ref[...] + new_ref[...]

    def run(first_ref, second_ref, odd):
        first_sh, second_sh = (
            (other_back_ref, own_back_ref) if odd else (own_back_ref, other_back_ref)
        )
        middle = through(first_ref, into).astype(BF16)
        second_back = through(second_sh, middle)
        first_back = through(first_sh, into)
        sent = first_back + returned(first_ref, second_back.astype(BF16))
        sent_ref[...] = sent.astype(BF16)
        first_back_ref[...] = first_back
        second_back_ref[...] = second_back
        inflow_ref[...] = middle if odd else into

    by_order(own_ref, other_ref, run)


def back_kernel(
    own_ref, other_ref, first_back_ref, second_back_ref, to_ref, new_ref, to_out_ref, sent_ref
):
    to = to_ref[...] + new_ref[...]
    to_out_ref[...] = to

    def run(first_ref, second_ref, odd):
        middle = (second_back_ref[...] + returned(second_ref, to)).astype(BF16)
        sent_ref[...] = (first_back_ref[...] + returned(first_ref, middle)).astype(BF16)

    by_order(own_ref, other_ref, run)


def small_call(kernel, outs, name, *args):
    width = args[0].shape[1]
    rows = args[0].shape[0] - width
    vm = pl.BlockSpec(memory_space=pltpu.VMEM)
    return pl.pallas_call(
        kernel,
        out_shape=tuple(jax.ShapeDtypeStruct((rows, width), t) for t in outs),
        in_specs=[vm] * len(args),
        out_specs=(vm,) * len(outs),
        compiler_params=pltpu.CompilerParams(vmem_limit_bytes=SMALL_LIMIT),
        cost_estimate=pl.CostEstimate(
            flops=4 * rows * width**2, bytes_accessed=4 * width**2, transcendentals=0
        ),
        name=name,
    )(*args)


def lower_kernel(shift_ref, inflow_ref, cur_ref, hop_ref, part_ref, piv_ref, low_ref, pbuf, sem):
    slabs, rows, width = cur_ref.shape
    shift = shift_ref[0]

    def fetch(k):
        return pltpu.make_async_copy(piv_ref.at[shift, k], pbuf.at[k], sem.at[k])

    for k in range(slabs):
        fetch(k).start()
    down = lax.broadcasted_iota(jnp.int32, (width, width), 0).astype(jnp.int16)
    places = part_ref[...].astype(jnp.int16)
    value = inflow_ref[...].astype(F32)
    for k in range(slabs):
        bonds = jnp.where(down == places[k : k + 1, :], jnp.ones((), BF16), jnp.zeros((), BF16))
        high, low = halves(value)
        pulled = mm(jnp.concatenate([high, low], axis=0), bonds)
        reduced = cur_ref[k] - hop_ref[k : k + 1, :] * (pulled[:rows] + pulled[rows:])
        fetch(k).wait()
        value = mm(reduced.astype(BF16), pbuf[k])
        low_ref[k] = value


def lower_sweep(shift_index, inflow, current, hopping, partner, pivot_inverse):
    slabs, rows, width = current.shape
    vm = pl.BlockSpec(memory_space=pltpu.VMEM)
    return pl.pallas_call(
        lower_kernel,
        out_shape=jax.ShapeDtypeStruct((slabs, rows, width), F32),
        in_specs=[pl.BlockSpec(memory_space=pltpu.SMEM), vm, vm, vm, vm]
        + [pl.BlockSpec(memory_space=pl.ANY)],
        out_specs=vm,
        scratch_shapes=[
            pltpu.VMEM((slabs, width, width), BF16),
            pltpu.SemaphoreType.DMA((slabs,)),
        ],
        compiler_params=pltpu.CompilerParams(vmem_limit_bytes=LOWER_LIMIT),
        cost_estimate=pl.CostEstimate(
            flops=2 * slabs * rows * width**2, bytes_accessed=2 * slabs * width**2, transcendentals=0
        ),
        name="lower_sweep",
    )(shift_index, inflow, current, hopping, partner, pivot_inverse)


def known_kernel(cur_ref, prev_ref, below_ref, above_ref, out_ref):
    slabs, rows, width = cur_ref.shape
    near = 2 * below_ref.shape[1]
    two = 2 * rows
    total = None
    for k in range(slabs):
        cur_high, cur_low = halves(cur_ref[k])
        prev_high, prev_low = halves(prev_ref[k])
        stack = jnp.concatenate(
            [below_ref[k], above_ref[k], cur_high, prev_high, cur_low, prev_low], axis=0
        )
        part = mm_t(stack, stack)
        total = part if total is None else total + part
    first = total[near : near + two]
    second = total[near + two :]
    among = first[:, near : near + two] + first[:, near + two :]
    among = among + second[:, near : near + two] + second[:, near + two :]
    out_ref[:near, :] = total[:near, :near]
    out_ref[near : near + two, :] = first[:, :near] + second[:, :near]
    out_ref[near + two : near + two + rows, :] = jnp.zeros((rows, near), F32)
    out_ref[near + two + rows :, :] = jnp.concatenate(
        [jnp.zeros((rows, near - 2 * two), F32), among[:rows], among[rows:]], axis=1
    )


def known_products(current, previous, below, above):
    slabs, rows, width = current.shape
    near = 2 * below.shape[1]
    return pl.pallas_call(
        known_kernel,
        out_shape=jax.ShapeDtypeStruct((near + 4 * rows, near), F32),
        compiler_params=pltpu.CompilerParams(vmem_limit_bytes=SMALL_LIMIT),
        cost_estimate=pl.CostEstimate(
            flops=2 * slabs * 192 * 192 * width, bytes_accessed=3 * 2**19, transcendentals=0
        ),
        name="known_products",
    )(current, previous, below, above)


def upper_kernel(
    own_ref, other_ref, second_back_ref, to_ref, new_ref, low_ref, hop_ref, cur_ref, prev_ref, below_ref, above_ref, known_ref, q_ref,
    x_ref, out_ref, carried,
):
    slabs, rows, width = low_ref.shape
    near = 2 * below_ref.shape[1]
    to = to_ref[...] + new_ref[...]

    def run(first_ref, second_ref, odd):
        if odd:
            carried[...] = to
        else:
            carried[...] = (second_back_ref[...] + returned(second_ref, to)).astype(BF16)

    by_order(own_ref, other_ref, run)
    push = carried[...]
    total = None
    for k in range(slabs - 1, -1, -1):
        value = low_ref[k] - mm(push, q_ref[k])
        x_ref[k] = value
        push = (value * hop_ref[k : k + 1, :]).astype(BF16)
        high, low = halves(value)
        pair = jnp.concatenate([high, low], axis=0)
        cur_high, cur_low = halves(cur_ref[k])
        prev_high, prev_low = halves(prev_ref[k])
        stack = jnp.concatenate(
            [below_ref[k], above_ref[k], high, cur_high, prev_high, low, cur_low, prev_low], axis=0
        )
        part = mm_t(pair, stack)
        total = part if total is None else total + part
    joined = total[:rows] + total[rows:]
    three = 3 * rows
    own = joined[:, near : near + three] + joined[:, near + three :]
    top = near + 2 * rows
    out_ref[:top, :] = known_ref[:top, :]
    out_ref[top : top + rows, :] = joined[:, :near]
    out_ref[top + rows :, :] = known_ref[top + rows :, :] + jnp.concatenate(
        [own, jnp.zeros((rows, near - three), F32)], axis=1
    )


def upper_sweep(
    own, other, second_back, to, new, low, hopping, current, previous, below, above, known, q
):
    slabs, rows, width = low.shape
    vm = pl.BlockSpec(memory_space=pltpu.VMEM)
    return pl.pallas_call(
        upper_kernel,
        out_shape=(
            jax.ShapeDtypeStruct((slabs, rows, width), F32),
            jax.ShapeDtypeStruct(known.shape, F32),
        ),
        in_specs=[vm] * 13,
        out_specs=(vm, vm),
        scratch_shapes=[pltpu.VMEM((rows, width), BF16)],
        compiler_params=pltpu.CompilerParams(vmem_limit_bytes=SMALL_LIMIT),
        cost_estimate=pl.CostEstimate(
            flops=2 * slabs * rows * width**2, bytes_accessed=2 * slabs * width**2, transcendentals=0
        ),
        name="upper_sweep",
    )(own, other, second_back, to, new, low, hopping, current, previous, below, above, known, q)


def factor_steps(gram, done):
    size = gram.shape[0]
    down = lax.broadcasted_iota(jnp.int32, (size, size), 0)
    across = lax.broadcasted_iota(jnp.int32, (size, size), 1)
    left = gram
    right = jnp.where(down == across, 1.0, 0.0)
    column = lax.broadcasted_iota(jnp.int32, (size, 1), 0)
    pivots = jnp.zeros((size, 1), F32)
    for j in range(size):
        pivot = left[j : j + 1, j : j + 1]
        pivots = jnp.where(column == j, pivot, pivots)
        if j < size - 1:
            scale = jnp.where(column > j, left[:, j : j + 1] / pivot, 0.0)
            left_row = left[j : j + 1, :]
            right_row = right[j : j + 1, :]
            left = left - scale * left_row
            right = right - scale * right_row
            yield
    inverse_root = 1.0 / jnp.sqrt(pivots)
    done.append(jnp.where(across >= down, left * inverse_root, 0.0))
    done.append(right * inverse_root)


def eigenvalue_steps(matrix, done):
    size = matrix.shape[0]
    full = (size, 128)
    down = lax.broadcasted_iota(jnp.int32, full, 0)
    across = lax.broadcasted_iota(jnp.int32, full, 1)
    bound = jnp.max(jnp.sum(jnp.abs(matrix), axis=1, keepdims=True), axis=0, keepdims=True)
    bound = bound * (1.0 + 2.0**-18)
    matrix = jnp.concatenate([matrix, jnp.zeros((size, 128 - size), F32)], axis=1)
    diagonal = []
    squares = []

    def upright(value):
        return jnp.broadcast_to(
            jnp.sum(jnp.where(down == across, value, 0.0), axis=1, keepdims=True), full
        )

    def line(value, i):
        return jnp.broadcast_to(value[i : i + 1, :], full)

    def total(value):
        return jnp.broadcast_to(jnp.sum(value, axis=0, keepdims=True), full)

    row = line(matrix, 0)
    col = upright(row)
    for j in range(size - 2):
        diagonal.append(col[j : j + 1, :])
        next_row = line(matrix, j + 1)
        next_col = upright(next_row)
        below = jnp.where(down > j, col, 0.0)
        beside = jnp.where(across > j, row, 0.0)
        image_row = total(matrix * below)
        image_col = upright(image_row)
        square = total(below * below)
        squares.append(square[0:1, :])
        length = jnp.sqrt(square)
        lead = line(col, j + 1)
        signed = jnp.where(lead >= 0.0, length, -length)
        half = square + length * jnp.abs(lead)
        scale = jnp.where(half > 0.0, 1.0 / jnp.where(half > 0.0, half, 1.0), 0.0)
        v_row = beside + jnp.where(across == j + 1, signed, 0.0)
        v_col = below + jnp.where(down == j + 1, signed, 0.0)
        q_row = image_row + signed * next_row
        q_col = image_col + signed * next_col
        along = 0.5 * scale * (scale * total(q_col * v_col))
        w_row = scale * q_row - along * v_row
        w_col = scale * q_col - along * v_col
        matrix = matrix - (v_col * w_row + w_col * v_row)
        lead_v = line(v_col, j + 1)
        lead_w = line(w_col, j + 1)
        row = next_row - (v_row * lead_w + w_row * lead_v)
        col = next_col - (v_col * lead_w + w_col * lead_v)
        yield
    a = size - 2
    diagonal.append(col[a : a + 1, :])
    squares.append(col[a + 1 : a + 2, :] * col[a + 1 : a + 2, :])
    diagonal.append(upright(line(matrix, a + 1))[a + 1 : a + 2, :])
    shape = (8, 128)
    wide_diagonal = [jnp.broadcast_to(value, shape) for value in diagonal]
    wide_squares = [jnp.broadcast_to(value, shape) for value in squares]
    lane = lax.broadcasted_iota(jnp.int32, shape, 1)
    level = lax.broadcasted_iota(jnp.int32, shape, 0)
    second_half = lane >= 64
    rank = 2 * level + jnp.where(second_half, 1, 0)
    point = (lane - jnp.where(second_half, 64, 0) + 1).astype(F32)
    start = jnp.broadcast_to(-bound, shape)
    step = jnp.broadcast_to(bound * (2.0 / 65.0), shape)
    tiny = 1e-30
    for _ in range(SECTIONS):
        shifted = start + point * step
        pivot = wide_diagonal[0] - shifted
        pivot = jnp.where(jnp.abs(pivot) < tiny, -tiny, pivot)
        count = jnp.where(pivot < 0.0, 1, 0)
        for i in range(1, size):
            pivot = wide_diagonal[i] - shifted - wide_squares[i - 1] / pivot
            pivot = jnp.where(jnp.abs(pivot) < tiny, -tiny, pivot)
            count = count + jnp.where(pivot < 0.0, 1, 0)
            if i % 4 == 0:
                yield
        passed = jnp.where(count <= rank, 1.0, 0.0)
        all_passed = jnp.sum(passed, axis=1, keepdims=True)
        late_passed = jnp.sum(jnp.where(second_half, passed, 0.0), axis=1, keepdims=True)
        cut = jnp.where(second_half, late_passed, all_passed - late_passed)
        start = start + cut * step
        step = step * (1.0 / 65.0)
    middle = start + 32.5 * step
    even = jnp.broadcast_to(middle[:, 0:1], shape)
    odd = jnp.broadcast_to(middle[:, 127:128], shape)
    place = jnp.where(lane == 2 * level, even, jnp.where(lane == 2 * level + 1, odd, 0.0))
    done.append(jnp.sum(place, axis=0, keepdims=True)[:, :size])


def finish_kernel(
    scale, products_ref, coupling_ref, x_ref, cur_ref, prev_ref, below_ref, above_ref,
    next_ref, upper_ref, ritz_ref,
):
    slabs, rows, width = x_ref.shape
    near = products_ref.shape[1]
    two = 2 * rows
    products = products_ref[...] * scale
    near_near = products[:near]
    known_near = products[near : near + two]
    x_near = products[near + two : near + two + rows]
    tail = products[near + two + rows :]
    x_x = tail[:, :rows]
    x_known = tail[:, rows : 3 * rows]
    among = jnp.concatenate([tail[:, near - 2 * two : near - two], tail[:, near - two :]], axis=0)
    projection_t = tail[:, rows:two]
    ritz = []
    eigen = eigenvalue_steps(0.5 * (projection_t + jnp.transpose(projection_t)), ritz)
    next(eigen)
    fixed = jnp.concatenate([-projection_t, -coupling_ref[...]], axis=1)
    coefficients_t = x_near + exact(fixed, known_near)
    next(eigen)
    with_known = x_known + exact(fixed, among) - exact_t(coefficients_t, known_near)
    with_near = coefficients_t - exact(coefficients_t, near_near)
    next(eigen)
    gram = x_x + exact_t(fixed, x_known) - exact_t(coefficients_t, x_near)
    gram = gram + exact_t(with_known, fixed) - exact_t(with_near, coefficients_t)
    next(eigen)
    factors = []
    for _ in factor_steps(gram, factors):
        next(eigen)
    upper, inverse_t = factors
    upper_ref[...] = upper
    next(eigen)
    down = lax.broadcasted_iota(jnp.int32, (rows, rows), 0)
    across = lax.broadcasted_iota(jnp.int32, (rows, rows), 1)
    unit = jnp.where(down == across, 1.0, 0.0)
    weights = exact(inverse_t, jnp.concatenate([unit, fixed, -coefficients_t], axis=1))
    weight_high, weight_low = halves(weights)
    both = jnp.concatenate([weight_high, weight_low], axis=0)
    for k in range(slabs):
        x_high, x_low = halves(x_ref[k])
        cur_high, cur_low = halves(cur_ref[k])
        prev_high, prev_low = halves(prev_ref[k])
        stack = jnp.concatenate(
            [x_high, cur_high, prev_high, below_ref[k], above_ref[k]], axis=0
        )
        rest = jnp.concatenate([x_low, cur_low, prev_low], axis=0)
        main = mm(both, stack)
        next_ref[k] = main[:rows] + main[rows:] + mm(weight_high[:, : 3 * rows], rest)
        next(eigen, None)
    for _ in eigen:
        pass
    ritz_ref[...] = ritz[0]


def finish(scale, products, coupling, x, current, previous, below, above):
    slabs, rows, width = x.shape
    return pl.pallas_call(
        functools.partial(finish_kernel, scale),
        out_shape=(
            jax.ShapeDtypeStruct((slabs, rows, width), F32),
            jax.ShapeDtypeStruct((rows, rows), F32),
            jax.ShapeDtypeStruct((1, rows), F32),
        ),
        compiler_params=pltpu.CompilerParams(vmem_limit_bytes=SMALL_LIMIT),
        name="finish",
    )(products, coupling, x, current, previous, below, above)


def per_device(
    current_block,
    previous_block,
    previous_coupling,
    locked_vectors,
    pivot_inverse,
    hopping,
    partner,
    shift_index,
):
    devices = lax.axis_size("slab")
    slices = lax.axis_size("cuts")
    current = current_block[0]
    previous = previous_block[0]
    slabs, rows, width = current.shape
    scale = 1.0 / (slabs * devices * width)
    swap = [(i, i ^ 1) for i in range(devices)]

    fg, own, op = forward_range(
        shift_index, hopping, partner, current, pivot_inverse
    )
    fg_other = lax.ppermute(fg, "slab", swap)
    sh, q = backward_range(shift_index, hopping, partner, own, op, pivot_inverse)
    sh_other = lax.ppermute(sh, "slab", swap)

    locked = jnp.swapaxes(locked_vectors[0], 0, 1)
    even_pairs = [(i, i ^ 1) for i in range(slices)]
    odd_pairs = [(i, i + 1) for i in range(1, slices - 1, 2)]
    odd_pairs = odd_pairs + [(j, i) for i, j in odd_pairs]
    above = lax.ppermute(locked, "cuts", odd_pairs)

    def up(value, r):
        return lax.ppermute(value, "slab", [(r, r + 2), (r + 1, r + 3)])

    def back(value, r):
        return lax.ppermute(value, "slab", [(r, r - 2), (r + 1, r - 1)])

    (sent,) = small_call(start_kernel, (BF16,), "start", fg, fg_other)
    into = jnp.zeros((rows, width), BF16)
    new = up(sent, 0)
    for r in range(2, devices - 2, 2):
        into, sent = small_call(pass_kernel, (BF16, BF16), "pass_on", fg, fg_other, into, new)
        if r == 4:
            near, sent = lax.optimization_barrier((locked, sent))
            below = lax.ppermute(near, "cuts", even_pairs)
        new = up(sent, r)
    inflow, first_back, second_back, sent = small_call(
        turn_kernel, (BF16, F32, F32, BF16), "turn", fg, fg_other, sh, sh_other, into, new
    )
    low = lower_sweep(shift_index, inflow, current, hopping, partner, pivot_inverse)
    known = known_products(current, previous, below, above)
    to = jnp.zeros((rows, width), BF16)
    new = back(sent, devices - 2)
    low, new = lax.optimization_barrier((low, new))
    for r in range(devices - 4, 0, -2):
        to, sent = small_call(
            back_kernel, (BF16, BF16), "pass_back", fg, fg_other, first_back, second_back, to, new
        )
        new = back(sent, r)
    x, products = upper_sweep(
        fg, fg_other, second_back, to, new, low, hopping, current, previous, below, above, known, q
    )
    step = 1
    while step < devices:
        products = products + lax.ppermute(products, "slab", [(i, i ^ step) for i in range(devices)])
        step *= 2
    next_block, upper, ritz = finish(
        scale, products, previous_coupling[0], x, current, previous, below, above
    )
    return next_block[None], upper[None], ritz


def solution(mesh):
    return jax.shard_map(
        per_device,
        mesh=mesh,
        in_specs=(
            P("cuts", "slab", None, None),
            P("cuts", "slab", None, None),
            P("cuts", None, None),
            P("cuts", None, "slab", None),
            P(None, "slab", None, None),
            P("slab", None),
            P("slab", None),
            P("cuts"),
        ),
        out_specs=(P("cuts", "slab", None, None), P("cuts", None, None), P("cuts", None)),
        check_vma=False,
    )
```

```python
import functools

import jax
import jax.numpy as jnp
from jax import lax
from jax.experimental import pallas as pl
from jax.experimental.pallas import tpu as pltpu
from jax.sharding import PartitionSpec as P

F32 = jnp.float32
BF16 = jnp.bfloat16
VMEM_LIMIT = 56 * 1024 * 1024
SMALL_LIMIT = 16 * 1024 * 1024
LOWER_LIMIT = 50 * 1024 * 1024
SECTIONS = 4
AHEAD = 3


def mm(left, right):
    return jnp.dot(left, right, preferred_element_type=F32)


def mm_t(left, right):
    return lax.dot_general(left, right, (((1,), (1,)), ((), ())), preferred_element_type=F32)


def exact(left, right):
    return jnp.dot(left, right, precision=lax.Precision.HIGHEST, preferred_element_type=F32)


def exact_t(left, right):
    return lax.dot_general(
        left, right, (((1,), (1,)), ((), ())),
        precision=lax.Precision.HIGHEST, preferred_element_type=F32,
    )


def halves(value):
    high = value.astype(BF16)
    return high, (value - high.astype(F32)).astype(BF16)


def forward_kernel(
    shift_ref, hop_ref, part_ref, cur_ref, piv_ref,
    fg_ref, own_ref, op_ref,
    pbuf, opbuf, hops, parts, sources, in_sem, op_sem, small_sem,
):
    slabs, width = hop_ref.shape
    shift = shift_ref[0]

    def fetch(k):
        return pltpu.make_async_copy(piv_ref.at[shift, k], pbuf.at[k], in_sem.at[k])

    def give_op(k):
        return pltpu.make_async_copy(opbuf.at[k], op_ref.at[k], op_sem.at[k])

    small = [
        pltpu.make_async_copy(part_ref, parts, small_sem.at[0]),
        pltpu.make_async_copy(hop_ref, hops, small_sem.at[1]),
        pltpu.make_async_copy(cur_ref, sources, small_sem.at[2]),
    ]
    for copy in small:
        copy.start()
    for k in range(AHEAD):
        fetch(k).start()
    down = lax.broadcasted_iota(jnp.int32, (width, width), 0).astype(jnp.int16)
    for copy in small:
        copy.wait()
    places = parts[...].astype(jnp.int16)
    weights = (-hops[...]).astype(BF16)
    def mixed(k):
        gather = jnp.where(
            down == places[k : k + 1, :], weights[k : k + 1, :], jnp.zeros((), BF16)
        )
        fetch(k).wait()
        if k + AHEAD < slabs:
            fetch(k + AHEAD).start()
        product = mm(jnp.concatenate([gather, sources[k].astype(BF16)], axis=0), pbuf[k])
        return product[:width].astype(BF16), product[width:]

    step, vectors = mixed(0)
    opbuf[0] = step
    give_op(0).start()
    own_ref[0] = vectors
    following = mixed(1)
    for k in range(1, slabs):
        step, source = following
        if k + 1 < slabs:
            following = mixed(k + 1)
        moved = mm(jnp.concatenate([opbuf[k - 1], vectors.astype(BF16)], axis=0), step)
        opbuf[k] = moved[:width].astype(BF16)
        vectors = source + moved[width:]
        give_op(k).start()
        own_ref[k] = vectors
    fg_ref[:width, :] = opbuf[slabs - 1]
    fg_ref[width:, :] = vectors.astype(BF16)
    for k in range(slabs):
        give_op(k).wait()


def forward_range(shift_index, hopping, partner, current, pivot_inverse):
    slabs, rows, width = current.shape
    vm = pl.BlockSpec(memory_space=pltpu.VMEM)
    hbm = pl.BlockSpec(memory_space=pl.ANY)
    return pl.pallas_call(
        forward_kernel,
        out_shape=(
            jax.ShapeDtypeStruct((width + rows, width), BF16),
            jax.ShapeDtypeStruct((slabs, rows, width), F32),
            jax.ShapeDtypeStruct((slabs, width, width), BF16),
        ),
        in_specs=[pl.BlockSpec(memory_space=pltpu.SMEM), hbm, hbm, hbm, hbm],
        out_specs=(vm, vm, hbm),
        scratch_shapes=[
            pltpu.VMEM((slabs, width, width), BF16),
            pltpu.VMEM((slabs, width, width), BF16),
            pltpu.VMEM((slabs, width), F32),
            pltpu.VMEM((slabs, width), jnp.int32),
            pltpu.VMEM((slabs, rows, width), F32),
            pltpu.SemaphoreType.DMA((slabs,)),
            pltpu.SemaphoreType.DMA((slabs,)),
            pltpu.SemaphoreType.DMA((3,)),
        ],
        compiler_params=pltpu.CompilerParams(vmem_limit_bytes=VMEM_LIMIT),
        cost_estimate=pl.CostEstimate(
            flops=4 * slabs * width**3, bytes_accessed=6 * slabs * width**2, transcendentals=0
        ),
        name="forward_range",
    )(shift_index, hopping, partner, current, pivot_inverse)


def backward_kernel(
    shift_ref, hop_ref, part_ref, own_ref, op_ref, piv_ref,
    sh_ref, q_ref,
    pbuf, opbuf, qbuf, in_sem, op_sem, q_sem,
):
    slabs, width = hop_ref.shape
    shift = shift_ref[0]

    def fetch(k):
        return pltpu.make_async_copy(piv_ref.at[shift, k], pbuf.at[k], in_sem.at[k])

    def fetch_op(k):
        return pltpu.make_async_copy(op_ref.at[k], opbuf.at[k], op_sem.at[k])

    def give_q(k, source):
        return pltpu.make_async_copy(source.at[k], q_ref.at[k], q_sem.at[k])

    last = slabs - 1
    for k in range(last, -1, -1):
        fetch(k).start()
        fetch_op(k).start()
    across = lax.broadcasted_iota(jnp.int32, (width, width), 1)
    part_columns = jnp.transpose(part_ref[...].astype(F32)).astype(jnp.int32)

    def scatter(k):
        return jnp.where(across == part_columns[:, k : k + 1], 1.0, 0.0).astype(BF16)

    def scaled(k):
        hop = hop_ref[k : k + 1, :]
        return jnp.concatenate(
            [(response * hop).astype(BF16), (vectors * hop).astype(BF16)], axis=0
        )

    fetch(last).wait()
    give_q(last, pbuf).start()
    fetch_op(last).wait()
    response = opbuf[last].astype(F32)
    vectors = own_ref[last]
    def turned(k):
        fetch(k).wait()
        permuted = mm(scatter(k + 1), pbuf[k]).astype(BF16)
        qbuf[k] = permuted
        give_q(k, qbuf).start()
        return permuted

    following = turned(last - 1)
    for k in range(slabs - 2, -1, -1):
        permuted = following
        if k > 0:
            following = turned(k - 1)
        moved = mm(scaled(k + 1), permuted)
        fetch_op(k).wait()
        response = opbuf[k].astype(F32) - moved[:width]
        vectors = own_ref[k] - moved[width:]
    sh_ref[...] = mm(scaled(0), scatter(0)).astype(BF16)
    give_q(last, pbuf).wait()
    for k in range(last):
        give_q(k, qbuf).wait()


def backward_range(shift_index, hopping, partner, own, op, pivot_inverse):
    slabs, rows, width = own.shape
    vm = pl.BlockSpec(memory_space=pltpu.VMEM)
    hbm = pl.BlockSpec(memory_space=pl.ANY)
    stack = jax.ShapeDtypeStruct((slabs, width, width), BF16)
    return pl.pallas_call(
        backward_kernel,
        out_shape=(jax.ShapeDtypeStruct((width + rows, width), BF16), stack),
        in_specs=[pl.BlockSpec(memory_space=pltpu.SMEM), vm, vm, vm, hbm, hbm],
        out_specs=(vm, hbm),
        scratch_shapes=[pltpu.VMEM((slabs, width, width), BF16)] * 3
        + [pltpu.SemaphoreType.DMA((slabs,))] * 3,
        compiler_params=pltpu.CompilerParams(vmem_limit_bytes=VMEM_LIMIT),
        cost_estimate=pl.CostEstimate(
            flops=4 * slabs * width**3, bytes_accessed=6 * slabs * width**2, transcendentals=0
        ),
        name="backward_range",
    )(shift_index, hopping, partner, own, op, pivot_inverse)


def by_order(own_ref, other_ref, run):
    odd = lax.axis_index("slab") % 2

    @pl.when(odd == 0)
    def _():
        run(own_ref, other_ref, 0)

    @pl.when(odd == 1)
    def _():
        run(other_ref, own_ref, 1)


def through(op_ref, value):
    width = op_ref.shape[1]
    return op_ref[width:, :].astype(F32) + mm(value, op_ref[:width, :])


def returned(op_ref, value):
    width = op_ref.shape[1]
    return mm_t(value, op_ref[:width, :])


def start_kernel(own_ref, other_ref, sent_ref):
    def run(first_ref, second_ref, odd):
        width = first_ref.shape[1]
        sent_ref[...] = through(second_ref, first_ref[width:, :]).astype(BF16)

    by_order(own_ref, other_ref, run)


def pass_kernel(own_ref, other_ref, into_ref, new_ref, into_out_ref, sent_ref):
    into = into_ref[...] + new_ref[...]
    into_out_ref[...] = into

    def run(first_ref, second_ref, odd):
        middle = through(first_ref, into).astype(BF16)
        sent_ref[...] = through(second_ref, middle).astype(BF16)

    by_order(own_ref, other_ref, run)


def turn_kernel(
    own_ref, other_ref, own_back_ref, other_back_ref, into_ref, new_ref,
    inflow_ref, first_back_ref, second_back_ref, sent_ref,
):
    into = into_ref[...] + new_ref[...]

    def run(first_ref, second_ref, odd):
        first_sh, second_sh = (
            (other_back_ref, own_back_ref) if odd else (own_back_ref, other_back_ref)
        )
        middle = through(first_ref, into).astype(BF16)
        second_back = through(second_sh, middle)
        first_back = through(first_sh, into)
        sent = first_back + returned(first_ref, second_back.astype(BF16))
        sent_ref[...] = sent.astype(BF16)
        first_back_ref[...] = first_back
        second_back_ref[...] = second_back
        inflow_ref[...] = middle if odd else into

    by_order(own_ref, other_ref, run)


def back_kernel(
    own_ref, other_ref, first_back_ref, second_back_ref, to_ref, new_ref, to_out_ref, sent_ref
):
    to = to_ref[...] + new_ref[...]
    to_out_ref[...] = to

    def run(first_ref, second_ref, odd):
        middle = (second_back_ref[...] + returned(second_ref, to)).astype(BF16)
        sent_ref[...] = (first_back_ref[...] + returned(first_ref, middle)).astype(BF16)

    by_order(own_ref, other_ref, run)


def small_call(kernel, outs, name, *args):
    width = args[0].shape[1]
    rows = args[0].shape[0] - width
    vm = pl.BlockSpec(memory_space=pltpu.VMEM)
    return pl.pallas_call(
        kernel,
        out_shape=tuple(jax.ShapeDtypeStruct((rows, width), t) for t in outs),
        in_specs=[vm] * len(args),
        out_specs=(vm,) * len(outs),
        compiler_params=pltpu.CompilerParams(vmem_limit_bytes=SMALL_LIMIT),
        cost_estimate=pl.CostEstimate(
            flops=4 * rows * width**2, bytes_accessed=4 * width**2, transcendentals=0
        ),
        name=name,
    )(*args)


def lower_kernel(shift_ref, inflow_ref, cur_ref, hop_ref, part_ref, piv_ref, low_ref, pbuf, sem):
    slabs, rows, width = cur_ref.shape
    shift = shift_ref[0]

    def fetch(k):
        return pltpu.make_async_copy(piv_ref.at[shift, k], pbuf.at[k], sem.at[k])

    for k in range(slabs):
        fetch(k).start()
    down = lax.broadcasted_iota(jnp.int32, (width, width), 0).astype(jnp.int16)
    places = part_ref[...].astype(jnp.int16)
    value = inflow_ref[...].astype(F32)
    for k in range(slabs):
        bonds = jnp.where(down == places[k : k + 1, :], jnp.ones((), BF16), jnp.zeros((), BF16))
        high, low = halves(value)
        pulled = mm(jnp.concatenate([high, low], axis=0), bonds)
        reduced = cur_ref[k] - hop_ref[k : k + 1, :] * (pulled[:rows] + pulled[rows:])
        fetch(k).wait()
        value = mm(reduced.astype(BF16), pbuf[k])
        low_ref[k] = value


def lower_sweep(shift_index, inflow, current, hopping, partner, pivot_inverse):
    slabs, rows, width = current.shape
    vm = pl.BlockSpec(memory_space=pltpu.VMEM)
    return pl.pallas_call(
        lower_kernel,
        out_shape=jax.ShapeDtypeStruct((slabs, rows, width), F32),
        in_specs=[pl.BlockSpec(memory_space=pltpu.SMEM), vm, vm, vm, vm]
        + [pl.BlockSpec(memory_space=pl.ANY)],
        out_specs=vm,
        scratch_shapes=[
            pltpu.VMEM((slabs, width, width), BF16),
            pltpu.SemaphoreType.DMA((slabs,)),
        ],
        compiler_params=pltpu.CompilerParams(vmem_limit_bytes=LOWER_LIMIT),
        cost_estimate=pl.CostEstimate(
            flops=2 * slabs * rows * width**2, bytes_accessed=2 * slabs * width**2, transcendentals=0
        ),
        name="lower_sweep",
    )(shift_index, inflow, current, hopping, partner, pivot_inverse)


def known_kernel(cur_ref, prev_ref, below_ref, above_ref, out_ref):
    slabs, rows, width = cur_ref.shape
    near = 2 * below_ref.shape[1]
    two = 2 * rows
    total = None
    for k in range(slabs):
        cur_high, cur_low = halves(cur_ref[k])
        prev_high, prev_low = halves(prev_ref[k])
        stack = jnp.concatenate(
            [below_ref[k], above_ref[k], cur_high, prev_high, cur_low, prev_low], axis=0
        )
        part = mm_t(stack, stack)
        total = part if total is None else total + part
    first = total[near : near + two]
    second = total[near + two :]
    among = first[:, near : near + two] + first[:, near + two :]
    among = among + second[:, near : near + two] + second[:, near + two :]
    half = near // 2
    down = lax.broadcasted_iota(jnp.int32, (half, half), 0)
    across = lax.broadcasted_iota(jnp.int32, (half, half), 1)
    low_block = total[:half, :half]
    high_block = total[half:near, half:near]
    edge = jnp.sum(jnp.where(down == across, high_block, 0.0), axis=0, keepdims=True)
    out_ref[:half, :] = jnp.concatenate(
        [jnp.where(across >= down, low_block, high_block), total[:half, half:near]], axis=1
    )
    out_ref[half : half + two, :] = first[:, :near] + second[:, :near]
    out_ref[half + two : half + two + rows, :] = jnp.zeros((rows, near), F32)
    out_ref[half + two + rows : half + two + 2 * rows, :] = jnp.concatenate(
        [jnp.zeros((rows, near - 2 * two), F32), among[:rows], among[rows:]], axis=1
    )
    out_ref[half + two + 2 * rows :, :] = jnp.broadcast_to(
        jnp.concatenate([edge, jnp.zeros((1, near - half), F32)], axis=1), (8, near)
    )


def known_products(current, previous, below, above):
    slabs, rows, width = current.shape
    near = 2 * below.shape[1]
    return pl.pallas_call(
        known_kernel,
        out_shape=jax.ShapeDtypeStruct((near // 2 + 4 * rows + 8, near), F32),
        compiler_params=pltpu.CompilerParams(vmem_limit_bytes=SMALL_LIMIT),
        cost_estimate=pl.CostEstimate(
            flops=2 * slabs * 192 * 192 * width, bytes_accessed=3 * 2**19, transcendentals=0
        ),
        name="known_products",
    )(current, previous, below, above)


def upper_kernel(
    own_ref, other_ref, second_back_ref, to_ref, new_ref, low_ref, hop_ref, cur_ref, prev_ref, below_ref, above_ref, known_ref, q_ref,
    x_ref, out_ref, carried,
):
    slabs, rows, width = low_ref.shape
    near = 2 * below_ref.shape[1]
    to = to_ref[...] + new_ref[...]

    def run(first_ref, second_ref, odd):
        if odd:
            carried[...] = to
        else:
            carried[...] = (second_back_ref[...] + returned(second_ref, to)).astype(BF16)

    by_order(own_ref, other_ref, run)
    push = carried[...]
    total = None
    for k in range(slabs - 1, -1, -1):
        value = low_ref[k] - mm(push, q_ref[k])
        x_ref[k] = value
        push = (value * hop_ref[k : k + 1, :]).astype(BF16)
        high, low = halves(value)
        pair = jnp.concatenate([high, low], axis=0)
        cur_high, cur_low = halves(cur_ref[k])
        prev_high, prev_low = halves(prev_ref[k])
        stack = jnp.concatenate(
            [below_ref[k], above_ref[k], high, cur_high, prev_high, low, cur_low, prev_low], axis=0
        )
        part = mm_t(pair, stack)
        total = part if total is None else total + part
    joined = total[:rows] + total[rows:]
    three = 3 * rows
    own = joined[:, near : near + three] + joined[:, near + three :]
    top = near // 2 + 2 * rows
    last = top + 2 * rows
    out_ref[:top, :] = known_ref[:top, :]
    out_ref[top : top + rows, :] = joined[:, :near]
    out_ref[top + rows : last, :] = known_ref[top + rows : last, :] + jnp.concatenate(
        [own, jnp.zeros((rows, near - three), F32)], axis=1
    )
    out_ref[last:, :] = known_ref[last:, :]


def upper_sweep(
    own, other, second_back, to, new, low, hopping, current, previous, below, above, known, q
):
    slabs, rows, width = low.shape
    vm = pl.BlockSpec(memory_space=pltpu.VMEM)
    return pl.pallas_call(
        upper_kernel,
        out_shape=(
            jax.ShapeDtypeStruct((slabs, rows, width), F32),
            jax.ShapeDtypeStruct(known.shape, F32),
        ),
        in_specs=[vm] * 13,
        out_specs=(vm, vm),
        scratch_shapes=[pltpu.VMEM((rows, width), BF16)],
        compiler_params=pltpu.CompilerParams(vmem_limit_bytes=SMALL_LIMIT),
        cost_estimate=pl.CostEstimate(
            flops=2 * slabs * rows * width**2, bytes_accessed=2 * slabs * width**2, transcendentals=0
        ),
        name="upper_sweep",
    )(own, other, second_back, to, new, low, hopping, current, previous, below, above, known, q)


def factor_steps(gram, done):
    size = gram.shape[0]
    down = lax.broadcasted_iota(jnp.int32, (size, size), 0)
    across = lax.broadcasted_iota(jnp.int32, (size, size), 1)
    left = gram
    right = jnp.where(down == across, 1.0, 0.0)
    column = lax.broadcasted_iota(jnp.int32, (size, 1), 0)
    pivots = jnp.zeros((size, 1), F32)
    for j in range(size):
        pivot = left[j : j + 1, j : j + 1]
        pivots = jnp.where(column == j, pivot, pivots)
        if j < size - 1:
            scale = jnp.where(column > j, left[:, j : j + 1] / pivot, 0.0)
            left_row = left[j : j + 1, :]
            right_row = right[j : j + 1, :]
            left = left - scale * left_row
            right = right - scale * right_row
            yield
    inverse_root = 1.0 / jnp.sqrt(pivots)
    done.append(jnp.where(across >= down, left * inverse_root, 0.0))
    done.append(right * inverse_root)


def eigenvalue_steps(matrix, done):
    size = matrix.shape[0]
    full = (size, 128)
    down = lax.broadcasted_iota(jnp.int32, full, 0)
    across = lax.broadcasted_iota(jnp.int32, full, 1)
    bound = jnp.max(jnp.sum(jnp.abs(matrix), axis=1, keepdims=True), axis=0, keepdims=True)
    bound = bound * (1.0 + 2.0**-18)
    matrix = jnp.concatenate([matrix, jnp.zeros((size, 128 - size), F32)], axis=1)
    diagonal = []
    squares = []

    def upright(value):
        return jnp.broadcast_to(
            jnp.sum(jnp.where(down == across, value, 0.0), axis=1, keepdims=True), full
        )

    def line(value, i):
        return jnp.broadcast_to(value[i : i + 1, :], full)

    def total(value):
        return jnp.broadcast_to(jnp.sum(value, axis=0, keepdims=True), full)

    row = line(matrix, 0)
    col = upright(row)
    for j in range(size - 2):
        diagonal.append(col[j : j + 1, :])
        next_row = line(matrix, j + 1)
        next_col = upright(next_row)
        below = jnp.where(down > j, col, 0.0)
        beside = jnp.where(across > j, row, 0.0)
        image_row = total(matrix * below)
        image_col = upright(image_row)
        square = total(below * below)
        squares.append(square[0:1, :])
        length = jnp.sqrt(square)
        lead = line(col, j + 1)
        signed = jnp.where(lead >= 0.0, length, -length)
        half = square + length * jnp.abs(lead)
        scale = jnp.where(half > 0.0, 1.0 / jnp.where(half > 0.0, half, 1.0), 0.0)
        v_row = beside + jnp.where(across == j + 1, signed, 0.0)
        v_col = below + jnp.where(down == j + 1, signed, 0.0)
        q_row = image_row + signed * next_row
        q_col = image_col + signed * next_col
        along = 0.5 * scale * (scale * total(q_col * v_col))
        w_row = scale * q_row - along * v_row
        w_col = scale * q_col - along * v_col
        matrix = matrix - (v_col * w_row + w_col * v_row)
        lead_v = line(v_col, j + 1)
        lead_w = line(w_col, j + 1)
        row = next_row - (v_row * lead_w + w_row * lead_v)
        col = next_col - (v_col * lead_w + w_col * lead_v)
        yield
    a = size - 2
    diagonal.append(col[a : a + 1, :])
    squares.append(col[a + 1 : a + 2, :] * col[a + 1 : a + 2, :])
    diagonal.append(upright(line(matrix, a + 1))[a + 1 : a + 2, :])
    shape = (8, 128)
    wide_diagonal = [jnp.broadcast_to(value, shape) for value in diagonal]
    wide_squares = [jnp.broadcast_to(value, shape) for value in squares]
    lane = lax.broadcasted_iota(jnp.int32, shape, 1)
    level = lax.broadcasted_iota(jnp.int32, shape, 0)
    second_half = lane >= 64
    rank = 2 * level + jnp.where(second_half, 1, 0)
    point = (lane - jnp.where(second_half, 64, 0) + 1).astype(F32)
    start = jnp.broadcast_to(-bound, shape)
    step = jnp.broadcast_to(bound * (2.0 / 65.0), shape)
    tiny = 1e-30
    for _ in range(SECTIONS):
        shifted = start + point * step
        pivot = wide_diagonal[0] - shifted
        pivot = jnp.where(jnp.abs(pivot) < tiny, -tiny, pivot)
        count = jnp.where(pivot < 0.0, 1, 0)
        for i in range(1, size):
            pivot = wide_diagonal[i] - shifted - wide_squares[i - 1] / pivot
            pivot = jnp.where(jnp.abs(pivot) < tiny, -tiny, pivot)
            count = count + jnp.where(pivot < 0.0, 1, 0)
            if i % 4 == 0:
                yield
        passed = jnp.where(count <= rank, 1.0, 0.0)
        all_passed = jnp.sum(passed, axis=1, keepdims=True)
        late_passed = jnp.sum(jnp.where(second_half, passed, 0.0), axis=1, keepdims=True)
        cut = jnp.where(second_half, late_passed, all_passed - late_passed)
        start = start + cut * step
        step = step * (1.0 / 65.0)
    middle = start + 32.5 * step
    even = jnp.broadcast_to(middle[:, 0:1], shape)
    odd = jnp.broadcast_to(middle[:, 127:128], shape)
    place = jnp.where(lane == 2 * level, even, jnp.where(lane == 2 * level + 1, odd, 0.0))
    done.append(jnp.sum(place, axis=0, keepdims=True)[:, :size])


def finish_kernel(
    scale, products_ref, coupling_ref, x_ref, cur_ref, prev_ref, below_ref, above_ref,
    next_ref, upper_ref, ritz_ref,
):
    slabs, rows, width = x_ref.shape
    near = products_ref.shape[1]
    two = 2 * rows
    products = products_ref[...] * scale
    half = near // 2
    down = lax.broadcasted_iota(jnp.int32, (half, half), 0)
    across = lax.broadcasted_iota(jnp.int32, (half, half), 1)
    folded = products[:half, :half]
    turned = jnp.transpose(folded)
    between = products[:half, half:]
    edge = products[half + two + 2 * rows : half + two + 2 * rows + 1, :half]
    low_block = jnp.where(across >= down, folded, turned)
    high_block = jnp.where(across == down, edge, jnp.where(across < down, folded, turned))
    near_near = jnp.concatenate(
        [
            jnp.concatenate([low_block, between], axis=1),
            jnp.concatenate([jnp.transpose(between), high_block], axis=1),
        ],
        axis=0,
    )
    known_near = products[half : half + two]
    x_near = products[half + two : half + two + rows]
    tail = products[half + two + rows : half + two + 2 * rows]
    x_x = tail[:, :rows]
    x_known = tail[:, rows : 3 * rows]
    among = jnp.concatenate([tail[:, near - 2 * two : near - two], tail[:, near - two :]], axis=0)
    projection_t = tail[:, rows:two]
    ritz = []
    eigen = eigenvalue_steps(0.5 * (projection_t + jnp.transpose(projection_t)), ritz)
    next(eigen)
    fixed = jnp.concatenate([-projection_t, -coupling_ref[...]], axis=1)
    coefficients_t = x_near + exact(fixed, known_near)
    next(eigen)
    with_known = x_known + exact(fixed, among) - exact_t(coefficients_t, known_near)
    with_near = coefficients_t - exact(coefficients_t, near_near)
    next(eigen)
    gram = x_x + exact_t(fixed, x_known) - exact_t(coefficients_t, x_near)
    gram = gram + exact_t(with_known, fixed) - exact_t(with_near, coefficients_t)
    next(eigen)
    factors = []
    for _ in factor_steps(gram, factors):
        next(eigen)
    upper, inverse_t = factors
    upper_ref[...] = upper
    next(eigen)
    down = lax.broadcasted_iota(jnp.int32, (rows, rows), 0)
    across = lax.broadcasted_iota(jnp.int32, (rows, rows), 1)
    unit = jnp.where(down == across, 1.0, 0.0)
    weights = exact(inverse_t, jnp.concatenate([unit, fixed, -coefficients_t], axis=1))
    weight_high, weight_low = halves(weights)
    both = jnp.concatenate([weight_high, weight_low], axis=0)
    for k in range(slabs):
        x_high, x_low = halves(x_ref[k])
        cur_high, cur_low = halves(cur_ref[k])
        prev_high, prev_low = halves(prev_ref[k])
        stack = jnp.concatenate(
            [x_high, cur_high, prev_high, below_ref[k], above_ref[k]], axis=0
        )
        rest = jnp.concatenate([x_low, cur_low, prev_low], axis=0)
        main = mm(both, stack)
        next_ref[k] = main[:rows] + main[rows:] + mm(weight_high[:, : 3 * rows], rest)
        next(eigen, None)
    for _ in eigen:
        pass
    ritz_ref[...] = ritz[0]


def finish(scale, products, coupling, x, current, previous, below, above):
    slabs, rows, width = x.shape
    return pl.pallas_call(
        functools.partial(finish_kernel, scale),
        out_shape=(
            jax.ShapeDtypeStruct((slabs, rows, width), F32),
            jax.ShapeDtypeStruct((rows, rows), F32),
            jax.ShapeDtypeStruct((1, rows), F32),
        ),
        compiler_params=pltpu.CompilerParams(vmem_limit_bytes=SMALL_LIMIT),
        name="finish",
    )(products, coupling, x, current, previous, below, above)


def per_device(
    current_block,
    previous_block,
    previous_coupling,
    locked_vectors,
    pivot_inverse,
    hopping,
    partner,
    shift_index,
):
    devices = lax.axis_size("slab")
    slices = lax.axis_size("cuts")
    current = current_block[0]
    previous = previous_block[0]
    slabs, rows, width = current.shape
    scale = 1.0 / (slabs * devices * width)
    swap = [(i, i ^ 1) for i in range(devices)]

    fg, own, op = forward_range(
        shift_index, hopping, partner, current, pivot_inverse
    )
    fg_other = lax.ppermute(fg, "slab", swap)
    sh, q = backward_range(shift_index, hopping, partner, own, op, pivot_inverse)
    sh_other = lax.ppermute(sh, "slab", swap)

    locked = jnp.swapaxes(locked_vectors[0], 0, 1)
    even_pairs = [(i, i ^ 1) for i in range(slices)]
    odd_pairs = [(i, i + 1) for i in range(1, slices - 1, 2)]
    odd_pairs = odd_pairs + [(j, i) for i, j in odd_pairs]
    above = lax.ppermute(locked, "cuts", odd_pairs)

    def up(value, r):
        return lax.ppermute(value, "slab", [(r, r + 2), (r + 1, r + 3)])

    def back(value, r):
        return lax.ppermute(value, "slab", [(r, r - 2), (r + 1, r - 1)])

    (sent,) = small_call(start_kernel, (BF16,), "start", fg, fg_other)
    into = jnp.zeros((rows, width), BF16)
    new = up(sent, 0)
    for r in range(2, devices - 2, 2):
        into, sent = small_call(pass_kernel, (BF16, BF16), "pass_on", fg, fg_other, into, new)
        if r == 4:
            near, sent = lax.optimization_barrier((locked, sent))
            below = lax.ppermute(near, "cuts", even_pairs)
        new = up(sent, r)
    inflow, first_back, second_back, sent = small_call(
        turn_kernel, (BF16, F32, F32, BF16), "turn", fg, fg_other, sh, sh_other, into, new
    )
    low = lower_sweep(shift_index, inflow, current, hopping, partner, pivot_inverse)
    known = known_products(current, previous, below, above)
    to = jnp.zeros((rows, width), BF16)
    new = back(sent, devices - 2)
    low, new = lax.optimization_barrier((low, new))
    for r in range(devices - 4, 0, -2):
        to, sent = small_call(
            back_kernel, (BF16, BF16), "pass_back", fg, fg_other, first_back, second_back, to, new
        )
        new = back(sent, r)
    x, products = upper_sweep(
        fg, fg_other, second_back, to, new, low, hopping, current, previous, below, above, known, q
    )
    step = 1
    while step < devices:
        products = products + lax.ppermute(products, "slab", [(i, i ^ step) for i in range(devices)])
        step *= 2
    next_block, upper, ritz = finish(
        scale, products, previous_coupling[0], x, current, previous, below, above
    )
    return next_block[None], upper[None], ritz


def solution(mesh):
    return jax.shard_map(
        per_device,
        mesh=mesh,
        in_specs=(
            P("cuts", "slab", None, None),
            P("cuts", "slab", None, None),
            P("cuts", None, None),
            P("cuts", None, "slab", None),
            P(None, "slab", None, None),
            P("slab", None),
            P("slab", None),
            P("cuts"),
        ),
        out_specs=(P("cuts", "slab", None, None), P("cuts", None, None), P("cuts", None)),
        check_vma=False,
    )
```

```python
import functools

import jax
import jax.numpy as jnp
from jax import lax
from jax.experimental import pallas as pl
from jax.experimental.pallas import tpu as pltpu
from jax.sharding import PartitionSpec as P

F32 = jnp.float32
BF16 = jnp.bfloat16
VMEM_LIMIT = 56 * 1024 * 1024
SMALL_LIMIT = 16 * 1024 * 1024
LOWER_LIMIT = 50 * 1024 * 1024
SECTIONS = 4
AHEAD = 3


def mm(left, right):
    return jnp.dot(left, right, preferred_element_type=F32)


def mm_t(left, right):
    return lax.dot_general(left, right, (((1,), (1,)), ((), ())), preferred_element_type=F32)


def exact(left, right):
    return jnp.dot(left, right, precision=lax.Precision.HIGHEST, preferred_element_type=F32)


def exact_t(left, right):
    return lax.dot_general(
        left, right, (((1,), (1,)), ((), ())),
        precision=lax.Precision.HIGHEST, preferred_element_type=F32,
    )


def halves(value):
    high = value.astype(BF16)
    return high, (value - high.astype(F32)).astype(BF16)


def forward_kernel(
    shift_ref, hop_ref, part_ref, cur_ref, piv_ref,
    fg_ref, own_ref, op_ref,
    pbuf, opbuf, hops, parts, sources, in_sem, op_sem, small_sem,
):
    slabs, width = hop_ref.shape
    shift = shift_ref[0]

    def fetch(k):
        return pltpu.make_async_copy(piv_ref.at[shift, k], pbuf.at[k], in_sem.at[k])

    def give_op(k):
        return pltpu.make_async_copy(opbuf.at[k], op_ref.at[k], op_sem.at[k])

    small = [
        pltpu.make_async_copy(part_ref, parts, small_sem.at[0]),
        pltpu.make_async_copy(hop_ref, hops, small_sem.at[1]),
        pltpu.make_async_copy(cur_ref, sources, small_sem.at[2]),
    ]
    for copy in small:
        copy.start()
    for k in range(AHEAD):
        fetch(k).start()
    down = lax.broadcasted_iota(jnp.int32, (width, width), 0).astype(jnp.int16)
    for copy in small:
        copy.wait()
    places = parts[...].astype(jnp.int16)
    weights = (-hops[...]).astype(BF16)
    def mixed(k):
        gather = jnp.where(
            down == places[k : k + 1, :], weights[k : k + 1, :], jnp.zeros((), BF16)
        )
        fetch(k).wait()
        if k + AHEAD < slabs:
            fetch(k + AHEAD).start()
        product = mm(jnp.concatenate([gather, sources[k].astype(BF16)], axis=0), pbuf[k])
        return product[:width].astype(BF16), product[width:]

    step, vectors = mixed(0)
    opbuf[0] = step
    give_op(0).start()
    own_ref[0] = vectors
    following = mixed(1)
    for k in range(1, slabs):
        step, source = following
        if k + 1 < slabs:
            following = mixed(k + 1)
        moved = mm(jnp.concatenate([opbuf[k - 1], vectors.astype(BF16)], axis=0), step)
        opbuf[k] = moved[:width].astype(BF16)
        vectors = source + moved[width:]
        give_op(k).start()
        own_ref[k] = vectors
    fg_ref[:width, :] = opbuf[slabs - 1]
    fg_ref[width:, :] = vectors.astype(BF16)
    for k in range(slabs):
        give_op(k).wait()


def forward_range(shift_index, hopping, partner, current, pivot_inverse):
    slabs, rows, width = current.shape
    vm = pl.BlockSpec(memory_space=pltpu.VMEM)
    hbm = pl.BlockSpec(memory_space=pl.ANY)
    return pl.pallas_call(
        forward_kernel,
        out_shape=(
            jax.ShapeDtypeStruct((width + rows, width), BF16),
            jax.ShapeDtypeStruct((slabs, rows, width), F32),
            jax.ShapeDtypeStruct((slabs, width, width), BF16),
        ),
        in_specs=[pl.BlockSpec(memory_space=pltpu.SMEM), hbm, hbm, hbm, hbm],
        out_specs=(vm, vm, hbm),
        scratch_shapes=[
            pltpu.VMEM((slabs, width, width), BF16),
            pltpu.VMEM((slabs, width, width), BF16),
            pltpu.VMEM((slabs, width), F32),
            pltpu.VMEM((slabs, width), jnp.int32),
            pltpu.VMEM((slabs, rows, width), F32),
            pltpu.SemaphoreType.DMA((slabs,)),
            pltpu.SemaphoreType.DMA((slabs,)),
            pltpu.SemaphoreType.DMA((3,)),
        ],
        compiler_params=pltpu.CompilerParams(vmem_limit_bytes=VMEM_LIMIT),
        cost_estimate=pl.CostEstimate(
            flops=4 * slabs * width**3, bytes_accessed=6 * slabs * width**2, transcendentals=0
        ),
        name="forward_range",
    )(shift_index, hopping, partner, current, pivot_inverse)


def backward_kernel(
    shift_ref, hop_ref, part_ref, own_ref, op_ref, piv_ref,
    sh_ref, q_ref,
    pbuf, opbuf, qbuf, in_sem, op_sem, q_sem,
):
    slabs, width = hop_ref.shape
    shift = shift_ref[0]

    def fetch(k):
        return pltpu.make_async_copy(piv_ref.at[shift, k], pbuf.at[k], in_sem.at[k])

    def fetch_op(k):
        return pltpu.make_async_copy(op_ref.at[k], opbuf.at[k], op_sem.at[k])

    def give_q(k, source):
        return pltpu.make_async_copy(source.at[k], q_ref.at[k], q_sem.at[k])

    last = slabs - 1
    for k in range(last, -1, -1):
        fetch(k).start()
        fetch_op(k).start()
    across = lax.broadcasted_iota(jnp.int32, (width, width), 1)
    part_columns = jnp.transpose(part_ref[...].astype(F32)).astype(jnp.int32)

    def scatter(k):
        return jnp.where(across == part_columns[:, k : k + 1], 1.0, 0.0).astype(BF16)

    def scaled(k):
        hop = hop_ref[k : k + 1, :]
        return jnp.concatenate(
            [(response * hop).astype(BF16), (vectors * hop).astype(BF16)], axis=0
        )

    fetch(last).wait()
    give_q(last, pbuf).start()
    fetch_op(last).wait()
    response = opbuf[last].astype(F32)
    vectors = own_ref[last]
    def turned(k):
        fetch(k).wait()
        permuted = mm(scatter(k + 1), pbuf[k]).astype(BF16)
        qbuf[k] = permuted
        give_q(k, qbuf).start()
        return permuted

    following = turned(last - 1)
    for k in range(slabs - 2, -1, -1):
        permuted = following
        if k > 0:
            following = turned(k - 1)
        moved = mm(scaled(k + 1), permuted)
        fetch_op(k).wait()
        response = opbuf[k].astype(F32) - moved[:width]
        vectors = own_ref[k] - moved[width:]
    sh_ref[...] = mm(scaled(0), scatter(0)).astype(BF16)
    give_q(last, pbuf).wait()
    for k in range(last):
        give_q(k, qbuf).wait()


def backward_range(shift_index, hopping, partner, own, op, pivot_inverse):
    slabs, rows, width = own.shape
    vm = pl.BlockSpec(memory_space=pltpu.VMEM)
    hbm = pl.BlockSpec(memory_space=pl.ANY)
    stack = jax.ShapeDtypeStruct((slabs, width, width), BF16)
    return pl.pallas_call(
        backward_kernel,
        out_shape=(jax.ShapeDtypeStruct((width + rows, width), BF16), stack),
        in_specs=[pl.BlockSpec(memory_space=pltpu.SMEM), vm, vm, vm, hbm, hbm],
        out_specs=(vm, hbm),
        scratch_shapes=[pltpu.VMEM((slabs, width, width), BF16)] * 3
        + [pltpu.SemaphoreType.DMA((slabs,))] * 3,
        compiler_params=pltpu.CompilerParams(vmem_limit_bytes=VMEM_LIMIT),
        cost_estimate=pl.CostEstimate(
            flops=4 * slabs * width**3, bytes_accessed=6 * slabs * width**2, transcendentals=0
        ),
        name="backward_range",
    )(shift_index, hopping, partner, own, op, pivot_inverse)


def by_order(own_ref, other_ref, run):
    odd = lax.axis_index("slab") % 2

    @pl.when(odd == 0)
    def _():
        run(own_ref, other_ref, 0)

    @pl.when(odd == 1)
    def _():
        run(other_ref, own_ref, 1)


def through(op_ref, value):
    width = op_ref.shape[1]
    return op_ref[width:, :].astype(F32) + mm(value, op_ref[:width, :])


def returned(op_ref, value):
    width = op_ref.shape[1]
    return mm_t(value, op_ref[:width, :])


def start_kernel(own_ref, other_ref, sent_ref):
    def run(first_ref, second_ref, odd):
        width = first_ref.shape[1]
        sent_ref[...] = through(second_ref, first_ref[width:, :]).astype(BF16)

    by_order(own_ref, other_ref, run)


def pass_kernel(own_ref, other_ref, into_ref, new_ref, into_out_ref, sent_ref):
    into = into_ref[...] + new_ref[...]
    into_out_ref[...] = into

    def run(first_ref, second_ref, odd):
        middle = through(first_ref, into).astype(BF16)
        sent_ref[...] = through(second_ref, middle).astype(BF16)

    by_order(own_ref, other_ref, run)


def turn_kernel(
    own_ref, other_ref, own_back_ref, other_back_ref, into_ref, new_ref,
    inflow_ref, first_back_ref, second_back_ref, sent_ref,
):
    into = into_ref[...] + new_ref[...]

    def run(first_ref, second_ref, odd):
        first_sh, second_sh = (
            (other_back_ref, own_back_ref) if odd else (own_back_ref, other_back_ref)
        )
        middle = through(first_ref, into).astype(BF16)
        second_back = through(second_sh, middle)
        first_back = through(first_sh, into)
        sent = first_back + returned(first_ref, second_back.astype(BF16))
        sent_ref[...] = sent.astype(BF16)
        first_back_ref[...] = first_back
        second_back_ref[...] = second_back
        inflow_ref[...] = middle if odd else into

    by_order(own_ref, other_ref, run)


def back_kernel(
    own_ref, other_ref, first_back_ref, second_back_ref, to_ref, new_ref, to_out_ref, sent_ref
):
    to = to_ref[...] + new_ref[...]
    to_out_ref[...] = to

    def run(first_ref, second_ref, odd):
        middle = (second_back_ref[...] + returned(second_ref, to)).astype(BF16)
        sent_ref[...] = (first_back_ref[...] + returned(first_ref, middle)).astype(BF16)

    by_order(own_ref, other_ref, run)


def small_call(kernel, outs, name, *args):
    width = args[0].shape[1]
    rows = args[0].shape[0] - width
    vm = pl.BlockSpec(memory_space=pltpu.VMEM)
    return pl.pallas_call(
        kernel,
        out_shape=tuple(jax.ShapeDtypeStruct((rows, width), t) for t in outs),
        in_specs=[vm] * len(args),
        out_specs=(vm,) * len(outs),
        compiler_params=pltpu.CompilerParams(vmem_limit_bytes=SMALL_LIMIT),
        cost_estimate=pl.CostEstimate(
            flops=4 * rows * width**2, bytes_accessed=4 * width**2, transcendentals=0
        ),
        name=name,
    )(*args)


def lower_kernel(shift_ref, inflow_ref, cur_ref, hop_ref, part_ref, piv_ref, low_ref, pbuf, sem):
    slabs, rows, width = cur_ref.shape
    shift = shift_ref[0]

    def fetch(k):
        return pltpu.make_async_copy(piv_ref.at[shift, k], pbuf.at[k], sem.at[k])

    for k in range(slabs):
        fetch(k).start()
    down = lax.broadcasted_iota(jnp.int32, (width, width), 0).astype(jnp.int16)
    places = part_ref[...].astype(jnp.int16)
    value = inflow_ref[...].astype(F32)
    for k in range(slabs):
        bonds = jnp.where(down == places[k : k + 1, :], jnp.ones((), BF16), jnp.zeros((), BF16))
        high, low = halves(value)
        pulled = mm(jnp.concatenate([high, low], axis=0), bonds)
        reduced = cur_ref[k] - hop_ref[k : k + 1, :] * (pulled[:rows] + pulled[rows:])
        fetch(k).wait()
        value = mm(reduced.astype(BF16), pbuf[k])
        low_ref[k] = value


def lower_sweep(shift_index, inflow, current, hopping, partner, pivot_inverse):
    slabs, rows, width = current.shape
    vm = pl.BlockSpec(memory_space=pltpu.VMEM)
    return pl.pallas_call(
        lower_kernel,
        out_shape=jax.ShapeDtypeStruct((slabs, rows, width), F32),
        in_specs=[pl.BlockSpec(memory_space=pltpu.SMEM), vm, vm, vm, vm]
        + [pl.BlockSpec(memory_space=pl.ANY)],
        out_specs=vm,
        scratch_shapes=[
            pltpu.VMEM((slabs, width, width), BF16),
            pltpu.SemaphoreType.DMA((slabs,)),
        ],
        compiler_params=pltpu.CompilerParams(vmem_limit_bytes=LOWER_LIMIT),
        cost_estimate=pl.CostEstimate(
            flops=2 * slabs * rows * width**2, bytes_accessed=2 * slabs * width**2, transcendentals=0
        ),
        name="lower_sweep",
    )(shift_index, inflow, current, hopping, partner, pivot_inverse)


def known_kernel(cur_ref, prev_ref, below_ref, above_ref, out_ref):
    slabs, rows, width = cur_ref.shape
    near = 2 * below_ref.shape[1]
    two = 2 * rows
    total = None
    for k in range(slabs):
        cur_high, cur_low = halves(cur_ref[k])
        prev_high, prev_low = halves(prev_ref[k])
        stack = jnp.concatenate(
            [below_ref[k], above_ref[k], cur_high, prev_high, cur_low, prev_low], axis=0
        )
        part = mm_t(stack, stack)
        total = part if total is None else total + part
    first = total[near : near + two]
    second = total[near + two :]
    among = first[:, near : near + two] + first[:, near + two :]
    among = among + second[:, near : near + two] + second[:, near + two :]
    half = near // 2
    down = lax.broadcasted_iota(jnp.int32, (half, half), 0)
    across = lax.broadcasted_iota(jnp.int32, (half, half), 1)
    low_block = total[:half, :half]
    high_block = total[half:near, half:near]
    edge = jnp.sum(jnp.where(down == across, high_block, 0.0), axis=0, keepdims=True)
    out_ref[:half, :] = jnp.concatenate(
        [jnp.where(across >= down, low_block, high_block), total[:half, half:near]], axis=1
    )
    out_ref[half : half + two, :] = first[:, :near] + second[:, :near]
    out_ref[half + two : half + two + rows, :] = jnp.zeros((rows, near), F32)
    out_ref[half + two + rows : half + two + 2 * rows, :] = jnp.concatenate(
        [jnp.zeros((rows, near - 2 * two), F32), among[:rows], among[rows:]], axis=1
    )
    out_ref[half + two + 2 * rows :, :] = jnp.broadcast_to(
        jnp.concatenate([edge, jnp.zeros((1, near - half), F32)], axis=1), (8, near)
    )


def known_products(current, previous, below, above):
    slabs, rows, width = current.shape
    near = 2 * below.shape[1]
    return pl.pallas_call(
        known_kernel,
        out_shape=jax.ShapeDtypeStruct((near // 2 + 4 * rows + 8, near), F32),
        compiler_params=pltpu.CompilerParams(vmem_limit_bytes=SMALL_LIMIT),
        cost_estimate=pl.CostEstimate(
            flops=2 * slabs * 192 * 192 * width, bytes_accessed=3 * 2**19, transcendentals=0
        ),
        name="known_products",
    )(current, previous, below, above)


def upper_kernel(
    own_ref, other_ref, second_back_ref, to_ref, new_ref, low_ref, hop_ref, cur_ref, prev_ref, below_ref, above_ref, known_ref, q_ref,
    x_ref, out_ref, carried,
):
    slabs, rows, width = low_ref.shape
    near = 2 * below_ref.shape[1]
    to = to_ref[...] + new_ref[...]

    def run(first_ref, second_ref, odd):
        if odd:
            carried[...] = to
        else:
            carried[...] = (second_back_ref[...] + returned(second_ref, to)).astype(BF16)

    by_order(own_ref, other_ref, run)
    push = carried[...]
    total = None
    for k in range(slabs - 1, -1, -1):
        value = low_ref[k] - mm(push, q_ref[k])
        x_ref[k] = value
        push = (value * hop_ref[k : k + 1, :]).astype(BF16)
        high, low = halves(value)
        pair = jnp.concatenate([high, low], axis=0)
        cur_high, cur_low = halves(cur_ref[k])
        prev_high, prev_low = halves(prev_ref[k])
        stack = jnp.concatenate(
            [below_ref[k], above_ref[k], high, cur_high, prev_high, low, cur_low, prev_low], axis=0
        )
        part = mm_t(pair, stack)
        total = part if total is None else total + part
    joined = total[:rows] + total[rows:]
    three = 3 * rows
    own = joined[:, near : near + three] + joined[:, near + three :]
    top = near // 2 + 2 * rows
    last = top + 2 * rows
    out_ref[:top, :] = known_ref[:top, :]
    out_ref[top : top + rows, :] = joined[:, :near]
    out_ref[top + rows : last, :] = known_ref[top + rows : last, :] + jnp.concatenate(
        [own, jnp.zeros((rows, near - three), F32)], axis=1
    )
    out_ref[last:, :] = known_ref[last:, :]


def upper_sweep(
    own, other, second_back, to, new, low, hopping, current, previous, below, above, known, q
):
    slabs, rows, width = low.shape
    vm = pl.BlockSpec(memory_space=pltpu.VMEM)
    return pl.pallas_call(
        upper_kernel,
        out_shape=(
            jax.ShapeDtypeStruct((slabs, rows, width), F32),
            jax.ShapeDtypeStruct(known.shape, F32),
        ),
        in_specs=[vm] * 13,
        out_specs=(vm, vm),
        scratch_shapes=[pltpu.VMEM((rows, width), BF16)],
        compiler_params=pltpu.CompilerParams(vmem_limit_bytes=SMALL_LIMIT),
        cost_estimate=pl.CostEstimate(
            flops=2 * slabs * rows * width**2, bytes_accessed=2 * slabs * width**2, transcendentals=0
        ),
        name="upper_sweep",
    )(own, other, second_back, to, new, low, hopping, current, previous, below, above, known, q)


def factor_steps(gram, done):
    size = gram.shape[0]
    down = lax.broadcasted_iota(jnp.int32, (size, size), 0)
    across = lax.broadcasted_iota(jnp.int32, (size, size), 1)
    left = gram
    right = jnp.where(down == across, 1.0, 0.0)
    column = lax.broadcasted_iota(jnp.int32, (size, 1), 0)
    pivots = jnp.zeros((size, 1), F32)
    for j in range(size):
        pivot = left[j : j + 1, j : j + 1]
        pivots = jnp.where(column == j, pivot, pivots)
        if j < size - 1:
            scale = jnp.where(column > j, left[:, j : j + 1] / pivot, 0.0)
            left_row = left[j : j + 1, :]
            right_row = right[j : j + 1, :]
            left = left - scale * left_row
            right = right - scale * right_row
            yield
    inverse_root = 1.0 / jnp.sqrt(pivots)
    done.append(jnp.where(across >= down, left * inverse_root, 0.0))
    done.append(right * inverse_root)


def eigenvalue_steps(matrix, done):
    size = matrix.shape[0]
    full = (size, 128)
    down = lax.broadcasted_iota(jnp.int32, full, 0)
    across = lax.broadcasted_iota(jnp.int32, full, 1)
    bound = jnp.max(jnp.sum(jnp.abs(matrix), axis=1, keepdims=True), axis=0, keepdims=True)
    bound = bound * (1.0 + 2.0**-18)
    matrix = jnp.concatenate([matrix, jnp.zeros((size, 128 - size), F32)], axis=1)
    diagonal = []
    squares = []

    def upright(value):
        return jnp.broadcast_to(
            jnp.sum(jnp.where(down == across, value, 0.0), axis=1, keepdims=True), full
        )

    def line(value, i):
        return jnp.broadcast_to(value[i : i + 1, :], full)

    def total(value):
        return jnp.broadcast_to(jnp.sum(value, axis=0, keepdims=True), full)

    row = line(matrix, 0)
    col = upright(row)
    for j in range(size - 2):
        diagonal.append(col[j : j + 1, :])
        next_row = line(matrix, j + 1)
        next_col = upright(next_row)
        below = jnp.where(down > j, col, 0.0)
        beside = jnp.where(across > j, row, 0.0)
        image_row = total(matrix * below)
        image_col = upright(image_row)
        square = total(below * below)
        squares.append(square[0:1, :])
        length = jnp.sqrt(square)
        lead = line(col, j + 1)
        signed = jnp.where(lead >= 0.0, length, -length)
        half = square + length * jnp.abs(lead)
        scale = jnp.where(half > 0.0, 1.0 / jnp.where(half > 0.0, half, 1.0), 0.0)
        v_row = beside + jnp.where(across == j + 1, signed, 0.0)
        v_col = below + jnp.where(down == j + 1, signed, 0.0)
        q_row = image_row + signed * next_row
        q_col = image_col + signed * next_col
        along = 0.5 * scale * (scale * total(q_col * v_col))
        w_row = scale * q_row - along * v_row
        w_col = scale * q_col - along * v_col
        matrix = matrix - (v_col * w_row + w_col * v_row)
        lead_v = line(v_col, j + 1)
        lead_w = line(w_col, j + 1)
        row = next_row - (v_row * lead_w + w_row * lead_v)
        col = next_col - (v_col * lead_w + w_col * lead_v)
        yield
    a = size - 2
    diagonal.append(col[a : a + 1, :])
    squares.append(col[a + 1 : a + 2, :] * col[a + 1 : a + 2, :])
    diagonal.append(upright(line(matrix, a + 1))[a + 1 : a + 2, :])
    shape = (8, 128)
    wide_diagonal = [jnp.broadcast_to(value, shape) for value in diagonal]
    wide_squares = [jnp.broadcast_to(value, shape) for value in squares]
    lane = lax.broadcasted_iota(jnp.int32, shape, 1)
    level = lax.broadcasted_iota(jnp.int32, shape, 0)
    second_half = lane >= 64
    rank = 2 * level + jnp.where(second_half, 1, 0)
    point = (lane - jnp.where(second_half, 64, 0) + 1).astype(F32)
    start = jnp.broadcast_to(-bound, shape)
    step = jnp.broadcast_to(bound * (2.0 / 65.0), shape)
    tiny = 1e-30
    for _ in range(SECTIONS):
        shifted = start + point * step
        pivot = wide_diagonal[0] - shifted
        pivot = jnp.where(jnp.abs(pivot) < tiny, -tiny, pivot)
        count = jnp.where(pivot < 0.0, 1, 0)
        for i in range(1, size):
            pivot = wide_diagonal[i] - shifted - wide_squares[i - 1] / pivot
            pivot = jnp.where(jnp.abs(pivot) < tiny, -tiny, pivot)
            count = count + jnp.where(pivot < 0.0, 1, 0)
            if i % 4 == 0:
                yield
        passed = jnp.where(count <= rank, 1.0, 0.0)
        all_passed = jnp.sum(passed, axis=1, keepdims=True)
        late_passed = jnp.sum(jnp.where(second_half, passed, 0.0), axis=1, keepdims=True)
        cut = jnp.where(second_half, late_passed, all_passed - late_passed)
        start = start + cut * step
        step = step * (1.0 / 65.0)
    middle = start + 32.5 * step
    even = jnp.broadcast_to(middle[:, 0:1], shape)
    odd = jnp.broadcast_to(middle[:, 127:128], shape)
    place = jnp.where(lane == 2 * level, even, jnp.where(lane == 2 * level + 1, odd, 0.0))
    done.append(jnp.sum(place, axis=0, keepdims=True)[:, :size])


def finish_kernel(
    scale, products_ref, coupling_ref, x_ref, cur_ref, prev_ref, below_ref, above_ref,
    next_ref, upper_ref, ritz_ref, following, sem,
):
    slabs, rows, width = x_ref.shape
    near = products_ref.shape[1]
    two = 2 * rows
    products = products_ref[...] * scale
    half = near // 2
    down = lax.broadcasted_iota(jnp.int32, (half, half), 0)
    across = lax.broadcasted_iota(jnp.int32, (half, half), 1)
    folded = products[:half, :half]
    turned = jnp.transpose(folded)
    between = products[:half, half:]
    edge = products[half + two + 2 * rows : half + two + 2 * rows + 1, :half]
    low_block = jnp.where(across >= down, folded, turned)
    high_block = jnp.where(across == down, edge, jnp.where(across < down, folded, turned))
    near_near = jnp.concatenate(
        [
            jnp.concatenate([low_block, between], axis=1),
            jnp.concatenate([jnp.transpose(between), high_block], axis=1),
        ],
        axis=0,
    )
    known_near = products[half : half + two]
    x_near = products[half + two : half + two + rows]
    tail = products[half + two + rows : half + two + 2 * rows]
    x_x = tail[:, :rows]
    x_known = tail[:, rows : 3 * rows]
    among = jnp.concatenate([tail[:, near - 2 * two : near - two], tail[:, near - two :]], axis=0)
    projection_t = tail[:, rows:two]
    ritz = []
    eigen = eigenvalue_steps(0.5 * (projection_t + jnp.transpose(projection_t)), ritz)
    next(eigen)
    fixed = jnp.concatenate([-projection_t, -coupling_ref[...]], axis=1)
    coefficients_t = x_near + exact(fixed, known_near)
    next(eigen)
    with_known = x_known + exact(fixed, among) - exact_t(coefficients_t, known_near)
    with_near = coefficients_t - exact(coefficients_t, near_near)
    next(eigen)
    gram = x_x + exact_t(fixed, x_known) - exact_t(coefficients_t, x_near)
    gram = gram + exact_t(with_known, fixed) - exact_t(with_near, coefficients_t)
    next(eigen)
    factors = []
    for _ in factor_steps(gram, factors):
        next(eigen)
    upper, inverse_t = factors
    upper_ref[...] = upper
    next(eigen)
    down = lax.broadcasted_iota(jnp.int32, (rows, rows), 0)
    across = lax.broadcasted_iota(jnp.int32, (rows, rows), 1)
    unit = jnp.where(down == across, 1.0, 0.0)
    weights = exact(inverse_t, jnp.concatenate([unit, fixed, -coefficients_t], axis=1))
    weight_high, weight_low = halves(weights)
    both = jnp.concatenate([weight_high, weight_low], axis=0)
    for k in range(slabs):
        x_high, x_low = halves(x_ref[k])
        cur_high, cur_low = halves(cur_ref[k])
        prev_high, prev_low = halves(prev_ref[k])
        stack = jnp.concatenate(
            [x_high, cur_high, prev_high, below_ref[k], above_ref[k]], axis=0
        )
        rest = jnp.concatenate([x_low, cur_low, prev_low], axis=0)
        main = mm(both, stack)
        following[k] = main[:rows] + main[rows:] + mm(weight_high[:, : 3 * rows], rest)
        pltpu.make_async_copy(following.at[k], next_ref.at[k], sem.at[k]).start()
        next(eigen, None)
    for _ in eigen:
        pass
    ritz_ref[...] = ritz[0]
    for k in range(slabs):
        pltpu.make_async_copy(following.at[k], next_ref.at[k], sem.at[k]).wait()


def finish(scale, products, coupling, x, current, previous, below, above):
    slabs, rows, width = x.shape
    return pl.pallas_call(
        functools.partial(finish_kernel, scale),
        out_shape=(
            jax.ShapeDtypeStruct((slabs, rows, width), F32),
            jax.ShapeDtypeStruct((rows, rows), F32),
            jax.ShapeDtypeStruct((1, rows), F32),
        ),
        in_specs=[pl.BlockSpec(memory_space=pltpu.VMEM)] * 7,
        out_specs=(
            pl.BlockSpec(memory_space=pl.ANY),
            pl.BlockSpec(memory_space=pltpu.VMEM),
            pl.BlockSpec(memory_space=pltpu.VMEM),
        ),
        scratch_shapes=[
            pltpu.VMEM((slabs, rows, width), F32),
            pltpu.SemaphoreType.DMA((slabs,)),
        ],
        compiler_params=pltpu.CompilerParams(vmem_limit_bytes=SMALL_LIMIT),
        name="finish",
    )(products, coupling, x, current, previous, below, above)


def per_device(
    current_block,
    previous_block,
    previous_coupling,
    locked_vectors,
    pivot_inverse,
    hopping,
    partner,
    shift_index,
):
    devices = lax.axis_size("slab")
    slices = lax.axis_size("cuts")
    current = current_block[0]
    previous = previous_block[0]
    slabs, rows, width = current.shape
    scale = 1.0 / (slabs * devices * width)
    swap = [(i, i ^ 1) for i in range(devices)]

    fg, own, op = forward_range(
        shift_index, hopping, partner, current, pivot_inverse
    )
    fg_other = lax.ppermute(fg, "slab", swap)
    sh, q = backward_range(shift_index, hopping, partner, own, op, pivot_inverse)
    sh_other = lax.ppermute(sh, "slab", swap)

    locked = jnp.swapaxes(locked_vectors[0], 0, 1)
    even_pairs = [(i, i ^ 1) for i in range(slices)]
    odd_pairs = [(i, i + 1) for i in range(1, slices - 1, 2)]
    odd_pairs = odd_pairs + [(j, i) for i, j in odd_pairs]
    above = lax.ppermute(locked, "cuts", odd_pairs)

    def up(value, r):
        return lax.ppermute(value, "slab", [(r, r + 2), (r + 1, r + 3)])

    def back(value, r):
        return lax.ppermute(value, "slab", [(r, r - 2), (r + 1, r - 1)])

    (sent,) = small_call(start_kernel, (BF16,), "start", fg, fg_other)
    into = jnp.zeros((rows, width), BF16)
    new = up(sent, 0)
    for r in range(2, devices - 2, 2):
        into, sent = small_call(pass_kernel, (BF16, BF16), "pass_on", fg, fg_other, into, new)
        if r == 4:
            near, sent = lax.optimization_barrier((locked, sent))
            below = lax.ppermute(near, "cuts", even_pairs)
        new = up(sent, r)
    inflow, first_back, second_back, sent = small_call(
        turn_kernel, (BF16, F32, F32, BF16), "turn", fg, fg_other, sh, sh_other, into, new
    )
    low = lower_sweep(shift_index, inflow, current, hopping, partner, pivot_inverse)
    known = known_products(current, previous, below, above)
    to = jnp.zeros((rows, width), BF16)
    new = back(sent, devices - 2)
    low, new = lax.optimization_barrier((low, new))
    for r in range(devices - 4, 0, -2):
        to, sent = small_call(
            back_kernel, (BF16, BF16), "pass_back", fg, fg_other, first_back, second_back, to, new
        )
        new = back(sent, r)
    x, products = upper_sweep(
        fg, fg_other, second_back, to, new, low, hopping, current, previous, below, above, known, q
    )
    step = 1
    while step < devices:
        products = products + lax.ppermute(products, "slab", [(i, i ^ step) for i in range(devices)])
        step *= 2
    next_block, upper, ritz = finish(
        scale, products, previous_coupling[0], x, current, previous, below, above
    )
    return next_block[None], upper[None], ritz


def solution(mesh):
    return jax.shard_map(
        per_device,
        mesh=mesh,
        in_specs=(
            P("cuts", "slab", None, None),
            P("cuts", "slab", None, None),
            P("cuts", None, None),
            P("cuts", None, "slab", None),
            P(None, "slab", None, None),
            P("slab", None),
            P("slab", None),
            P("cuts"),
        ),
        out_specs=(P("cuts", "slab", None, None), P("cuts", None, None), P("cuts", None)),
        check_vma=False,
    )
```
